128 devices in a mesh: lat: 8 (over x, core), lon: 16 (over z, y).
Axes of the slice: x: 4, y: 4, z: 4, core: 2. Of those that a mesh axis runs over, the one named last changes fastest.
Arguments:
- fields: bfloat16 [256, 2048, 128], P('lat', 'lon'), may hold values from -6 to 6
- cotangent: bfloat16 [256, 2048, 128], P('lat', 'lon'), may hold values from -6 to 6
- kernel_bank: bfloat16 [256, 9, 128, 128], P(('lat', 'lon')), may hold values from -0.1875 to 0.1875
- block_expert: int32 [16, 128], P('lat', 'lon'), may hold values from 0 to 255, as said below
- owner: int32 [256], replicated, may hold values from 0 to 255, as said below
Outputs:
- outputs: bfloat16 [256, 2048, 128], P('lat', 'lon')
- grad_fields: bfloat16 [256, 2048, 128], P('lat', 'lon')
- grad_bank: float32 [256, 9, 128, 128], P(('lat', 'lon'))
The draws below stay inside these ranges and needn't reach their ends.
Inputs may be any that keep to these rules, and one draw needn't show every extreme that they name: owner is a permutation: each expert is stored in exactly one row of kernel_bank. `block_expert`: call the lon column of expert e the value (owner[e] // 2) modulo the number of devices along lon. Among the 2 x 8 blocks of one device, at most 2 name experts of any one lon column; in every latitude band of devices one column is named by exactly 2 blocks of each device of that band.
All inputs are finite; a program needn't handle non-finite values.
Results may differ from the reference program's by a relative error of at most 0.0032.
Values may be sent and summed in bfloat16 or wider, within the bound.
A program may use at most 192 MiB of HBM per device.

```python
import jax
import jax.numpy as jnp
from jax import lax

C = 128
EXPERTS = 256
BS = 16
CAP = 2
BLAT_DEV = 2
BLON_DEV = 8
EXP_DEV = 2
EXP_COL = 16
NBLAT = 16
NBLON = 128
HEIGHT = 256
WIDTH = 2048


def storage_slots(key):
    return jax.random.permutation(jax.random.fold_in(key, 11), EXPERTS).astype(jnp.int32)


def draw_owner(key, part):
    return storage_slots(key)


def draw_block_expert(key, part):
    slots = storage_slots(key)
    holder = jnp.argsort(slots, stable=True).astype(jnp.int32)
    lat_devices = NBLAT // BLAT_DEV
    lon_devices = NBLON // BLON_DEV
    block_total = BLAT_DEV * BLON_DEV
    entry_total = lon_devices * CAP
    full_column = jax.random.randint(jax.random.fold_in(key, 23), (lat_devices,), 0, lon_devices)

    def one_device(device_index):
        device_key = jax.random.fold_in(jax.random.fold_in(key, 37), device_index)
        band = device_index // lon_devices
        entries = jax.random.permutation(jax.random.fold_in(device_key, 1), entry_total).astype(jnp.int32)
        columns = entries // CAP
        ranking = jnp.where(columns == full_column[band], -1, jnp.arange(entry_total, dtype=jnp.int32))
        ordered = entries[jnp.argsort(ranking, stable=True)]
        picked = ordered[:block_total] // CAP
        mixing = jax.random.permutation(jax.random.fold_in(device_key, 2), block_total)
        placed = picked[mixing]
        first_pick = jax.random.randint(jax.random.fold_in(device_key, 3), (block_total,), 0, EXP_COL)
        second_pick = jax.random.randint(jax.random.fold_in(device_key, 4), (block_total,), 0, EXP_COL)
        local_ids = jnp.minimum(first_pick, second_pick)
        stored = (local_ids // EXP_DEV * lon_devices + placed) * EXP_DEV + local_ids % EXP_DEV
        return holder[stored]
    table = jax.vmap(one_device)(jnp.arange(lat_devices * lon_devices, dtype=jnp.int32))
    table = table.reshape(lat_devices, lon_devices, BLAT_DEV, BLON_DEV).transpose(0, 2, 1, 3)
    return table.reshape(NBLAT, NBLON).astype(jnp.int32)


def steps_of(own_key, extent, split, least, high):
    level = 1.0
    for dim, shards_of in split:
        heights = jax.random.uniform(jax.random.fold_in(jax.random.fold_in(own_key, 6), dim), (shards_of,), jnp.float32, least / len(split), high / len(split))
        level = level * jnp.repeat(jnp.exp(heights), extent[dim] // shards_of).reshape((-1,) + (1,) * (len(extent) - 1 - dim))
    return level


def scatter_about(rng, extent, scale, most, cuts=(), kind=jnp.bfloat16):
    level = steps_of(rng, extent, cuts, -0.22, 0.18) if cuts else 1.0
    array = jax.random.normal(rng, extent, jnp.float32) * scale * level
    return jnp.minimum(jnp.maximum(array, -most), most).astype(kind)


def setup_inputs(seed: int = 0) -> dict:
    arg_keys = jax.random.split(jax.random.key(seed), 6)
    return {
        "fields": scatter_about(arg_keys[0], (HEIGHT, WIDTH, C), 1.0, 6.0, ((0, 8), (1, 16))),
        "cotangent": scatter_about(arg_keys[1], (HEIGHT, WIDTH, C), 1.0, 6.0, ((0, 8), (1, 16))),
        "kernel_bank": scatter_about(arg_keys[2], (EXPERTS, 9, C, C), (9 * C) ** -0.5, 0.1875, ((0, 128),)),
        "block_expert": draw_block_expert(jax.random.fold_in(arg_keys[5], 71), 0),
        "owner": draw_owner(jax.random.fold_in(arg_keys[5], 71), 0),
    }


def windows(source, along):
    blocks_n = (source.shape[along] - 2) // BS
    leading = lax.slice_in_dim(source, 0, BS * blocks_n, axis=along)
    trailing = lax.slice_in_dim(source, BS, BS * blocks_n + 2, axis=along)
    padding = [(0, 0)] * source.ndim
    padding[along] = (0, BS - 2)
    trailing = jnp.pad(trailing, padding)
    new_shape = source.shape[:along] + (blocks_n, BS) + source.shape[along + 1:]
    leading = leading.reshape(new_shape)
    trailing = lax.slice_in_dim(trailing.reshape(new_shape), 0, 2, axis=along + 1)
    return jnp.concatenate([leading, trailing], axis=along + 1)


def tiles_to_grid(blocks):
    lat_blocks, lon_blocks, tile_rows, tile_cols, chans = blocks.shape
    return blocks.transpose(0, 2, 1, 3, 4).reshape(lat_blocks * tile_rows, lon_blocks * tile_cols, chans)


def place_portion(portion, row_shift, col_shift):
    padded = jnp.pad(portion, ((0, 0), (0, 0), (0, BS - portion.shape[2]), (0, BS - portion.shape[3]), (0, 0)))
    grid = tiles_to_grid(padded)
    return jnp.pad(grid, ((row_shift, BS - row_shift), (col_shift, BS - col_shift), (0, 0)))


def place_blocks(blocks):
    row_total = blocks.shape[0] * BS
    col_total = blocks.shape[1] * BS
    canvas = place_portion(blocks[:, :, :BS, :BS], 0, 0)
    canvas = canvas + place_portion(blocks[:, :, :BS, BS:], 0, BS)
    canvas = canvas + place_portion(blocks[:, :, BS:, :BS], BS, 0)
    canvas = canvas + place_portion(blocks[:, :, BS:, BS:], BS, BS)
    return canvas[:row_total + 2, :col_total + 2]


def block_math(patch_in, cot_in, kernel_in):
    patch_f = patch_in.astype(jnp.float32)
    cot_f = cot_in.astype(jnp.float32)
    kernel_f = kernel_in.astype(jnp.float32)
    hp = lax.Precision.HIGHEST
    total = jnp.zeros(cot_in.shape, jnp.float32)
    spread = jnp.zeros(patch_in.shape, jnp.float32)
    grads = []
    for tap_index in range(9):
        row_off = tap_index // 3
        col_off = tap_index % 3
        window = patch_f[:, row_off:row_off + BS, col_off:col_off + BS]
        total = total + jnp.einsum("sxyc,scd->sxyd", window, kernel_f[:, tap_index], precision=hp)
        term = jnp.einsum("sxyd,scd->sxyc", cot_f, kernel_f[:, tap_index], precision=hp)
        spread = spread + jnp.pad(term, ((0, 0), (row_off, 2 - row_off), (col_off, 2 - col_off), (0, 0)))
        grads.append(jnp.einsum("sxyc,sxyd->scd", window, cot_f, precision=hp))
    return total, spread, jnp.stack(grads, axis=1)


def reference(fields, cotangent, kernel_bank, block_expert, owner):
    height, width, chans = fields.shape
    wrapped = jnp.concatenate([fields[:, -1:], fields, fields[:, :1]], axis=1)
    extended = jnp.pad(wrapped, ((1, 1), (0, 0), (0, 0)))
    patches = windows(windows(extended, 0), 2).transpose(0, 2, 1, 3, 4)
    cot_blocks = cotangent.reshape(NBLAT, BS, NBLON, BS, chans).transpose(0, 2, 1, 3, 4)
    storage = owner[block_expert].astype(jnp.int32)

    def one_row(grad_carry, inputs):
        row_patches, row_cot, row_storage = inputs
        kernels = kernel_bank[row_storage]
        total, spread, per_block = block_math(row_patches, row_cot, kernels)
        grad_carry = grad_carry.at[row_storage].add(per_block)
        return grad_carry, (total.astype(jnp.bfloat16), spread.astype(jnp.bfloat16))

    start_grad = jnp.zeros((EXPERTS, 9, chans, chans), jnp.float32)
    grad_bank, (out_blocks, spread_blocks) = lax.scan(one_row, start_grad, (patches, cot_blocks, storage))
    outputs = tiles_to_grid(out_blocks)
    canvas = place_blocks(spread_blocks.astype(jnp.float32))
    middle = canvas[1:height + 1]
    result = middle[:, 1:width + 1]
    result = result.at[:, 0].add(middle[:, width + 1])
    result = result.at[:, width - 1].add(middle[:, 0])
    return outputs, result.astype(jnp.bfloat16), grad_bank
```

```python
import jax
import jax.numpy as jnp
from jax import lax
from jax.experimental import pallas as pl
from jax.experimental.pallas import tpu as pltpu
from jax.sharding import PartitionSpec as P

BS = 16
CAP = 2
C = 128
NLAT = 8
NLON = 16
RING = 4
BLK = 16
BLON = 8
HEIGHT = 32
WIDTH = 128
ROWS = BS + 2
TILES = ROWS + 4
EXT_ROWS = HEIGHT + 2
EXT_COLS = WIDTH + 2 * BS
MESH = pl.DeviceIdType.MESH
F32 = jnp.float32
BF16 = jnp.bfloat16


def peer_lon(me, k):
    z, y = me // RING, lax.rem(me, RING)
    return lax.rem(z + k // RING, RING) * RING + lax.rem(y + lax.rem(k, RING), RING)


def source_lon(me, k):
    z, y = me // RING, lax.rem(me, RING)
    return lax.rem(z + RING - k // RING, RING) * RING + lax.rem(y + RING - lax.rem(k, RING), RING)


def greet(lat, lon, diagonal):
    barrier = pltpu.get_barrier_semaphore()

    def signal(device):
        pl.semaphore_signal(barrier, inc=1, device_id=device, device_id_type=MESH)

    @pl.loop(1, NLON)
    def _(k):
        signal((lat, peer_lon(lon, k)))

    @pl.loop(1, NLAT)
    def _(k):
        signal((lax.rem(lat + k, NLAT), lon))

    for up, side in diagonal:
        signal((lax.rem(lat + up, NLAT), lax.rem(lon + side, NLON)))
    pl.semaphore_wait(barrier, NLON - 1 + NLAT - 1 + len(diagonal))


DIAGONAL = ((NLAT - 1, NLON - 1), (NLAT - 1, 1), (1, NLON - 1), (1, 1))


def index_tables(expert_ref, owner_ref, column, local, slot_block):
    for b in range(BLK):
        stored = owner_ref[expert_ref[b // BLON, b % BLON]]
        group = stored >> 1
        column[b] = group & (NLON - 1)
        local[b] = (group >> 4) * 2 + (stored & 1)

    @pl.loop(0, NLON)
    def _(c):
        first = jnp.int32(-1)
        second = jnp.int32(-1)
        for b in range(BLK):
            here = column[b] == c
            second = jnp.where(here & (first >= 0), b, second)
            first = jnp.where(here & (first < 0), b, first)
        slot_block[2 * c] = first
        slot_block[2 * c + 1] = second


def send_kernel(
    expert_ref, owner_ref, fields, cot, bank,
    patch_out, cot_out, id_out, kern_out,
    column, local, slot_block, ext, wide, side_l, side_r, cot_in, patch_in, cot_stage, patch_stage, id_stage,
    load_sem, halo_send, halo_recv, bank_send, bank_recv, cot_send, cot_recv,
    patch_send, patch_recv, id_send, id_recv,
):
    lat, lon = lax.axis_index("lat"), lax.axis_index("lon")
    load_fields = pltpu.make_async_copy(
        fields, ext.at[pl.ds(1, HEIGHT), pl.ds(BS, WIDTH)], load_sem.at[0]
    )
    load_fields.start()

    def load_cot(b):
        rows = pl.ds(pl.multiple_of((b // BLON) * BS, BS), BS)
        cols = pl.ds(pl.multiple_of(lax.rem(b, BLON) * BS, BS), BS)
        return pltpu.make_async_copy(cot.at[rows, cols], cot_in.at[b], load_sem.at[6 + b])

    @pl.loop(0, BLK)
    def _(b):
        load_cot(b).start()

    own_bank = pltpu.make_async_copy(bank, kern_out.at[lat], load_sem.at[2])
    own_bank.start()
    index_tables(expert_ref, owner_ref, column, local, slot_block)
    greet(lat, lon, DIAGONAL)

    up, down = lax.rem(lat + NLAT - 1, NLAT), lax.rem(lat + 1, NLAT)
    left, right = lax.rem(lon + NLON - 1, NLON), lax.rem(lon + 1, NLON)
    top, bottom = pl.ds(0, 1), pl.ds(HEIGHT - 1, 1)
    first, last = pl.ds(0, BS), pl.ds(WIDTH - BS, BS)
    all_rows, all_cols = pl.ds(0, HEIGHT), pl.ds(0, WIDTH)
    mid_rows, mid_cols = pl.ds(1, HEIGHT), pl.ds(BS, WIDTH)
    low, high = pl.ds(0, BS), pl.ds(BS + WIDTH, BS)
    zero, end = pl.ds(0, 1), pl.ds(EXT_ROWS - 1, 1)
    moves = (
        (top, all_cols, end, mid_cols, (up, lon)),
        (bottom, all_cols, zero, mid_cols, (down, lon)),
        (all_rows, first, mid_rows, high, (lat, left)),
        (all_rows, last, mid_rows, low, (lat, right)),
        (top, first, end, high, (up, left)),
        (top, last, end, low, (up, right)),
        (bottom, first, zero, high, (down, left)),
        (bottom, last, zero, low, (down, right)),
    )
    halos = []
    for i, (rows, cols, to_rows, to_cols, device) in enumerate(moves):
        copy = pltpu.make_async_remote_copy(
            fields.at[rows, cols], ext.at[to_rows, to_cols], halo_send.at[i], halo_recv.at[i],
            device_id=device, device_id_type=MESH,
        )
        copy.start()
        halos.append(copy)

    def cot_copy(k, r):
        dst = peer_lon(lon, k)
        return pltpu.make_async_remote_copy(
            cot_stage.at[dst, r], cot_out.at[lon, r], cot_send.at[r, k], cot_recv.at[r, k],
            device_id=(lat, dst), device_id_type=MESH,
        )

    def id_copy(k):
        dst = peer_lon(lon, k)
        return pltpu.make_async_remote_copy(
            id_stage.at[dst], id_out.at[lon], id_send.at[k], id_recv.at[k],
            device_id=(lat, dst), device_id_type=MESH,
        )

    def patch_copy(k, r):
        dst = peer_lon(lon, k)
        return pltpu.make_async_remote_copy(
            patch_stage.at[dst, r], patch_out.at[lon, r], patch_send.at[r, k], patch_recv.at[r, k],
            device_id=(lat, dst), device_id_type=MESH,
        )

    def bank_copy(k):
        return pltpu.make_async_remote_copy(
            bank, kern_out.at[lat], bank_send.at[k], bank_recv.at[k],
            device_id=(lax.rem(lat + k, NLAT), lon), device_id_type=MESH,
        )

    lane = lax.broadcasted_iota(jnp.int32, (1, C), 1)

    @pl.loop(0, BLK)
    def _(b):
        load_cot(b).wait()

    def stage_cot(k, r):
        dst = peer_lon(lon, k)
        cot_stage[dst, r] = cot_in[jnp.maximum(slot_block[2 * dst + r], 0)]

    @pl.loop(1, NLON)
    def _(k):
        stage_cot(k, 0)
        cot_copy(k, 0).start()

    @pl.loop(1, NLAT)
    def _(k):
        bank_copy(k).start()

    @pl.loop(1, NLON)
    def _(k):
        stage_cot(k, 1)
        cot_copy(k, 1).start()

    @pl.loop(0, NLON)
    def _(c):
        ids = []
        for r in range(CAP):
            found = slot_block[2 * c + r]
            ids.append(jnp.where(found < 0, -1, local[jnp.maximum(found, 0)]))
        id_stage[c] = jnp.where(lane == 0, ids[0], ids[1])

    @pl.loop(1, NLON)
    def _(k):
        id_copy(k).start()

    stage_cot(0, 0)
    stage_cot(0, 1)
    own_cot = pltpu.make_async_copy(cot_stage.at[lon], cot_out.at[lon], load_sem.at[3])
    own_ids = pltpu.make_async_copy(id_stage.at[lon], id_out.at[lon], load_sem.at[4])
    own_cot.start()
    own_ids.start()

    load_fields.wait()
    for copy in halos:
        copy.wait()

    @pl.when(lat == 0)
    def _():
        ext[0] = jnp.zeros((EXT_COLS, C), BF16)

    @pl.when(lat == NLAT - 1)
    def _():
        ext[EXT_ROWS - 1] = jnp.zeros((EXT_COLS, C), BF16)

    @pl.loop(0, EXT_ROWS)
    def _(r):
        wide[pl.ds(pl.multiple_of(r * EXT_COLS, BS), EXT_COLS), :] = ext[r].astype(F32)

    @pl.loop(0, BLON)
    def _(k):
        side_l[k, pl.ds(0, EXT_ROWS)] = wide[
            pl.ds(k * BS + BS - 1, EXT_ROWS, stride=EXT_COLS), :
        ].astype(BF16)
        side_r[k, pl.ds(0, EXT_ROWS)] = wide[
            pl.ds(k * BS + 2 * BS, EXT_ROWS, stride=EXT_COLS), :
        ].astype(BF16)

    @pl.loop(0, BLK)
    def _(b):
        row = pl.multiple_of((b // BLON) * BS, BS)
        col = lax.rem(b, BLON)
        patch_in[b, pl.ds(0, ROWS)] = ext[
            pl.ds(row, ROWS), pl.ds(pl.multiple_of((col + 1) * BS, BS), BS), :
        ]
        patch_in[b, pl.ds(ROWS, 2)] = side_l[col, pl.ds(row, 2 * BS)].reshape(2, BS, C)
        patch_in[b, pl.ds(ROWS + 2, 2)] = side_r[col, pl.ds(row, 2 * BS)].reshape(2, BS, C)

    def stage_patch(k, r):
        dst = peer_lon(lon, k)
        patch_stage[dst, r] = patch_in[jnp.maximum(slot_block[2 * dst + r], 0)]

    for r in range(CAP):
        @pl.loop(1, NLON)
        def _(k):
            stage_patch(k, r)
            patch_copy(k, r).start()

    stage_patch(0, 0)
    stage_patch(0, 1)
    own_patch = pltpu.make_async_copy(patch_stage.at[lon], patch_out.at[lon], load_sem.at[5])
    own_patch.start()
    own_bank.wait()
    own_cot.wait()
    own_ids.wait()
    own_patch.wait()

    @pl.loop(1, NLAT)
    def _(k):
        bank_copy(k).wait()

    @pl.loop(1, NLON)
    def _(k):
        id_copy(k).wait()
        for r in range(CAP):
            cot_copy(k, r).wait()
            patch_copy(k, r).wait()


def send_blocks(block_expert, owner, fields, cotangent, bank):
    hbm = pl.BlockSpec(memory_space=pltpu.HBM)
    smem = pl.BlockSpec(memory_space=pltpu.SMEM)
    dma = pltpu.SemaphoreType.DMA
    return pl.pallas_call(
        send_kernel,
        out_shape=(
            jax.ShapeDtypeStruct((NLON, CAP, TILES, BS, C), BF16),
            jax.ShapeDtypeStruct((NLON, CAP, BS, BS, C), BF16),
            jax.ShapeDtypeStruct((NLON, 1, C), jnp.int32),
            jax.ShapeDtypeStruct((NLAT,) + bank.shape, BF16),
        ),
        in_specs=[smem, smem, hbm, hbm, hbm],
        out_specs=(hbm, hbm, hbm, hbm),
        scratch_shapes=[
            pltpu.SMEM((BLK,), jnp.int32),
            pltpu.SMEM((BLK,), jnp.int32),
            pltpu.SMEM((NLON * CAP,), jnp.int32),
            pltpu.VMEM((EXT_ROWS, EXT_COLS, C), BF16),
            pltpu.VMEM((EXT_ROWS * EXT_COLS, C), F32),
            pltpu.VMEM((BLON, 3 * BS, C), BF16),
            pltpu.VMEM((BLON, 3 * BS, C), BF16),
            pltpu.VMEM((BLK, BS, BS, C), BF16),
            pltpu.VMEM((BLK, TILES, BS, C), BF16),
            pltpu.VMEM((NLON, CAP, BS, BS, C), BF16),
            pltpu.VMEM((NLON, CAP, TILES, BS, C), BF16),
            pltpu.VMEM((NLON, 1, C), jnp.int32),
            dma((6 + BLK,)),
            dma((8,)), dma((8,)),
            dma((NLAT,)), dma((NLAT,)),
            dma((CAP, NLON)), dma((CAP, NLON)),
            dma((CAP, NLON)), dma((CAP, NLON)),
            dma((NLON,)), dma((NLON,)),
        ],
        compiler_params=pltpu.CompilerParams(
            collective_id=0, has_side_effects=True, vmem_limit_bytes=40 << 20
        ),
    )(block_expert, owner, fields, cotangent, bank)


def compute_kernel(
    ids, patch, cot, kern, out, spread, grads,
    pad, taps, wide_cot, shift, total, started,
):
    step = pl.program_id(0)

    @pl.when(step == 0)
    def _():
        wide_cot[...] = jnp.zeros_like(wide_cot)
        for e in range(NLON):
            started[e] = 0

    for r in range(CAP):
        found = ids[step, 0, r]

        @pl.when(found >= 0)
        def _():
            e = jnp.maximum(found, 0)
            pad[:, pl.ds(8, BS), :] = patch[0, r, pl.ds(0, ROWS)].astype(F32)
            left = patch[0, r, pl.ds(ROWS, 2)].reshape(2 * BS, C)[:ROWS].astype(F32)
            right = patch[0, r, pl.ds(ROWS + 2, 2)].reshape(2 * BS, C)[:ROWS].astype(F32)
            pad[:, 7, :] = left
            pad[:, BS + 8, :] = right
            for b in range(3):
                taps[:, pl.ds(b * C, C)] = pad[:, pl.ds(7 + b, BS), :].reshape(ROWS * BS, C).astype(BF16)
            cots = cot[0, r].reshape(BS * BS, C)
            for a in range(3):
                wide_cot[pl.ds(a * BS, BS * BS), pl.ds(a * C, C)] = cots
            weights = [kern[e, pl.ds(3 * a, 3)].reshape(3 * C, C) for a in range(3)]
            result = jnp.zeros((BS * BS, C), F32)
            for a in range(3):
                result += jnp.dot(
                    taps[pl.ds(a * BS, BS * BS), :], weights[a], preferred_element_type=F32
                )
            out[0, r] = result.astype(BF16).reshape(BS, BS, C)
            both = jnp.concatenate(weights, axis=1)
            grid = lax.dot_general(
                wide_cot[...], both, (((1,), (1,)), ((), ())), preferred_element_type=F32
            )
            shift[0, :, pl.ds(8, BS), :] = grid[:, :C].reshape(ROWS, BS, C)
            shift[1, :, pl.ds(8, BS), :] = grid[:, 2 * C:].reshape(ROWS, BS, C)
            place = lax.broadcasted_iota(jnp.int32, (ROWS, BS, C), 1)
            main = grid[:, C:2 * C].reshape(ROWS, BS, C)
            main += jnp.where(place == BS - 1, 0.0, shift[0, :, pl.ds(9, BS), :])
            main += jnp.where(place == 0, 0.0, shift[1, :, pl.ds(7, BS), :])
            spread[0, r, pl.ds(0, ROWS)] = main.astype(BF16)
            tail = jnp.zeros((2 * BS - ROWS, C), F32)
            lefts = jnp.concatenate([shift[0, :, 8, :], tail], axis=0)
            rights = jnp.concatenate([shift[1, :, BS + 7, :], tail], axis=0)
            spread[0, r, pl.ds(ROWS, 2)] = lefts.astype(BF16).reshape(2, BS, C)
            spread[0, r, pl.ds(ROWS + 2, 2)] = rights.astype(BF16).reshape(2, BS, C)
            keep = started[e] > 0
            for a in range(3):
                term = lax.dot_general(
                    taps[pl.ds(a * BS, BS * BS), :], cots, (((0,), (0,)), ((), ())),
                    preferred_element_type=F32,
                ).reshape(3, C, C)
                before = total[e, pl.ds(3 * a, 3)]
                total[e, pl.ds(3 * a, 3)] = jnp.where(keep, before, 0.0) + term
            started[e] = 1

    @pl.when(step == NLON - 1)
    def _():
        @pl.loop(0, NLON)
        def _(e):
            grads[e] = jnp.where(started[e] > 0, total[e], 0.0).astype(BF16)


def compute(ids, patches, cots, kernels):
    slot = lambda rows: pl.BlockSpec((1, CAP, rows, BS, C), lambda s: (s, 0, 0, 0, 0))
    whole = pl.BlockSpec((NLON, 9, C, C), lambda s: (0, 0, 0, 0), pipeline_mode=pl.Buffered(1))
    return pl.pallas_call(
        compute_kernel,
        grid=(NLON,),
        out_shape=(
            jax.ShapeDtypeStruct((NLON, CAP, BS, BS, C), BF16),
            jax.ShapeDtypeStruct((NLON, CAP, TILES, BS, C), BF16),
            jax.ShapeDtypeStruct((NLON, 9, C, C), BF16),
        ),
        in_specs=[pl.BlockSpec(memory_space=pltpu.SMEM), slot(TILES), slot(BS), whole],
        out_specs=(slot(BS), slot(TILES), whole),
        scratch_shapes=[
            pltpu.VMEM((ROWS, 2 * BS, C), F32),
            pltpu.VMEM((ROWS * BS, 3 * C), BF16),
            pltpu.VMEM((ROWS * BS, 3 * C), BF16),
            pltpu.VMEM((2, ROWS, 2 * BS, C), F32),
            pltpu.VMEM((NLON, 9, C, C), F32),
            pltpu.SMEM((NLON,), jnp.int32),
        ],
        compiler_params=pltpu.CompilerParams(vmem_limit_bytes=48 << 20),
    )(ids, patches, cots, kernels)


def return_kernel(
    expert_ref, owner_ref, blocks, spreads, grads,
    outputs, result, bank_out,
    column, local, slot_block, block_slot, got_out, got_spread, got_grads, canvas, block,
    row_in, col_in, corner_in,
    load_sem, grad_send, grad_recv, out_send, out_recv, spread_send, spread_recv, halo_send, halo_recv,
):
    lat, lon = lax.axis_index("lat"), lax.axis_index("lon")
    own = [
        pltpu.make_async_copy(blocks.at[lon], got_out.at[pl.ds(2 * lon, CAP)], load_sem.at[0]),
        pltpu.make_async_copy(spreads.at[lon], got_spread.at[pl.ds(2 * lon, CAP)], load_sem.at[1]),
        pltpu.make_async_copy(grads.at[lat], got_grads.at[lat], load_sem.at[2]),
    ]
    for copy in own:
        copy.start()
    greet(lat, lon, DIAGONAL)

    def spread_copy(k, r):
        dst = peer_lon(lon, k)
        return pltpu.make_async_remote_copy(
            spreads.at[dst, r], got_spread.at[2 * lon + r], spread_send.at[r, k], spread_recv.at[r, k],
            device_id=(lat, dst), device_id_type=MESH,
        )

    def out_copy(k, r):
        dst = peer_lon(lon, k)
        return pltpu.make_async_remote_copy(
            blocks.at[dst, r], got_out.at[2 * lon + r], out_send.at[r, k], out_recv.at[r, k],
            device_id=(lat, dst), device_id_type=MESH,
        )

    def grad_copy(k):
        dst = lax.rem(lat + k, NLAT)
        return pltpu.make_async_remote_copy(
            grads.at[dst], got_grads.at[lat], grad_send.at[k], grad_recv.at[k],
            device_id=(dst, lon), device_id_type=MESH,
        )

    @pl.loop(1, NLON)
    def _(k):
        spread_copy(k, 0).start()

    @pl.loop(1, NLAT)
    def _(k):
        grad_copy(k).start()

    @pl.loop(1, NLON)
    def _(k):
        spread_copy(k, 1).start()

    for r in range(CAP):
        @pl.loop(1, NLON)
        def _(k):
            out_copy(k, r).start()

    index_tables(expert_ref, owner_ref, column, local, slot_block)
    for b in range(BLK):
        c = column[b]
        block_slot[b] = 2 * c + jnp.where(slot_block[2 * c + 1] == b, 1, 0)
    canvas[...] = jnp.zeros_like(canvas)

    @pl.loop(1, NLON)
    def _(k):
        for r in range(CAP):
            spread_copy(k, r).wait()

    for copy in own:
        copy.wait()

    @pl.loop(0, BLK)
    def _(b):
        bi, bj = b // BLON, lax.rem(b, BLON)
        slot = block_slot[b]
        base = bi * BS * EXT_COLS + (bj + 1) * BS
        block[...] = got_spread[slot]

        @pl.loop(0, ROWS)
        def _(i):
            at = pl.ds(pl.multiple_of(base + i * EXT_COLS, BS), BS)
            canvas[at, :] += block[i].astype(F32)

        lefts = block[pl.ds(ROWS, 2)].reshape(2 * BS, C)[:ROWS].astype(F32)
        rights = block[pl.ds(ROWS + 2, 2)].reshape(2 * BS, C)[:ROWS].astype(F32)
        canvas[pl.ds(base - 1, ROWS, stride=EXT_COLS), :] += lefts
        canvas[pl.ds(base + BS, ROWS, stride=EXT_COLS), :] += rights

    up, down = lax.rem(lat + NLAT - 1, NLAT), lax.rem(lat + 1, NLAT)
    left, right = lax.rem(lon + NLON - 1, NLON), lax.rem(lon + 1, NLON)
    grid = canvas.reshape(EXT_ROWS, EXT_COLS, C)
    half = BS // 2
    low, high = pl.ds(half, half), pl.ds(BS + WIDTH, half)
    cols, rows = pl.ds(BS, WIDTH), pl.ds(1, HEIGHT)
    moves = (
        (grid.at[0, cols], row_in.at[0], (up, lon)),
        (grid.at[EXT_ROWS - 1, cols], row_in.at[1], (down, lon)),
        (grid.at[rows, low], col_in.at[0], (lat, left)),
        (grid.at[rows, high], col_in.at[1], (lat, right)),
        (grid.at[0, low], corner_in.at[0], (up, left)),
        (grid.at[0, high], corner_in.at[1], (up, right)),
        (grid.at[EXT_ROWS - 1, low], corner_in.at[2], (down, left)),
        (grid.at[EXT_ROWS - 1, high], corner_in.at[3], (down, right)),
    )
    halos = []
    for i, (source, target, device) in enumerate(moves):
        copy = pltpu.make_async_remote_copy(
            source, target, halo_send.at[i], halo_recv.at[i],
            device_id=device, device_id_type=MESH,
        )
        copy.start()
        halos.append(copy)

    @pl.loop(1, NLAT)
    def _(k):
        grad_copy(k).wait()

    for e in range(2):
        @pl.loop(0, 9)
        def _(t):
            sums = got_grads[0, e, t].astype(F32)
            for i in range(1, NLAT):
                sums += got_grads[i, e, t].astype(F32)
            bank_out[e, t] = sums

    @pl.loop(1, NLON)
    def _(k):
        for r in range(CAP):
            out_copy(k, r).wait()

    @pl.loop(0, BLK)
    def _(b):
        bi, bj = b // BLON, lax.rem(b, BLON)
        slot = block_slot[b]
        outputs[
            pl.ds(pl.multiple_of(bi * BS, BS), BS), pl.ds(pl.multiple_of(bj * BS, BS), BS), :
        ] = got_out[slot]

    for copy in halos:
        copy.wait()
    from_down = jnp.where(lat < NLAT - 1, 1.0, 0.0).astype(F32)
    from_up = jnp.where(lat > 0, 1.0, 0.0).astype(F32)
    top, bottom = EXT_COLS, HEIGHT * EXT_COLS
    canvas[pl.ds(bottom + BS, WIDTH), :] += row_in[0] * from_down
    canvas[pl.ds(top + BS, WIDTH), :] += row_in[1] * from_up
    near, far = pl.ds(BS, half), pl.ds(BS + WIDTH - half, half)

    @pl.loop(0, HEIGHT)
    def _(i):
        start = pl.multiple_of((i + 1) * EXT_COLS, BS)
        canvas[pl.ds(start + BS + WIDTH - half, half), :] += col_in[0, i]
        canvas[pl.ds(start + BS, half), :] += col_in[1, i]

    canvas[pl.ds(bottom + BS + WIDTH - half, half), :] += corner_in[0] * from_down
    canvas[pl.ds(bottom + BS, half), :] += corner_in[1] * from_down
    canvas[pl.ds(top + BS + WIDTH - half, half), :] += corner_in[2] * from_up
    canvas[pl.ds(top + BS, half), :] += corner_in[3] * from_up

    @pl.loop(0, HEIGHT)
    def _(i):
        start = pl.multiple_of((i + 1) * EXT_COLS + BS, BS)
        result[i] = canvas[pl.ds(start, WIDTH), :].astype(BF16)


def return_blocks(block_expert, owner, blocks, spreads, grads):
    hbm = pl.BlockSpec(memory_space=pltpu.HBM)
    smem = pl.BlockSpec(memory_space=pltpu.SMEM)
    vmem = pl.BlockSpec(memory_space=pltpu.VMEM)
    dma = pltpu.SemaphoreType.DMA
    return pl.pallas_call(
        return_kernel,
        out_shape=(
            jax.ShapeDtypeStruct((HEIGHT, WIDTH, C), BF16),
            jax.ShapeDtypeStruct((HEIGHT, WIDTH, C), BF16),
            jax.ShapeDtypeStruct((2, 9, C, C), F32),
        ),
        in_specs=[smem, smem, hbm, hbm, hbm],
        out_specs=(vmem, vmem, vmem),
        scratch_shapes=[
            pltpu.SMEM((BLK,), jnp.int32),
            pltpu.SMEM((BLK,), jnp.int32),
            pltpu.SMEM((NLON * CAP,), jnp.int32),
            pltpu.SMEM((BLK,), jnp.int32),
            pltpu.VMEM((NLON * CAP, BS, BS, C), BF16),
            pltpu.VMEM((NLON * CAP, TILES, BS, C), BF16),
            pltpu.VMEM((NLAT, 2, 9, C, C), BF16),
            pltpu.VMEM((EXT_ROWS * EXT_COLS, C), F32),
            pltpu.VMEM((TILES, BS, C), BF16),
            pltpu.VMEM((2, WIDTH, C), F32),
            pltpu.VMEM((2, HEIGHT, BS // 2, C), F32),
            pltpu.VMEM((4, BS // 2, C), F32),
            dma((3,)),
            dma((NLAT,)), dma((NLAT,)),
            dma((CAP, NLON)), dma((CAP, NLON)),
            dma((CAP, NLON)), dma((CAP, NLON)),
            dma((8,)), dma((8,)),
        ],
        compiler_params=pltpu.CompilerParams(
            collective_id=1, has_side_effects=True, vmem_limit_bytes=48 << 20
        ),
    )(block_expert, owner, blocks, spreads, grads)


def local(fields, cotangent, kernel_bank, block_expert, owner):
    patches, cots, ids, kernels = send_blocks(block_expert, owner, fields, cotangent, kernel_bank)
    blocks, spreads, grads = compute(ids, patches, cots, kernels.reshape(NLON, 9, C, C))
    return return_blocks(block_expert, owner, blocks, spreads, grads.reshape(NLAT, 2, 9, C, C))


def solution(mesh):
    return jax.shard_map(
        local,
        mesh=mesh,
        in_specs=(
            P("lat", "lon", None),
            P("lat", "lon", None),
            P(("lat", "lon"), None, None, None),
            P("lat", "lon"),
            P(),
        ),
        out_specs=(
            P("lat", "lon", None),
            P("lat", "lon", None),
            P(("lat", "lon"), None, None, None),
        ),
        check_vma=False,
    )
```

```python
import jax
import jax.numpy as jnp
from jax import lax
from jax.experimental import pallas as pl
from jax.experimental.pallas import tpu as pltpu
from jax.sharding import PartitionSpec as P

BS = 16
CAP = 2
C = 128
NLAT = 8
NLON = 16
RING = 4
BLK = 16
BLON = 8
HEIGHT = 32
WIDTH = 128
ROWS = BS + 2
TILES = ROWS + 4
EXT_ROWS = HEIGHT + 2
EXT_COLS = WIDTH + 2 * BS
MESH = pl.DeviceIdType.MESH
F32 = jnp.float32
BF16 = jnp.bfloat16


def peer_lon(me, k):
    z, y = me // RING, lax.rem(me, RING)
    return lax.rem(z + k // RING, RING) * RING + lax.rem(y + lax.rem(k, RING), RING)


def source_lon(me, k):
    z, y = me // RING, lax.rem(me, RING)
    return lax.rem(z + RING - k // RING, RING) * RING + lax.rem(y + RING - lax.rem(k, RING), RING)


def greet(lat, lon, diagonal):
    barrier = pltpu.get_barrier_semaphore()

    def signal(device):
        pl.semaphore_signal(barrier, inc=1, device_id=device, device_id_type=MESH)

    @pl.loop(1, NLON)
    def _(k):
        signal((lat, peer_lon(lon, k)))

    @pl.loop(1, NLAT)
    def _(k):
        signal((lax.rem(lat + k, NLAT), lon))

    for up, side in diagonal:
        signal((lax.rem(lat + up, NLAT), lax.rem(lon + side, NLON)))
    pl.semaphore_wait(barrier, NLON - 1 + NLAT - 1 + len(diagonal))


DIAGONAL = ((NLAT - 1, NLON - 1), (NLAT - 1, 1), (1, NLON - 1), (1, 1))


def index_tables(expert_ref, owner_ref, column, local, slot_block):
    for b in range(BLK):
        stored = owner_ref[expert_ref[b // BLON, b % BLON]]
        group = stored >> 1
        column[b] = group & (NLON - 1)
        local[b] = (group >> 4) * 2 + (stored & 1)

    @pl.loop(0, NLON)
    def _(c):
        first = jnp.int32(-1)
        second = jnp.int32(-1)
        for b in range(BLK):
            here = column[b] == c
            second = jnp.where(here & (first >= 0), b, second)
            first = jnp.where(here & (first < 0), b, first)
        slot_block[2 * c] = first
        slot_block[2 * c + 1] = second


def fused_kernel(
    expert_ref, owner_ref, fields, cot, bank,
    outputs, result, bank_out,
    column, local, slot_block, block_slot, ids, rank, order, final, canvas, ext, side_l, side_r,
    cot_in, patch_in, cot_stage, patch_stage, id_stage, got_cot, got_patch, got_id, kern,
    pad, taps, wide_cot, shift, total, running, out_stage, spread_stage, got_out, got_spread, block,
    pair_stage, got_pair, chip_stage, got_chip, row_in, col_in, corner_in,
    load_sem, cot_load, halo_send, halo_recv, bank_send, bank_recv, pass_send, pass_recv,
    cot_send, cot_recv, patch_send, patch_recv, id_send, id_recv,
    out_send, out_recv, spread_send, spread_recv, pair_sem, chip_send, chip_recv, edge_send, edge_recv,
    own_sem,
):
    lat, lon = lax.axis_index("lat"), lax.axis_index("lon")
    core = lax.rem(lat, 2)
    chip = lat // 2
    other = lat + 1 - 2 * core

    def remote(source, target, send, recv, device):
        return pltpu.make_async_remote_copy(
            source, target, send, recv, device_id=device, device_id_type=MESH
        )

    load_fields = pltpu.make_async_copy(
        fields, ext.at[pl.ds(1, HEIGHT), pl.ds(BS, WIDTH)], load_sem.at[0]
    )
    load_fields.start()
    load_bank = pltpu.make_async_copy(bank, kern.at[pl.ds(2 * lat, 2)], load_sem.at[1])
    load_bank.start()

    def load_cot(b):
        rows = pl.ds(pl.multiple_of((b // BLON) * BS, BS), BS)
        cols = pl.ds(pl.multiple_of(lax.rem(b, BLON) * BS, BS), BS)
        return pltpu.make_async_copy(cot.at[rows, cols], cot_in.at[b], cot_load.at[b])

    @pl.loop(0, BLK)
    def _(b):
        load_cot(b).start()

    index_tables(expert_ref, owner_ref, column, local, slot_block)
    for b in range(BLK):
        c = column[b]
        block_slot[b] = 2 * c + jnp.where(slot_block[2 * c + 1] == b, 1, 0)
    greet(lat, lon, DIAGONAL)

    up, down = lax.rem(lat + NLAT - 1, NLAT), lax.rem(lat + 1, NLAT)
    left, right = lax.rem(lon + NLON - 1, NLON), lax.rem(lon + 1, NLON)
    top, bottom = pl.ds(0, 1), pl.ds(HEIGHT - 1, 1)
    first, last = pl.ds(0, BS), pl.ds(WIDTH - BS, BS)
    all_rows, all_cols = pl.ds(0, HEIGHT), pl.ds(0, WIDTH)
    mid_rows, mid_cols = pl.ds(1, HEIGHT), pl.ds(BS, WIDTH)
    low, high = pl.ds(0, BS), pl.ds(BS + WIDTH, BS)
    zero, end = pl.ds(0, 1), pl.ds(EXT_ROWS - 1, 1)
    moves = (
        (top, all_cols, end, mid_cols, (up, lon)),
        (bottom, all_cols, zero, mid_cols, (down, lon)),
        (all_rows, first, mid_rows, high, (lat, left)),
        (all_rows, last, mid_rows, low, (lat, right)),
        (top, first, end, high, (up, left)),
        (top, last, end, low, (up, right)),
        (bottom, first, zero, high, (down, left)),
        (bottom, last, zero, low, (down, right)),
    )
    halos = []
    for i, (rows, cols, to_rows, to_cols, device) in enumerate(moves):
        copy = remote(
            fields.at[rows, cols], ext.at[to_rows, to_cols], halo_send.at[i], halo_recv.at[i], device
        )
        copy.start()
        halos.append(copy)

    def bank_copy(j):
        return remote(
            bank, kern.at[pl.ds(2 * lat, 2)], bank_send.at[j], bank_recv.at[j],
            (lax.rem(lat + 2 * j, NLAT), lon),
        )

    def pass_copy(j):
        part = kern.at[pl.ds(2 * lax.rem(lat + NLAT - 2 * j, NLAT), 2)]
        return remote(part, part, pass_send.at[j], pass_recv.at[j], (other, lon))

    share_bank = remote(
        bank, kern.at[pl.ds(2 * lat, 2)], pass_send.at[0], pass_recv.at[0], (other, lon)
    )
    for j in range(1, RING):
        bank_copy(j).start()
    share_bank.start()

    def cot_copy(k, r):
        dst = peer_lon(lon, k)
        return remote(
            cot_stage.at[dst, r], got_cot.at[2 * lon + r], cot_send.at[r, k], cot_recv.at[r, k], (lat, dst)
        )

    def patch_copy(k, r):
        dst = peer_lon(lon, k)
        return remote(
            patch_stage.at[dst, r], got_patch.at[2 * lon + r], patch_send.at[r, k], patch_recv.at[r, k],
            (lat, dst),
        )

    def id_copy(k):
        dst = peer_lon(lon, k)
        return remote(id_stage.at[dst], got_id.at[lon], id_send.at[k], id_recv.at[k], (lat, dst))

    def out_copy(k, r):
        dst = source_lon(lon, k)
        return remote(
            out_stage.at[2 * dst + r], got_out.at[2 * lon + r], out_send.at[r, k], out_recv.at[r, k], (lat, dst)
        )

    def spread_copy(k, r):
        dst = source_lon(lon, k)
        return remote(
            spread_stage.at[2 * dst + r], got_spread.at[2 * lon + r], spread_send.at[r, k],
            spread_recv.at[r, k], (lat, dst),
        )

    def own(source, target, i):
        return pltpu.make_async_copy(source, target, own_sem.at[i])

    own_slots = pl.ds(2 * lon, CAP)
    own_cot = own(cot_stage.at[lon], got_cot.at[own_slots], 0)
    own_patch = own(patch_stage.at[lon], got_patch.at[own_slots], 1)
    own_id = own(id_stage.at[lon], got_id.at[lon], 2)
    own_out = own(out_stage.at[own_slots], got_out.at[own_slots], 3)
    own_spread = own(spread_stage.at[own_slots], got_spread.at[own_slots], 4)

    lane = lax.broadcasted_iota(jnp.int32, (1, C), 1)

    @pl.loop(0, NLON)
    def _(c):
        found = [slot_block[2 * c + r] for r in range(CAP)]
        named = [jnp.where(f < 0, NLON, local[jnp.maximum(f, 0)]) for f in found]
        id_stage[c] = jnp.where(lane == 0, named[0], named[1])

    @pl.loop(1, NLON)
    def _(k):
        id_copy(k).start()

    @pl.loop(0, BLK)
    def _(b):
        load_cot(b).wait()

    def stage_cot(k, r):
        dst = peer_lon(lon, k)
        cot_stage[dst, r] = cot_in[jnp.maximum(slot_block[2 * dst + r], 0)]

    @pl.loop(1, NLON)
    def _(k):
        stage_cot(k, 0)
        cot_copy(k, 0).start()

    load_fields.wait()
    for copy in halos:
        copy.wait()

    @pl.when(lat == 0)
    def _():
        ext[0] = jnp.zeros((EXT_COLS, C), BF16)

    @pl.when(lat == NLAT - 1)
    def _():
        ext[EXT_ROWS - 1] = jnp.zeros((EXT_COLS, C), BF16)

    @pl.loop(0, EXT_ROWS)
    def _(r):
        canvas[pl.ds(pl.multiple_of(r * EXT_COLS, BS), EXT_COLS), :] = ext[r].astype(F32)

    @pl.loop(0, BLON)
    def _(k):
        side_l[k, pl.ds(0, EXT_ROWS)] = canvas[
            pl.ds(k * BS + BS - 1, EXT_ROWS, stride=EXT_COLS), :
        ].astype(BF16)
        side_r[k, pl.ds(0, EXT_ROWS)] = canvas[
            pl.ds(k * BS + 2 * BS, EXT_ROWS, stride=EXT_COLS), :
        ].astype(BF16)

    @pl.loop(0, BLK)
    def _(b):
        row = pl.multiple_of((b // BLON) * BS, BS)
        col = lax.rem(b, BLON)
        patch_in[b, pl.ds(0, ROWS)] = ext[
            pl.ds(row, ROWS), pl.ds(pl.multiple_of((col + 1) * BS, BS), BS), :
        ]
        patch_in[b, pl.ds(ROWS, 2)] = side_l[col, pl.ds(row, 2 * BS)].reshape(2, BS, C)
        patch_in[b, pl.ds(ROWS + 2, 2)] = side_r[col, pl.ds(row, 2 * BS)].reshape(2, BS, C)

    def stage_patch(k, r):
        dst = peer_lon(lon, k)
        patch_stage[dst, r] = patch_in[jnp.maximum(slot_block[2 * dst + r], 0)]

    @pl.loop(1, NLON)
    def _(k):
        stage_patch(k, 0)
        patch_copy(k, 0).start()

    @pl.loop(1, NLON)
    def _(k):
        stage_cot(k, 1)
        cot_copy(k, 1).start()

    @pl.loop(1, NLON)
    def _(k):
        stage_patch(k, 1)
        patch_copy(k, 1).start()

    for r in range(CAP):
        stage_cot(0, r)
        stage_patch(0, r)
    own_cot.start()
    own_patch.start()
    own_id.start()

    load_bank.wait()
    for j in range(1, RING):
        bank_copy(j).wait()
        pass_copy(j).start()

    own_id.wait()

    @pl.loop(1, NLON)
    def _(k):
        id_copy(k).wait()

    read_ids = pltpu.make_async_copy(got_id, ids, load_sem.at[2])
    read_ids.start()
    read_ids.wait()
    canvas[...] = jnp.zeros_like(canvas)
    wide_cot[...] = jnp.zeros_like(wide_cot)

    @pl.loop(0, NLON)
    def _(c):
        for r in range(CAP):
            mine = ids[c, 0, r]
            here = 2 * c + r
            before = jnp.int32(0)
            for s in range(NLON * CAP):
                it = ids[s // CAP, 0, s % CAP]
                before += jnp.where((it < mine) | ((it == mine) & (s < here)), 1, 0)
            rank[here] = before

    @pl.loop(0, NLON * CAP)
    def _(j):
        slot = jnp.int32(0)
        for s in range(NLON * CAP):
            slot = jnp.where(rank[s] == j, s, slot)
        order[j] = slot

    @pl.loop(0, NLON)
    def _(e):
        upto = jnp.int32(0)
        some = jnp.int32(0)
        for s in range(NLON * CAP):
            it = ids[s // CAP, 0, s % CAP]
            upto += jnp.where(it <= e, 1, 0)
            some += jnp.where(it == e, 1, 0)
        final[e] = jnp.where(some > 0, upto - 1, -1)

    share_bank.wait()
    for j in range(1, RING):
        pass_copy(j).wait()

    def build_taps(slot):
        pad[:, pl.ds(8, BS), :] = got_patch[slot, pl.ds(0, ROWS)].astype(F32)
        pad[:, 7, :] = got_patch[slot, pl.ds(ROWS, 2)].reshape(2 * BS, C)[:ROWS].astype(F32)
        pad[:, BS + 8, :] = got_patch[slot, pl.ds(ROWS + 2, 2)].reshape(2 * BS, C)[:ROWS].astype(F32)
        for b in range(3):
            taps[:, pl.ds(b * C, C)] = pad[:, pl.ds(7 + b, BS), :].reshape(ROWS * BS, C).astype(BF16)

    def convolve(slot, e):
        build_taps(slot)
        cots = got_cot[slot].reshape(BS * BS, C)
        for a in range(3):
            wide_cot[pl.ds(a * BS, BS * BS), pl.ds(a * C, C)] = cots
        weights = [kern[e, pl.ds(3 * a, 3)].reshape(3 * C, C) for a in range(3)]
        sums = jnp.zeros((BS * BS, C), F32)
        for a in range(3):
            sums += jnp.dot(taps[pl.ds(a * BS, BS * BS), :], weights[a], preferred_element_type=F32)
        out_stage[slot] = sums.astype(BF16).reshape(BS, BS, C)
        grid = lax.dot_general(
            wide_cot[...], jnp.concatenate(weights, axis=1), (((1,), (1,)), ((), ())),
            preferred_element_type=F32,
        )
        shift[0, :, pl.ds(8, BS), :] = grid[:, :C].reshape(ROWS, BS, C)
        shift[1, :, pl.ds(8, BS), :] = grid[:, 2 * C:].reshape(ROWS, BS, C)
        place = lax.broadcasted_iota(jnp.int32, (ROWS, BS, C), 1)
        main = grid[:, C:2 * C].reshape(ROWS, BS, C)
        main += jnp.where(place == BS - 1, 0.0, shift[0, :, pl.ds(9, BS), :])
        main += jnp.where(place == 0, 0.0, shift[1, :, pl.ds(7, BS), :])
        spread_stage[slot, pl.ds(0, ROWS)] = main.astype(BF16)
        tail = jnp.zeros((2 * BS - ROWS, C), F32)
        lefts = jnp.concatenate([shift[0, :, 8, :], tail], axis=0)
        rights = jnp.concatenate([shift[1, :, BS + 7, :], tail], axis=0)
        spread_stage[slot, pl.ds(ROWS, 2)] = lefts.astype(BF16).reshape(2, BS, C)
        spread_stage[slot, pl.ds(ROWS + 2, 2)] = rights.astype(BF16).reshape(2, BS, C)

    own_cot.wait()
    own_patch.wait()

    @pl.loop(0, CAP * NLON)
    def _(step):
        r, k = step // NLON, lax.rem(step, NLON)
        source = source_lon(lon, k)

        @pl.when(k > 0)
        def _():
            cot_copy(k, r).wait_recv()
            patch_copy(k, r).wait_recv()

        convolve(2 * source + r, jnp.minimum(ids[source, 0, r], NLON - 1))

        @pl.when(k > 0)
        def _():
            spread_copy(k, r).start()

        @pl.when((k > 0) & (r == 0))
        def _():
            out_copy(k, r).start()

    @pl.loop(1, NLON)
    def _(k):
        out_copy(k, 1).start()

    own_out.start()
    own_spread.start()

    @pl.loop(0, NLON * CAP)
    def _(j):
        slot = order[j]
        previous = order[jnp.maximum(j - 1, 0)]
        now = ids[slot >> 1, 0, slot & 1]
        same = (j > 0) & (ids[previous >> 1, 0, previous & 1] == now)
        build_taps(slot)
        cots = got_cot[slot].reshape(BS * BS, C)
        for a in range(3):
            term = lax.dot_general(
                taps[pl.ds(a * BS, BS * BS), :], cots, (((0,), (0,)), ((), ())),
                preferred_element_type=F32,
            ).reshape(3, C, C)
            sums = jnp.where(same, total[pl.ds(3 * a, 3)], 0.0) + term
            total[pl.ds(3 * a, 3)] = sums
            running[j, pl.ds(3 * a, 3)] = sums.astype(BF16)

    def gradient(e):
        at = final[e]
        return jnp.where(at < 0, 0.0, running[jnp.maximum(at, 0)].astype(F32))

    @pl.loop(0, NLAT)
    def _(i):
        e = 4 * (i // 2) + 2 * (1 - core) + lax.rem(i, 2)
        pair_stage[i] = gradient(e).astype(BF16)

    pair = remote(pair_stage, got_pair, pair_sem.at[0], pair_sem.at[1], (other, lon))
    pair.start()

    def chip_copy(j):
        to = lax.rem(chip + j, RING)
        return remote(
            chip_stage.at[to], got_chip.at[chip], chip_send.at[j], chip_recv.at[j], (2 * to + core, lon)
        )

    pair.wait()

    @pl.loop(1, RING)
    def _(j):
        to = lax.rem(chip + j, RING)
        for i in range(2):
            both = gradient(4 * to + 2 * core + i) + got_pair[2 * to + i].astype(F32)
            chip_stage[to, i] = both.astype(BF16)
        chip_copy(j).start()

    for i in range(2):
        bank_out[i] = gradient(4 * chip + 2 * core + i) + got_pair[2 * chip + i].astype(F32)

    own_spread.wait()

    @pl.loop(1, NLON)
    def _(k):
        for r in range(CAP):
            spread_copy(k, r).wait_recv()

    @pl.loop(0, BLK)
    def _(b):
        bi, bj = b // BLON, lax.rem(b, BLON)
        base = bi * BS * EXT_COLS + (bj + 1) * BS
        block[...] = got_spread[block_slot[b]]

        @pl.loop(0, ROWS)
        def _(i):
            at = pl.ds(pl.multiple_of(base + i * EXT_COLS, BS), BS)
            canvas[at, :] += block[i].astype(F32)

        lefts = block[pl.ds(ROWS, 2)].reshape(2 * BS, C)[:ROWS].astype(F32)
        rights = block[pl.ds(ROWS + 2, 2)].reshape(2 * BS, C)[:ROWS].astype(F32)
        canvas[pl.ds(base - 1, ROWS, stride=EXT_COLS), :] += lefts
        canvas[pl.ds(base + BS, ROWS, stride=EXT_COLS), :] += rights

    grid = canvas.reshape(EXT_ROWS, EXT_COLS, C)
    half = BS // 2
    edge_low, edge_high = pl.ds(half, half), pl.ds(BS + WIDTH, half)
    edges = (
        (grid.at[0, mid_cols], row_in.at[0], (up, lon)),
        (grid.at[EXT_ROWS - 1, mid_cols], row_in.at[1], (down, lon)),
        (grid.at[mid_rows, edge_low], col_in.at[0], (lat, left)),
        (grid.at[mid_rows, edge_high], col_in.at[1], (lat, right)),
        (grid.at[0, edge_low], corner_in.at[0], (up, left)),
        (grid.at[0, edge_high], corner_in.at[1], (up, right)),
        (grid.at[EXT_ROWS - 1, edge_low], corner_in.at[2], (down, left)),
        (grid.at[EXT_ROWS - 1, edge_high], corner_in.at[3], (down, right)),
    )
    edge_copies = []
    for i, (source, target, device) in enumerate(edges):
        copy = remote(source, target, edge_send.at[i], edge_recv.at[i], device)
        copy.start()
        edge_copies.append(copy)

    @pl.loop(1, RING)
    def _(j):
        chip_copy(j).wait()
        back = lax.rem(chip + RING - j, RING)
        for i in range(2):
            bank_out[i] += got_chip[back, i].astype(F32)

    own_out.wait()

    @pl.loop(1, NLON)
    def _(k):
        for r in range(CAP):
            out_copy(k, r).wait_recv()

    @pl.loop(0, BLK)
    def _(b):
        bi, bj = b // BLON, lax.rem(b, BLON)
        outputs[
            pl.ds(pl.multiple_of(bi * BS, BS), BS), pl.ds(pl.multiple_of(bj * BS, BS), BS), :
        ] = got_out[block_slot[b]]

    for copy in edge_copies:
        copy.wait()
    from_down = jnp.where(lat < NLAT - 1, 1.0, 0.0).astype(F32)
    from_up = jnp.where(lat > 0, 1.0, 0.0).astype(F32)
    upper, lower = EXT_COLS, HEIGHT * EXT_COLS
    canvas[pl.ds(lower + BS, WIDTH), :] += row_in[0] * from_down
    canvas[pl.ds(upper + BS, WIDTH), :] += row_in[1] * from_up

    @pl.loop(0, HEIGHT)
    def _(i):
        start = pl.multiple_of((i + 1) * EXT_COLS, BS)
        canvas[pl.ds(start + BS + WIDTH - half, half), :] += col_in[0, i]
        canvas[pl.ds(start + BS, half), :] += col_in[1, i]

    canvas[pl.ds(lower + BS + WIDTH - half, half), :] += corner_in[0] * from_down
    canvas[pl.ds(lower + BS, half), :] += corner_in[1] * from_down
    canvas[pl.ds(upper + BS + WIDTH - half, half), :] += corner_in[2] * from_up
    canvas[pl.ds(upper + BS, half), :] += corner_in[3] * from_up

    @pl.loop(0, HEIGHT)
    def _(i):
        start = pl.multiple_of((i + 1) * EXT_COLS + BS, BS)
        result[i] = canvas[pl.ds(start, WIDTH), :].astype(BF16)

    @pl.loop(1, NLON)
    def _(k):
        for r in range(CAP):
            cot_copy(k, r).wait_send()
            patch_copy(k, r).wait_send()
            spread_copy(k, r).wait_send()
            out_copy(k, r).wait_send()


def local(fields, cotangent, kernel_bank, block_expert, owner):
    hbm = pl.BlockSpec(memory_space=pltpu.HBM)
    smem = pl.BlockSpec(memory_space=pltpu.SMEM)
    vmem = pl.BlockSpec(memory_space=pltpu.VMEM)
    dma = pltpu.SemaphoreType.DMA
    slots = NLON * CAP
    return pl.pallas_call(
        fused_kernel,
        out_shape=(
            jax.ShapeDtypeStruct((HEIGHT, WIDTH, C), BF16),
            jax.ShapeDtypeStruct((HEIGHT, WIDTH, C), BF16),
            jax.ShapeDtypeStruct((2, 9, C, C), F32),
        ),
        in_specs=[smem, smem, hbm, hbm, hbm],
        out_specs=(vmem, vmem, vmem),
        scratch_shapes=[
            pltpu.SMEM((BLK,), jnp.int32),
            pltpu.SMEM((BLK,), jnp.int32),
            pltpu.SMEM((slots,), jnp.int32),
            pltpu.SMEM((BLK,), jnp.int32),
            pltpu.SMEM((NLON, 1, C), jnp.int32),
            pltpu.SMEM((slots,), jnp.int32),
            pltpu.SMEM((slots,), jnp.int32),
            pltpu.SMEM((NLON,), jnp.int32),
            pltpu.VMEM((EXT_ROWS * EXT_COLS, C), F32),
            pltpu.VMEM((EXT_ROWS, EXT_COLS, C), BF16),
            pltpu.VMEM((BLON, 3 * BS, C), BF16),
            pltpu.VMEM((BLON, 3 * BS, C), BF16),
            pltpu.VMEM((BLK, BS, BS, C), BF16),
            pltpu.VMEM((BLK, TILES, BS, C), BF16),
            pltpu.VMEM((NLON, CAP, BS, BS, C), BF16),
            pltpu.VMEM((NLON, CAP, TILES, BS, C), BF16),
            pltpu.VMEM((NLON, 1, C), jnp.int32),
            pltpu.VMEM((slots, BS, BS, C), BF16),
            pltpu.VMEM((slots, TILES, BS, C), BF16),
            pltpu.VMEM((NLON, 1, C), jnp.int32),
            pltpu.VMEM((NLON, 9, C, C), BF16),
            pltpu.VMEM((ROWS, 2 * BS, C), F32),
            pltpu.VMEM((ROWS * BS, 3 * C), BF16),
            pltpu.VMEM((ROWS * BS, 3 * C), BF16),
            pltpu.VMEM((2, ROWS, 2 * BS, C), F32),
            pltpu.VMEM((9, C, C), F32),
            pltpu.VMEM((slots, 9, C, C), BF16),
            pltpu.VMEM((slots, BS, BS, C), BF16),
            pltpu.VMEM((slots, TILES, BS, C), BF16),
            pltpu.VMEM((slots, BS, BS, C), BF16),
            pltpu.VMEM((slots, TILES, BS, C), BF16),
            pltpu.VMEM((TILES, BS, C), BF16),
            pltpu.VMEM((NLAT, 9, C, C), BF16),
            pltpu.VMEM((NLAT, 9, C, C), BF16),
            pltpu.VMEM((RING, 2, 9, C, C), BF16),
            pltpu.VMEM((RING, 2, 9, C, C), BF16),
            pltpu.VMEM((2, WIDTH, C), F32),
            pltpu.VMEM((2, HEIGHT, BS // 2, C), F32),
            pltpu.VMEM((4, BS // 2, C), F32),
            dma((3,)), dma((BLK,)),
            dma((8,)), dma((8,)),
            dma((RING,)), dma((RING,)),
            dma((RING,)), dma((RING,)),
            dma((CAP, NLON)), dma((CAP, NLON)),
            dma((CAP, NLON)), dma((CAP, NLON)),
            dma((NLON,)), dma((NLON,)),
            dma((CAP, NLON)), dma((CAP, NLON)),
            dma((CAP, NLON)), dma((CAP, NLON)),
            dma((2,)),
            dma((RING,)), dma((RING,)),
            dma((8,)), dma((8,)),
            dma((5,)),
        ],
        compiler_params=pltpu.CompilerParams(
            collective_id=0, has_side_effects=True, vmem_limit_bytes=62 << 20
        ),
    )(block_expert, owner, fields, cotangent, kernel_bank)


def solution(mesh):
    return jax.shard_map(
        local,
        mesh=mesh,
        in_specs=(
            P("lat", "lon", None),
            P("lat", "lon", None),
            P(("lat", "lon"), None, None, None),
            P("lat", "lon"),
            P(),
        ),
        out_specs=(
            P("lat", "lon", None),
            P("lat", "lon", None),
            P(("lat", "lon"), None, None, None),
        ),
        check_vma=False,
    )
```

```python
import jax
import jax.numpy as jnp
from jax import lax
from jax.experimental import pallas as pl
from jax.experimental.pallas import tpu as pltpu
from jax.sharding import PartitionSpec as P

BS = 16
CAP = 2
C = 128
NLAT = 8
NLON = 16
RING = 4
BLK = 16
BLON = 8
HEIGHT = 32
WIDTH = 128
ROWS = BS + 2
SIDE = 24
TILES = ROWS + 3
EXT_ROWS = HEIGHT + 2
EXT_COLS = WIDTH + 2 * BS
MESH = pl.DeviceIdType.MESH
F32 = jnp.float32
BF16 = jnp.bfloat16


def peer_lon(me, k):
    z, y = me // RING, lax.rem(me, RING)
    return lax.rem(z + k // RING, RING) * RING + lax.rem(y + lax.rem(k, RING), RING)


def source_lon(me, k):
    z, y = me // RING, lax.rem(me, RING)
    return lax.rem(z + RING - k // RING, RING) * RING + lax.rem(y + RING - lax.rem(k, RING), RING)


def greet(lat, lon, diagonal):
    barrier = pltpu.get_barrier_semaphore()

    def signal(device):
        pl.semaphore_signal(barrier, inc=1, device_id=device, device_id_type=MESH)

    @pl.loop(1, NLON)
    def _(k):
        signal((lat, peer_lon(lon, k)))

    @pl.loop(1, NLAT)
    def _(k):
        signal((lax.rem(lat + k, NLAT), lon))

    for up, side in diagonal:
        signal((lax.rem(lat + up, NLAT), lax.rem(lon + side, NLON)))


def await_greetings(diagonal):
    pl.semaphore_wait(pltpu.get_barrier_semaphore(), NLON - 1 + NLAT - 1 + len(diagonal))


DIAGONAL = ((NLAT - 1, NLON - 1), (NLAT - 1, 1), (1, NLON - 1), (1, 1))


def index_tables(expert_ref, owner_ref, column, local, slot_block):
    for b in range(BLK):
        stored = owner_ref[expert_ref[b // BLON, b % BLON]]
        group = stored >> 1
        column[b] = group & (NLON - 1)
        local[b] = (group >> 4) * 2 + (stored & 1)

    @pl.loop(0, NLON)
    def _(c):
        first = jnp.int32(-1)
        second = jnp.int32(-1)
        for b in range(BLK):
            here = column[b] == c
            second = jnp.where(here & (first >= 0), b, second)
            first = jnp.where(here & (first < 0), b, first)
        slot_block[2 * c] = first
        slot_block[2 * c + 1] = second


def fused_kernel(
    expert_ref, owner_ref, fields, cot, bank,
    outputs, result, bank_out,
    home, local, slot_block, block_slot, ids, rank, order, final, canvas, ext,
    col_stage, col_got, side_stage, sides, cot_in, patch_in, cot_stage, patch_stage, id_stage, got_cot, got_patch, got_id, kern,
    pad, taps, wide_cot, shift, total, running, out_stage, spread_stage, got_out, got_spread, block,
    pair_stage, got_pair, chip_stage, got_chip, row_in, col_in, corner_in,
    load_sem, cot_load, halo_send, halo_recv, bank_send, bank_recv, pass_send, pass_recv,
    cot_send, cot_recv, patch_send, patch_recv, id_send, id_recv,
    out_send, out_recv, spread_send, spread_recv, pair_sem, chip_send, chip_recv, edge_send, edge_recv,
    own_sem,
):
    lat, lon = lax.axis_index("lat"), lax.axis_index("lon")
    core = lax.rem(lat, 2)
    chip = lat // 2
    other = lat + 1 - 2 * core

    def remote(source, target, send, recv, device):
        return pltpu.make_async_remote_copy(
            source, target, send, recv, device_id=device, device_id_type=MESH
        )

    greet(lat, lon, DIAGONAL)
    load_fields = pltpu.make_async_copy(
        fields, ext.at[pl.ds(1, HEIGHT), pl.ds(BS, WIDTH)], load_sem.at[0]
    )
    load_fields.start()
    load_bank = pltpu.make_async_copy(bank, kern.at[pl.ds(2 * lat, 2)], load_sem.at[1])
    load_bank.start()

    def load_cot(b):
        rows = pl.ds(pl.multiple_of((b // BLON) * BS, BS), BS)
        cols = pl.ds(pl.multiple_of(lax.rem(b, BLON) * BS, BS), BS)
        return pltpu.make_async_copy(cot.at[rows, cols], cot_in.at[b], cot_load.at[b])

    @pl.loop(0, BLK)
    def _(b):
        load_cot(b).start()

    index_tables(expert_ref, owner_ref, home, local, slot_block)
    for b in range(BLK):
        c = home[b]
        block_slot[b] = 2 * c + jnp.where(slot_block[2 * c + 1] == b, 1, 0)
    await_greetings(DIAGONAL)

    up, down = lax.rem(lat + NLAT - 1, NLAT), lax.rem(lat + 1, NLAT)
    left, right = lax.rem(lon + NLON - 1, NLON), lax.rem(lon + 1, NLON)
    top, bottom = pl.ds(0, 1), pl.ds(HEIGHT - 1, 1)
    first, last = pl.ds(0, BS), pl.ds(WIDTH - BS, BS)
    all_cols, mid_cols = pl.ds(0, WIDTH), pl.ds(BS, WIDTH)
    low, high = pl.ds(0, BS), pl.ds(BS + WIDTH, BS)
    zero, end = pl.ds(0, 1), pl.ds(EXT_ROWS - 1, 1)
    moves = (
        (top, all_cols, end, mid_cols, (up, lon)),
        (bottom, all_cols, zero, mid_cols, (down, lon)),
        (top, first, end, high, (up, left)),
        (top, last, end, low, (up, right)),
        (bottom, first, zero, high, (down, left)),
        (bottom, last, zero, low, (down, right)),
    )
    halos = []
    for i, (rows, cols, to_rows, to_cols, device) in enumerate(moves):
        copy = remote(
            fields.at[rows, cols], ext.at[to_rows, to_cols], halo_send.at[i], halo_recv.at[i], device
        )
        copy.start()
        halos.append(copy)

    def column(where):
        return pl.ds(EXT_COLS + where, HEIGHT, stride=EXT_COLS)

    outer_left, inner_left, inner_right, outer_right = BS - 1, BS, BS + WIDTH - 1, BS + WIDTH
    load_fields.wait()

    def widen(r):
        canvas[pl.ds(pl.multiple_of(r * EXT_COLS, BS), EXT_COLS), :] = ext[r].astype(F32)

    @pl.loop(1, HEIGHT + 1)
    def _(r):
        widen(r)

    col_stage[0] = canvas[column(inner_left), :].astype(BF16)
    col_stage[1] = canvas[column(inner_right), :].astype(BF16)
    for i, device in enumerate(((lat, left), (lat, right))):
        copy = remote(col_stage.at[i], col_got.at[i], halo_send.at[6 + i], halo_recv.at[6 + i], device)
        copy.start()
        halos.append(copy)

    def bank_copy(j):
        return remote(
            bank, kern.at[pl.ds(2 * lat, 2)], bank_send.at[j], bank_recv.at[j],
            (lax.rem(lat + 2 * j, NLAT), lon),
        )

    def pass_copy(j):
        part = kern.at[pl.ds(2 * lax.rem(lat + NLAT - 2 * j, NLAT), 2)]
        return remote(part, part, pass_send.at[j], pass_recv.at[j], (other, lon))

    share_bank = remote(
        bank, kern.at[pl.ds(2 * lat, 2)], pass_send.at[0], pass_recv.at[0], (other, lon)
    )
    for j in range(1, RING):
        bank_copy(j).start()
    share_bank.start()

    def cot_copy(k, r):
        dst = peer_lon(lon, k)
        return remote(
            cot_stage.at[dst, r], got_cot.at[2 * lon + r], cot_send.at[r, k], cot_recv.at[r, k], (lat, dst)
        )

    def patch_copy(k, r):
        dst = peer_lon(lon, k)
        return remote(
            patch_stage.at[dst, r], got_patch.at[2 * lon + r], patch_send.at[r, k], patch_recv.at[r, k],
            (lat, dst),
        )

    def id_copy(k):
        dst = peer_lon(lon, k)
        return remote(id_stage.at[dst], got_id.at[lon], id_send.at[k], id_recv.at[k], (lat, dst))

    def out_copy(k, r):
        dst = source_lon(lon, k)
        return remote(
            out_stage.at[2 * dst + r], got_out.at[2 * lon + r], out_send.at[r, k], out_recv.at[r, k], (lat, dst)
        )

    def spread_copy(k, r):
        dst = source_lon(lon, k)
        return remote(
            spread_stage.at[2 * dst + r], got_spread.at[2 * lon + r], spread_send.at[r, k],
            spread_recv.at[r, k], (lat, dst),
        )

    def own(source, target, i):
        return pltpu.make_async_copy(source, target, own_sem.at[i])

    own_slots = pl.ds(2 * lon, CAP)
    own_cot = own(cot_stage.at[lon], got_cot.at[own_slots], 0)
    own_patch = own(patch_stage.at[lon], got_patch.at[own_slots], 1)
    own_id = own(id_stage.at[lon], got_id.at[lon], 2)
    own_out = own(out_stage.at[own_slots], got_out.at[own_slots], 3)
    own_spread = own(spread_stage.at[own_slots], got_spread.at[own_slots], 4)

    lane = lax.broadcasted_iota(jnp.int32, (1, C), 1)

    @pl.loop(0, NLON)
    def _(c):
        found = [slot_block[2 * c + r] for r in range(CAP)]
        named = [jnp.where(f < 0, NLON, local[jnp.maximum(f, 0)]) for f in found]
        id_stage[c] = jnp.where(lane == 0, named[0], named[1])

    @pl.loop(1, NLON)
    def _(k):
        id_copy(k).start()

    @pl.loop(0, BLK)
    def _(b):
        load_cot(b).wait()

    def stage_cot(k, r):
        dst = peer_lon(lon, k)
        cot_stage[dst, r] = cot_in[jnp.maximum(slot_block[2 * dst + r], 0)]

    @pl.loop(1, NLON)
    def _(k):
        stage_cot(k, 0)
        cot_copy(k, 0).start()

    for copy in halos:
        copy.wait()

    @pl.when(lat == 0)
    def _():
        ext[0] = jnp.zeros((EXT_COLS, C), BF16)

    @pl.when(lat == NLAT - 1)
    def _():
        ext[EXT_ROWS - 1] = jnp.zeros((EXT_COLS, C), BF16)

    widen(0)
    widen(EXT_ROWS - 1)
    canvas[column(outer_right), :] = col_got[0].astype(F32)
    canvas[column(outer_left), :] = col_got[1].astype(F32)

    @pl.loop(0, BLK)
    def _(b):
        row = pl.multiple_of((b // BLON) * BS, BS)
        col = pl.multiple_of((lax.rem(b, BLON) + 1) * BS, BS)
        patch_in[b, pl.ds(0, ROWS)] = ext[pl.ds(row, ROWS), pl.ds(col, BS), :]
        start = row * EXT_COLS + col
        sides[pl.ds(0, ROWS), :] = canvas[pl.ds(start - 1, ROWS, stride=EXT_COLS), :]
        sides[pl.ds(SIDE, ROWS), :] = canvas[pl.ds(start + BS, ROWS, stride=EXT_COLS), :]
        patch_in[b, pl.ds(ROWS, 3)] = sides[...].astype(BF16).reshape(3, BS, C)

    def stage_patch(k, r):
        dst = peer_lon(lon, k)
        patch_stage[dst, r] = patch_in[jnp.maximum(slot_block[2 * dst + r], 0)]

    @pl.loop(1, NLON)
    def _(k):
        stage_patch(k, 0)
        patch_copy(k, 0).start()

    @pl.loop(1, NLON)
    def _(k):
        stage_cot(k, 1)
        cot_copy(k, 1).start()

    @pl.loop(1, NLON)
    def _(k):
        stage_patch(k, 1)
        patch_copy(k, 1).start()

    for r in range(CAP):
        stage_cot(0, r)
        stage_patch(0, r)
    own_cot.start()
    own_patch.start()
    own_id.start()

    load_bank.wait()
    for j in range(1, RING):
        bank_copy(j).wait()
        pass_copy(j).start()

    own_id.wait()

    @pl.loop(1, NLON)
    def _(k):
        id_copy(k).wait()

    read_ids = pltpu.make_async_copy(got_id, ids, load_sem.at[2])
    read_ids.start()
    read_ids.wait()
    canvas[...] = jnp.zeros_like(canvas)
    wide_cot[...] = jnp.zeros_like(wide_cot)

    @pl.loop(0, NLON)
    def _(c):
        for r in range(CAP):
            mine = ids[c, 0, r]
            here = 2 * c + r
            before = jnp.int32(0)
            for s in range(NLON * CAP):
                it = ids[s // CAP, 0, s % CAP]
                before += jnp.where((it < mine) | ((it == mine) & (s < here)), 1, 0)
            rank[here] = before

    @pl.loop(0, NLON * CAP)
    def _(j):
        slot = jnp.int32(0)
        for s in range(NLON * CAP):
            slot = jnp.where(rank[s] == j, s, slot)
        order[j] = slot

    @pl.loop(0, NLON)
    def _(e):
        upto = jnp.int32(0)
        some = jnp.int32(0)
        for s in range(NLON * CAP):
            it = ids[s // CAP, 0, s % CAP]
            upto += jnp.where(it <= e, 1, 0)
            some += jnp.where(it == e, 1, 0)
        final[e] = jnp.where(some > 0, upto - 1, -1)

    share_bank.wait()
    for j in range(1, RING):
        pass_copy(j).wait()

    def build_taps(slot):
        pad[:, pl.ds(8, BS), :] = got_patch[slot, pl.ds(0, ROWS)].astype(F32)
        both = got_patch[slot, pl.ds(ROWS, 3)].reshape(3 * BS, C).astype(F32)
        pad[:, 7, :] = both[:ROWS]
        pad[:, BS + 8, :] = both[SIDE:SIDE + ROWS]
        for b in range(3):
            taps[:, pl.ds(b * C, C)] = pad[:, pl.ds(7 + b, BS), :].reshape(ROWS * BS, C).astype(BF16)

    def convolve(slot, e):
        build_taps(slot)
        cots = got_cot[slot].reshape(BS * BS, C)
        for a in range(3):
            wide_cot[pl.ds(a * BS, BS * BS), pl.ds(a * C, C)] = cots
        weights = [kern[e, pl.ds(3 * a, 3)].reshape(3 * C, C) for a in range(3)]
        sums = jnp.zeros((BS * BS, C), F32)
        for a in range(3):
            sums += jnp.dot(taps[pl.ds(a * BS, BS * BS), :], weights[a], preferred_element_type=F32)
        out_stage[slot] = sums.astype(BF16).reshape(BS, BS, C)
        grid = lax.dot_general(
            wide_cot[...], jnp.concatenate(weights, axis=1), (((1,), (1,)), ((), ())),
            preferred_element_type=F32,
        )
        shift[0, :, pl.ds(8, BS), :] = grid[:, :C].reshape(ROWS, BS, C)
        shift[1, :, pl.ds(8, BS), :] = grid[:, 2 * C:].reshape(ROWS, BS, C)
        place = lax.broadcasted_iota(jnp.int32, (ROWS, BS, C), 1)
        main = grid[:, C:2 * C].reshape(ROWS, BS, C)
        main += jnp.where(place == BS - 1, 0.0, shift[0, :, pl.ds(9, BS), :])
        main += jnp.where(place == 0, 0.0, shift[1, :, pl.ds(7, BS), :])
        spread_stage[slot, pl.ds(0, ROWS)] = main.astype(BF16)
        sides[pl.ds(0, ROWS), :] = shift[0, :, 8, :]
        sides[pl.ds(SIDE, ROWS), :] = shift[1, :, BS + 7, :]
        spread_stage[slot, pl.ds(ROWS, 3)] = sides[...].astype(BF16).reshape(3, BS, C)

    own_cot.wait()
    own_patch.wait()

    @pl.loop(0, CAP * NLON)
    def _(step):
        r, k = step // NLON, lax.rem(step, NLON)
        source = source_lon(lon, k)

        @pl.when(k > 0)
        def _():
            cot_copy(k, r).wait_recv()
            patch_copy(k, r).wait_recv()

        convolve(2 * source + r, jnp.minimum(ids[source, 0, r], NLON - 1))

        @pl.when(k > 0)
        def _():
            spread_copy(k, r).start()

        @pl.when((k > 0) & (r == 0))
        def _():
            out_copy(k, r).start()

    @pl.loop(1, NLON)
    def _(k):
        out_copy(k, 1).start()

    own_out.start()
    own_spread.start()

    @pl.loop(0, NLON * CAP)
    def _(j):
        slot = order[j]
        previous = order[jnp.maximum(j - 1, 0)]
        now = ids[slot >> 1, 0, slot & 1]
        same = (j > 0) & (ids[previous >> 1, 0, previous & 1] == now)
        build_taps(slot)
        cots = got_cot[slot].reshape(BS * BS, C)
        for a in range(3):
            term = lax.dot_general(
                taps[pl.ds(a * BS, BS * BS), :], cots, (((0,), (0,)), ((), ())),
                preferred_element_type=F32,
            ).reshape(3, C, C)
            sums = jnp.where(same, total[pl.ds(3 * a, 3)], 0.0) + term
            total[pl.ds(3 * a, 3)] = sums
            running[j, pl.ds(3 * a, 3)] = sums.astype(BF16)

    def gradient(e):
        at = final[e]
        return jnp.where(at < 0, 0.0, running[jnp.maximum(at, 0)].astype(F32))

    @pl.loop(0, NLAT)
    def _(i):
        e = 4 * (i // 2) + 2 * (1 - core) + lax.rem(i, 2)
        pair_stage[i] = gradient(e).astype(BF16)

    pair = remote(pair_stage, got_pair, pair_sem.at[0], pair_sem.at[1], (other, lon))
    pair.start()

    def chip_copy(j):
        to = lax.rem(chip + j, RING)
        return remote(
            chip_stage.at[to], got_chip.at[chip], chip_send.at[j], chip_recv.at[j], (2 * to + core, lon)
        )

    pair.wait()

    @pl.loop(1, RING)
    def _(j):
        to = lax.rem(chip + j, RING)
        for i in range(2):
            both = gradient(4 * to + 2 * core + i) + got_pair[2 * to + i].astype(F32)
            chip_stage[to, i] = both.astype(BF16)
        chip_copy(j).start()

    for i in range(2):
        bank_out[i] = gradient(4 * chip + 2 * core + i) + got_pair[2 * chip + i].astype(F32)

    own_spread.wait()

    @pl.loop(1, NLON)
    def _(k):
        for r in range(CAP):
            spread_copy(k, r).wait_recv()

    @pl.loop(0, BLK)
    def _(b):
        bi, bj = b // BLON, lax.rem(b, BLON)
        base = bi * BS * EXT_COLS + (bj + 1) * BS
        block[...] = got_spread[block_slot[b]]

        for i in range(ROWS):
            at = pl.ds(pl.multiple_of(base + i * EXT_COLS, BS), BS)
            canvas[at, :] += block[i].astype(F32)
        both = block[pl.ds(ROWS, 3)].reshape(3 * BS, C).astype(F32)
        canvas[pl.ds(base - 1, ROWS, stride=EXT_COLS), :] += both[:ROWS]
        canvas[pl.ds(base + BS, ROWS, stride=EXT_COLS), :] += both[SIDE:SIDE + ROWS]

    side_stage[0] = canvas[column(outer_left), :]
    side_stage[1] = canvas[column(outer_right), :]
    grid = canvas.reshape(EXT_ROWS, EXT_COLS, C)
    half = BS // 2
    edge_low, edge_high = pl.ds(half, half), pl.ds(BS + WIDTH, half)
    edges = (
        (grid.at[0, mid_cols], row_in.at[0], (up, lon)),
        (grid.at[EXT_ROWS - 1, mid_cols], row_in.at[1], (down, lon)),
        (side_stage.at[0], col_in.at[0], (lat, left)),
        (side_stage.at[1], col_in.at[1], (lat, right)),
        (grid.at[0, edge_low], corner_in.at[0], (up, left)),
        (grid.at[0, edge_high], corner_in.at[1], (up, right)),
        (grid.at[EXT_ROWS - 1, edge_low], corner_in.at[2], (down, left)),
        (grid.at[EXT_ROWS - 1, edge_high], corner_in.at[3], (down, right)),
    )
    edge_copies = []
    for i, (source, target, device) in enumerate(edges):
        copy = remote(source, target, edge_send.at[i], edge_recv.at[i], device)
        copy.start()
        edge_copies.append(copy)

    @pl.loop(1, RING)
    def _(j):
        chip_copy(j).wait()
        back = lax.rem(chip + RING - j, RING)
        for i in range(2):
            bank_out[i] += got_chip[back, i].astype(F32)

    own_out.wait()

    @pl.loop(1, NLON)
    def _(k):
        for r in range(CAP):
            out_copy(k, r).wait_recv()

    @pl.loop(0, BLK)
    def _(b):
        bi, bj = b // BLON, lax.rem(b, BLON)
        outputs[
            pl.ds(pl.multiple_of(bi * BS, BS), BS), pl.ds(pl.multiple_of(bj * BS, BS), BS), :
        ] = got_out[block_slot[b]]

    def round_cells(i, col, count):
        start = pl.multiple_of((i + 1) * EXT_COLS + BS + col, BS)
        result[i, pl.ds(col, count)] = canvas[pl.ds(start, count), :].astype(BF16)

    @pl.loop(1, HEIGHT - 1)
    def _(i):
        round_cells(i, BS, WIDTH - 2 * BS)

    for copy in edge_copies:
        copy.wait()
    from_down = jnp.where(lat < NLAT - 1, 1.0, 0.0).astype(F32)
    from_up = jnp.where(lat > 0, 1.0, 0.0).astype(F32)
    upper, lower = EXT_COLS, HEIGHT * EXT_COLS
    canvas[pl.ds(lower + BS, WIDTH), :] += row_in[0] * from_down
    canvas[pl.ds(upper + BS, WIDTH), :] += row_in[1] * from_up

    canvas[column(inner_right), :] += col_in[0]
    canvas[column(inner_left), :] += col_in[1]
    canvas[pl.ds(lower + BS + WIDTH - half, half), :] += corner_in[0] * from_down
    canvas[pl.ds(lower + BS, half), :] += corner_in[1] * from_down
    canvas[pl.ds(upper + BS + WIDTH - half, half), :] += corner_in[2] * from_up
    canvas[pl.ds(upper + BS, half), :] += corner_in[3] * from_up

    for i in (0, HEIGHT - 1):
        round_cells(i, 0, WIDTH)

    @pl.loop(1, HEIGHT - 1)
    def _(i):
        round_cells(i, 0, BS)
        round_cells(i, WIDTH - BS, BS)

    @pl.loop(1, NLON)
    def _(k):
        for r in range(CAP):
            cot_copy(k, r).wait_send()
            patch_copy(k, r).wait_send()
            spread_copy(k, r).wait_send()
            out_copy(k, r).wait_send()


def write_kernel(a, b, c, a_out, b_out, c_out, sem):
    pairs = ((a, a_out), (b, b_out), (c, c_out))
    copies = [pltpu.make_async_copy(x, y, sem.at[i]) for i, (x, y) in enumerate(pairs)]
    for copy in copies:
        copy.start()
    for copy in copies:
        copy.wait()


def local(fields, cotangent, kernel_bank, block_expert, owner):
    hbm = pl.BlockSpec(memory_space=pltpu.HBM)
    smem = pl.BlockSpec(memory_space=pltpu.SMEM)
    vmem = pl.BlockSpec(memory_space=pltpu.VMEM)
    dma = pltpu.SemaphoreType.DMA
    slots = NLON * CAP
    results = pl.pallas_call(
        fused_kernel,
        out_shape=(
            jax.ShapeDtypeStruct((HEIGHT, WIDTH, C), BF16),
            jax.ShapeDtypeStruct((HEIGHT, WIDTH, C), BF16),
            jax.ShapeDtypeStruct((2, 9, C, C), F32),
        ),
        in_specs=[smem, smem, hbm, hbm, hbm],
        out_specs=(vmem, vmem, vmem),
        scratch_shapes=[
            pltpu.SMEM((BLK,), jnp.int32),
            pltpu.SMEM((BLK,), jnp.int32),
            pltpu.SMEM((slots,), jnp.int32),
            pltpu.SMEM((BLK,), jnp.int32),
            pltpu.SMEM((NLON, 1, C), jnp.int32),
            pltpu.SMEM((slots,), jnp.int32),
            pltpu.SMEM((slots,), jnp.int32),
            pltpu.SMEM((NLON,), jnp.int32),
            pltpu.VMEM((EXT_ROWS * EXT_COLS, C), F32),
            pltpu.VMEM((EXT_ROWS, EXT_COLS, C), BF16),
            pltpu.VMEM((2, HEIGHT, C), BF16),
            pltpu.VMEM((2, HEIGHT, C), BF16),
            pltpu.VMEM((2, HEIGHT, C), F32),
            pltpu.VMEM((3 * BS, C), F32),
            pltpu.VMEM((BLK, BS, BS, C), BF16),
            pltpu.VMEM((BLK, TILES, BS, C), BF16),
            pltpu.VMEM((NLON, CAP, BS, BS, C), BF16),
            pltpu.VMEM((NLON, CAP, TILES, BS, C), BF16),
            pltpu.VMEM((NLON, 1, C), jnp.int32),
            pltpu.VMEM((slots, BS, BS, C), BF16),
            pltpu.VMEM((slots, TILES, BS, C), BF16),
            pltpu.VMEM((NLON, 1, C), jnp.int32),
            pltpu.VMEM((NLON, 9, C, C), BF16),
            pltpu.VMEM((ROWS, 2 * BS, C), F32),
            pltpu.VMEM((ROWS * BS, 3 * C), BF16),
            pltpu.VMEM((ROWS * BS, 3 * C), BF16),
            pltpu.VMEM((2, ROWS, 2 * BS, C), F32),
            pltpu.VMEM((9, C, C), F32),
            pltpu.VMEM((slots, 9, C, C), BF16),
            pltpu.VMEM((slots, BS, BS, C), BF16),
            pltpu.VMEM((slots, TILES, BS, C), BF16),
            pltpu.VMEM((slots, BS, BS, C), BF16),
            pltpu.VMEM((slots, TILES, BS, C), BF16),
            pltpu.VMEM((TILES, BS, C), BF16),
            pltpu.VMEM((NLAT, 9, C, C), BF16),
            pltpu.VMEM((NLAT, 9, C, C), BF16),
            pltpu.VMEM((RING, 2, 9, C, C), BF16),
            pltpu.VMEM((RING, 2, 9, C, C), BF16),
            pltpu.VMEM((2, WIDTH, C), F32),
            pltpu.VMEM((2, HEIGHT, C), F32),
            pltpu.VMEM((4, BS // 2, C), F32),
            dma((3,)), dma((BLK,)),
            dma((8,)), dma((8,)),
            dma((RING,)), dma((RING,)),
            dma((RING,)), dma((RING,)),
            dma((CAP, NLON)), dma((CAP, NLON)),
            dma((CAP, NLON)), dma((CAP, NLON)),
            dma((NLON,)), dma((NLON,)),
            dma((CAP, NLON)), dma((CAP, NLON)),
            dma((CAP, NLON)), dma((CAP, NLON)),
            dma((2,)),
            dma((RING,)), dma((RING,)),
            dma((8,)), dma((8,)),
            dma((5,)),
        ],
        compiler_params=pltpu.CompilerParams(
            collective_id=0, has_side_effects=True, vmem_limit_bytes=62 << 20
        ),
    )(block_expert, owner, fields, cotangent, kernel_bank)
    return pl.pallas_call(
        write_kernel,
        out_shape=tuple(jax.ShapeDtypeStruct(x.shape, x.dtype) for x in results),
        in_specs=[vmem, vmem, vmem],
        out_specs=(hbm, hbm, hbm),
        scratch_shapes=[dma((3,))],
    )(*results)


def solution(mesh):
    return jax.shard_map(
        local,
        mesh=mesh,
        in_specs=(
            P("lat", "lon", None),
            P("lat", "lon", None),
            P(("lat", "lon"), None, None, None),
            P("lat", "lon"),
            P(),
        ),
        out_specs=(
            P("lat", "lon", None),
            P("lat", "lon", None),
            P(("lat", "lon"), None, None, None),
        ),
        check_vma=False,
    )
```

```python
import jax
import jax.numpy as jnp
from jax import lax
from jax.experimental import pallas as pl
from jax.experimental.pallas import tpu as pltpu
from jax.sharding import PartitionSpec as P

BS = 16
CAP = 2
C = 128
NLAT = 8
NLON = 16
RING = 4
BLK = 16
BLON = 8
HEIGHT = 32
WIDTH = 128
ROWS = BS + 2
SIDE = 24
TILES = ROWS + 3
EXT_ROWS = HEIGHT + 2
EXT_COLS = WIDTH + 2 * BS
PEERS = NLON - 1
MESH = pl.DeviceIdType.MESH
F32 = jnp.float32
BF16 = jnp.bfloat16


def turn(m):
    return lax.rem(m + 1, RING)


def torus_step(k):
    p = lax.rem(k + 1, NLON)
    i, j = p // RING, lax.rem(p, RING)
    return lax.rem(i + 2 * j, RING), j


def peer_lon(me, k):
    z, y = me // RING, lax.rem(me, RING)
    dz, dy = torus_step(k)
    return lax.rem(z + dz, RING) * RING + lax.rem(y + dy, RING)


def source_lon(me, k):
    z, y = me // RING, lax.rem(me, RING)
    dz, dy = torus_step(k)
    return lax.rem(z + RING - dz, RING) * RING + lax.rem(y + RING - dy, RING)


def greet(lat, lon, diagonal):
    barrier = pltpu.get_barrier_semaphore()

    def signal(device):
        pl.semaphore_signal(barrier, inc=1, device_id=device, device_id_type=MESH)

    @pl.loop(0, PEERS)
    def _(k):
        signal((lat, peer_lon(lon, k)))

    @pl.loop(1, NLAT)
    def _(k):
        signal((lax.rem(lat + k, NLAT), lon))

    for up, side in diagonal:
        signal((lax.rem(lat + up, NLAT), lax.rem(lon + side, NLON)))


def await_greetings(diagonal):
    pl.semaphore_wait(pltpu.get_barrier_semaphore(), NLON - 1 + NLAT - 1 + len(diagonal))


DIAGONAL = ((NLAT - 1, NLON - 1), (NLAT - 1, 1), (1, NLON - 1), (1, 1))


def index_tables(expert_ref, owner_ref, column, local, slot_block):
    for b in range(BLK):
        stored = owner_ref[expert_ref[b // BLON, b % BLON]]
        group = stored >> 1
        column[b] = group & (NLON - 1)
        local[b] = (group >> 4) * 2 + (stored & 1)

    @pl.loop(0, NLON)
    def _(c):
        first = jnp.int32(-1)
        second = jnp.int32(-1)
        for b in range(BLK):
            here = column[b] == c
            second = jnp.where(here & (first >= 0), b, second)
            first = jnp.where(here & (first < 0), b, first)
        slot_block[2 * c] = first
        slot_block[2 * c + 1] = second


def fused_kernel(
    expert_ref, owner_ref, fields, cot, bank,
    outputs_hbm, result_hbm, bank_hbm,
    outputs, result, bank_out, home, local, slot_block, block_slot, ids, rank, order, final, canvas, ext,
    col_stage, col_got, side_stage, sides, cot_in, patch_in, cot_stage, patch_stage, id_stage, got_cot, got_patch, got_id, kern,
    pad, taps, wide_cot, shift, total, running, out_stage, spread_stage, got_out, got_spread, block,
    pair_stage, got_pair, chip_stage, got_chip, row_in, col_in, corner_in,
    load_sem, cot_load, halo_send, halo_recv, bank_send, bank_recv, pass_send, pass_recv,
    cot_send, cot_recv, patch_send, patch_recv, id_send, id_recv,
    out_send, out_recv, spread_send, spread_recv, pair_sem, chip_send, chip_recv, edge_send, edge_recv,
    own_sem, write_sem,
):
    lat, lon = lax.axis_index("lat"), lax.axis_index("lon")
    core = lax.rem(lat, 2)
    chip = lat // 2
    other = lat + 1 - 2 * core

    def remote(source, target, send, recv, device):
        return pltpu.make_async_remote_copy(
            source, target, send, recv, device_id=device, device_id_type=MESH
        )

    greet(lat, lon, DIAGONAL)
    load_fields = pltpu.make_async_copy(
        fields, ext.at[pl.ds(1, HEIGHT), pl.ds(BS, WIDTH)], load_sem.at[0]
    )
    load_fields.start()
    load_bank = pltpu.make_async_copy(bank, kern.at[pl.ds(2 * lat, 2)], load_sem.at[1])
    load_bank.start()

    def load_cot(b):
        rows = pl.ds(pl.multiple_of((b // BLON) * BS, BS), BS)
        cols = pl.ds(pl.multiple_of(lax.rem(b, BLON) * BS, BS), BS)
        return pltpu.make_async_copy(cot.at[rows, cols], cot_in.at[b], cot_load.at[b])

    @pl.loop(0, BLK)
    def _(b):
        load_cot(b).start()

    index_tables(expert_ref, owner_ref, home, local, slot_block)
    for b in range(BLK):
        c = home[b]
        block_slot[b] = 2 * c + jnp.where(slot_block[2 * c + 1] == b, 1, 0)
    up, down = lax.rem(lat + NLAT - 1, NLAT), lax.rem(lat + 1, NLAT)
    left, right = lax.rem(lon + NLON - 1, NLON), lax.rem(lon + 1, NLON)
    top, bottom = pl.ds(0, 1), pl.ds(HEIGHT - 1, 1)
    first, last = pl.ds(0, BS), pl.ds(WIDTH - BS, BS)
    all_cols, mid_cols = pl.ds(0, WIDTH), pl.ds(BS, WIDTH)
    low, high = pl.ds(0, BS), pl.ds(BS + WIDTH, BS)
    zero, end = pl.ds(0, 1), pl.ds(EXT_ROWS - 1, 1)
    moves = (
        (top, all_cols, end, mid_cols, (up, lon)),
        (bottom, all_cols, zero, mid_cols, (down, lon)),
        (top, first, end, high, (up, left)),
        (top, last, end, low, (up, right)),
        (bottom, first, zero, high, (down, left)),
        (bottom, last, zero, low, (down, right)),
    )
    def bank_copy(j):
        return remote(
            bank, kern.at[pl.ds(2 * lat, 2)], bank_send.at[j], bank_recv.at[j],
            (lax.rem(lat + 2 * j, NLAT), lon),
        )

    def pass_copy(j):
        part = kern.at[pl.ds(2 * lax.rem(lat + NLAT - 2 * j, NLAT), 2)]
        return remote(part, part, pass_send.at[j], pass_recv.at[j], (other, lon))

    share_bank = remote(
        bank, kern.at[pl.ds(2 * lat, 2)], pass_send.at[0], pass_recv.at[0], (other, lon)
    )

    def cot_copy(k, r):
        dst = peer_lon(lon, k)
        return remote(
            cot_stage.at[dst, r], got_cot.at[2 * lon + r], cot_send.at[r, k], cot_recv.at[r, k], (lat, dst)
        )

    def patch_copy(k, r):
        dst = peer_lon(lon, k)
        return remote(
            patch_stage.at[dst, r], got_patch.at[2 * lon + r], patch_send.at[r, k], patch_recv.at[r, k],
            (lat, dst),
        )

    def id_copy(k):
        dst = peer_lon(lon, k)
        return remote(id_stage.at[dst], got_id.at[lon], id_send.at[k], id_recv.at[k], (lat, dst))

    def out_copy(k, r):
        dst = source_lon(lon, k)
        return remote(
            out_stage.at[2 * dst + r], got_out.at[2 * lon + r], out_send.at[r, k], out_recv.at[r, k], (lat, dst)
        )

    def spread_copy(k, r):
        dst = source_lon(lon, k)
        return remote(
            spread_stage.at[2 * dst + r], got_spread.at[2 * lon + r], spread_send.at[r, k],
            spread_recv.at[r, k], (lat, dst),
        )

    def own(source, target, i):
        return pltpu.make_async_copy(source, target, own_sem.at[i])

    own_slots = pl.ds(2 * lon, CAP)
    own_cot = own(cot_stage.at[lon], got_cot.at[own_slots], 0)
    own_patch = own(patch_stage.at[lon], got_patch.at[own_slots], 1)
    own_id = own(id_stage.at[lon], got_id.at[lon], 2)
    own_out = own(out_stage.at[own_slots], got_out.at[own_slots], 3)
    own_spread = own(spread_stage.at[own_slots], got_spread.at[own_slots], 4)

    def stage_cot(k, r):
        dst = peer_lon(lon, k)
        cot_stage[dst, r] = cot_in[jnp.maximum(slot_block[2 * dst + r], 0)]

    def column(where):
        return pl.ds(EXT_COLS + where, HEIGHT, stride=EXT_COLS)

    outer_left, inner_left, inner_right, outer_right = BS - 1, BS, BS + WIDTH - 1, BS + WIDTH
    load_fields.wait()

    def widen(r):
        canvas[pl.ds(pl.multiple_of(r * EXT_COLS, BS), EXT_COLS), :] = ext[r].astype(F32)

    @pl.loop(1, HEIGHT + 1)
    def _(r):
        widen(r)

    col_stage[0] = canvas[column(inner_left), :].astype(BF16)
    col_stage[1] = canvas[column(inner_right), :].astype(BF16)
    lane = lax.broadcasted_iota(jnp.int32, (1, C), 1)

    @pl.loop(0, NLON)
    def _(c):
        found = [slot_block[2 * c + r] for r in range(CAP)]
        named = [jnp.where(f < 0, NLON, local[jnp.maximum(f, 0)]) for f in found]
        id_stage[c] = jnp.where(lane == 0, named[0], named[1])

    @pl.loop(0, BLK)
    def _(b):
        load_cot(b).wait()

    @pl.loop(0, NLON)
    def _(k):
        for r in range(CAP):
            stage_cot(k, r)

    own_cot.start()
    own_id.start()
    await_greetings(DIAGONAL)

    @pl.loop(0, PEERS)
    def _(k):
        cot_copy(k, 0).start()

    halos = []
    for i, (rows, cols, to_rows, to_cols, device) in enumerate(moves):
        copy = remote(
            fields.at[rows, cols], ext.at[to_rows, to_cols], halo_send.at[i], halo_recv.at[i], device
        )
        copy.start()
        halos.append(copy)

    for i, device in enumerate(((lat, left), (lat, right))):
        copy = remote(col_stage.at[i], col_got.at[i], halo_send.at[6 + i], halo_recv.at[6 + i], device)
        copy.start()
        halos.append(copy)

    for j in range(1, RING):
        bank_copy(j).start()
    share_bank.start()

    @pl.loop(0, PEERS)
    def _(k):
        id_copy(k).start()
        cot_copy(k, 1).start()

    for copy in halos:
        copy.wait()

    @pl.when(lat == 0)
    def _():
        ext[0] = jnp.zeros((EXT_COLS, C), BF16)

    @pl.when(lat == NLAT - 1)
    def _():
        ext[EXT_ROWS - 1] = jnp.zeros((EXT_COLS, C), BF16)

    widen(0)
    widen(EXT_ROWS - 1)
    canvas[column(outer_right), :] = col_got[0].astype(F32)
    canvas[column(outer_left), :] = col_got[1].astype(F32)

    @pl.loop(0, BLK)
    def _(b):
        row = pl.multiple_of((b // BLON) * BS, BS)
        col = pl.multiple_of((lax.rem(b, BLON) + 1) * BS, BS)
        patch_in[b, pl.ds(0, ROWS)] = ext[pl.ds(row, ROWS), pl.ds(col, BS), :]
        start = row * EXT_COLS + col
        sides[pl.ds(0, ROWS), :] = canvas[pl.ds(start - 1, ROWS, stride=EXT_COLS), :]
        sides[pl.ds(SIDE, ROWS), :] = canvas[pl.ds(start + BS, ROWS, stride=EXT_COLS), :]
        patch_in[b, pl.ds(ROWS, 3)] = sides[...].astype(BF16).reshape(3, BS, C)

    def stage_patch(k, r):
        dst = peer_lon(lon, k)
        patch_stage[dst, r] = patch_in[jnp.maximum(slot_block[2 * dst + r], 0)]

    @pl.loop(0, PEERS)
    def _(k):
        stage_patch(k, 0)
        patch_copy(k, 0).start()

    @pl.loop(0, PEERS)
    def _(k):
        stage_patch(k, 1)
        patch_copy(k, 1).start()

    for r in range(CAP):
        stage_patch(PEERS, r)
    own_patch.start()

    load_bank.wait()
    for j in range(1, RING):
        bank_copy(j).wait()
        pass_copy(j).start()

    own_id.wait()

    @pl.loop(0, PEERS)
    def _(k):
        id_copy(k).wait()

    read_ids = pltpu.make_async_copy(got_id, ids, load_sem.at[2])
    read_ids.start()
    read_ids.wait()
    canvas[...] = jnp.zeros_like(canvas)
    wide_cot[...] = jnp.zeros_like(wide_cot)

    @pl.loop(0, NLON)
    def _(c):
        for r in range(CAP):
            mine = ids[c, 0, r]
            here = 2 * c + r
            before = jnp.int32(0)
            for s in range(NLON * CAP):
                it = ids[s // CAP, 0, s % CAP]
                before += jnp.where((it < mine) | ((it == mine) & (s < here)), 1, 0)
            rank[here] = before

    @pl.loop(0, NLON * CAP)
    def _(j):
        slot = jnp.int32(0)
        for s in range(NLON * CAP):
            slot = jnp.where(rank[s] == j, s, slot)
        order[j] = slot

    @pl.loop(0, NLON)
    def _(e):
        upto = jnp.int32(0)
        some = jnp.int32(0)
        for s in range(NLON * CAP):
            it = ids[s // CAP, 0, s % CAP]
            upto += jnp.where(it <= e, 1, 0)
            some += jnp.where(it == e, 1, 0)
        final[e] = jnp.where(some > 0, upto - 1, -1)

    share_bank.wait()
    for j in range(1, RING):
        pass_copy(j).wait()

    def build_taps(slot):
        pad[:, pl.ds(8, BS), :] = got_patch[slot, pl.ds(0, ROWS)].astype(F32)
        both = got_patch[slot, pl.ds(ROWS, 3)].reshape(3 * BS, C).astype(F32)
        pad[:, 7, :] = both[:ROWS]
        pad[:, BS + 8, :] = both[SIDE:SIDE + ROWS]
        for b in range(3):
            taps[:, pl.ds(b * C, C)] = pad[:, pl.ds(7 + b, BS), :].reshape(ROWS * BS, C).astype(BF16)

    def convolve(slot, e):
        build_taps(slot)
        cots = got_cot[slot].reshape(BS * BS, C)
        for a in range(3):
            wide_cot[pl.ds(a * BS, BS * BS), pl.ds(a * C, C)] = cots
        weights = [kern[e, pl.ds(3 * a, 3)].reshape(3 * C, C) for a in range(3)]
        sums = jnp.zeros((BS * BS, C), F32)
        for a in range(3):
            sums += jnp.dot(taps[pl.ds(a * BS, BS * BS), :], weights[a], preferred_element_type=F32)
        out_stage[slot] = sums.astype(BF16).reshape(BS, BS, C)
        grid = lax.dot_general(
            wide_cot[...], jnp.concatenate(weights, axis=1), (((1,), (1,)), ((), ())),
            preferred_element_type=F32,
        )
        shift[0, :, pl.ds(8, BS), :] = grid[:, :C].reshape(ROWS, BS, C)
        shift[1, :, pl.ds(8, BS), :] = grid[:, 2 * C:].reshape(ROWS, BS, C)
        place = lax.broadcasted_iota(jnp.int32, (ROWS, BS, C), 1)
        main = grid[:, C:2 * C].reshape(ROWS, BS, C)
        main += jnp.where(place == BS - 1, 0.0, shift[0, :, pl.ds(9, BS), :])
        main += jnp.where(place == 0, 0.0, shift[1, :, pl.ds(7, BS), :])
        spread_stage[slot, pl.ds(0, ROWS)] = main.astype(BF16)
        sides[pl.ds(0, ROWS), :] = shift[0, :, 8, :]
        sides[pl.ds(SIDE, ROWS), :] = shift[1, :, BS + 7, :]
        spread_stage[slot, pl.ds(ROWS, 3)] = sides[...].astype(BF16).reshape(3, BS, C)

    own_cot.wait()
    own_patch.wait()

    @pl.loop(0, CAP * NLON)
    def _(step):
        r, k = step // NLON, lax.rem(step, NLON)
        source = source_lon(lon, k)

        @pl.when(k < PEERS)
        def _():
            cot_copy(k, r).wait_recv()
            patch_copy(k, r).wait_recv()

        convolve(2 * source + r, jnp.minimum(ids[source, 0, r], NLON - 1))

        @pl.when(k < PEERS)
        def _():
            spread_copy(k, r).start()

        @pl.when((k < PEERS) & (r == 0))
        def _():
            out_copy(k, r).start()

    @pl.loop(0, PEERS)
    def _(k):
        out_copy(k, 1).start()

    own_out.start()
    own_spread.start()

    @pl.loop(0, NLON * CAP)
    def _(j):
        slot = order[j]
        previous = order[jnp.maximum(j - 1, 0)]
        now = ids[slot >> 1, 0, slot & 1]
        same = (j > 0) & (ids[previous >> 1, 0, previous & 1] == now)
        build_taps(slot)
        cots = got_cot[slot].reshape(BS * BS, C)
        for a in range(3):
            term = lax.dot_general(
                taps[pl.ds(a * BS, BS * BS), :], cots, (((0,), (0,)), ((), ())),
                preferred_element_type=F32,
            ).reshape(3, C, C)
            sums = jnp.where(same, total[pl.ds(3 * a, 3)], 0.0) + term
            total[pl.ds(3 * a, 3)] = sums
            running[j, pl.ds(3 * a, 3)] = sums.astype(BF16)

    def gradient(e):
        at = final[e]
        return jnp.where(at < 0, 0.0, running[jnp.maximum(at, 0)].astype(F32))

    @pl.loop(0, NLAT)
    def _(i):
        e = 4 * (i // 2) + 2 * (1 - core) + lax.rem(i, 2)
        pair_stage[i] = gradient(e).astype(BF16)

    pair = remote(pair_stage, got_pair, pair_sem.at[0], pair_sem.at[1], (other, lon))
    pair.start()

    def chip_copy(j):
        to = lax.rem(chip + j, RING)
        return remote(
            chip_stage.at[to], got_chip.at[chip], chip_send.at[j], chip_recv.at[j], (2 * to + core, lon)
        )

    pair.wait()

    @pl.loop(1, RING)
    def _(j):
        to = lax.rem(chip + j, RING)
        for i in range(2):
            both = gradient(4 * to + 2 * core + i) + got_pair[2 * to + i].astype(F32)
            chip_stage[to, i] = both.astype(BF16)
        chip_copy(j).start()

    for i in range(2):
        bank_out[i] = gradient(4 * chip + 2 * core + i) + got_pair[2 * chip + i].astype(F32)

    own_spread.wait()

    @pl.loop(0, PEERS)
    def _(k):
        for r in range(CAP):
            spread_copy(k, r).wait_recv()

    @pl.loop(0, BLK)
    def _(b):
        bi, bj = b // BLON, lax.rem(b, BLON)
        base = bi * BS * EXT_COLS + (bj + 1) * BS
        block[...] = got_spread[block_slot[b]]

        for i in range(ROWS):
            at = pl.ds(pl.multiple_of(base + i * EXT_COLS, BS), BS)
            canvas[at, :] += block[i].astype(F32)
        both = block[pl.ds(ROWS, 3)].reshape(3 * BS, C).astype(F32)
        canvas[pl.ds(base - 1, ROWS, stride=EXT_COLS), :] += both[:ROWS]
        canvas[pl.ds(base + BS, ROWS, stride=EXT_COLS), :] += both[SIDE:SIDE + ROWS]

    side_stage[0] = canvas[column(outer_left), :]
    side_stage[1] = canvas[column(outer_right), :]
    grid = canvas.reshape(EXT_ROWS, EXT_COLS, C)
    half = BS // 2
    edge_low, edge_high = pl.ds(half, half), pl.ds(BS + WIDTH, half)
    edges = (
        (grid.at[0, mid_cols], row_in.at[0], (up, lon)),
        (grid.at[EXT_ROWS - 1, mid_cols], row_in.at[1], (down, lon)),
        (side_stage.at[0], col_in.at[0], (lat, left)),
        (side_stage.at[1], col_in.at[1], (lat, right)),
        (grid.at[0, edge_low], corner_in.at[0], (up, left)),
        (grid.at[0, edge_high], corner_in.at[1], (up, right)),
        (grid.at[EXT_ROWS - 1, edge_low], corner_in.at[2], (down, left)),
        (grid.at[EXT_ROWS - 1, edge_high], corner_in.at[3], (down, right)),
    )
    edge_copies = []
    for i, (source, target, device) in enumerate(edges):
        copy = remote(source, target, edge_send.at[i], edge_recv.at[i], device)
        copy.start()
        edge_copies.append(copy)

    @pl.loop(1, RING)
    def _(j):
        chip_copy(j).wait()
        back = lax.rem(chip + RING - j, RING)
        for i in range(2):
            bank_out[i] += got_chip[back, i].astype(F32)

    writes = [
        pltpu.make_async_copy(x, y, write_sem.at[i])
        for i, (x, y) in enumerate(((bank_out, bank_hbm), (outputs, outputs_hbm), (result, result_hbm)))
    ]
    writes[0].start()
    own_out.wait()

    @pl.loop(0, PEERS)
    def _(k):
        for r in range(CAP):
            out_copy(k, r).wait_recv()

    @pl.loop(0, BLK)
    def _(b):
        bi, bj = b // BLON, lax.rem(b, BLON)
        outputs[
            pl.ds(pl.multiple_of(bi * BS, BS), BS), pl.ds(pl.multiple_of(bj * BS, BS), BS), :
        ] = got_out[block_slot[b]]

    writes[1].start()

    def round_cells(i, col, count):
        start = pl.multiple_of((i + 1) * EXT_COLS + BS + col, BS)
        result[i, pl.ds(col, count)] = canvas[pl.ds(start, count), :].astype(BF16)

    @pl.loop(1, HEIGHT - 1)
    def _(i):
        round_cells(i, BS, WIDTH - 2 * BS)

    for copy in edge_copies:
        copy.wait()
    from_down = jnp.where(lat < NLAT - 1, 1.0, 0.0).astype(F32)
    from_up = jnp.where(lat > 0, 1.0, 0.0).astype(F32)
    upper, lower = EXT_COLS, HEIGHT * EXT_COLS
    canvas[pl.ds(lower + BS, WIDTH), :] += row_in[0] * from_down
    canvas[pl.ds(upper + BS, WIDTH), :] += row_in[1] * from_up

    canvas[column(inner_right), :] += col_in[0]
    canvas[column(inner_left), :] += col_in[1]
    canvas[pl.ds(lower + BS + WIDTH - half, half), :] += corner_in[0] * from_down
    canvas[pl.ds(lower + BS, half), :] += corner_in[1] * from_down
    canvas[pl.ds(upper + BS + WIDTH - half, half), :] += corner_in[2] * from_up
    canvas[pl.ds(upper + BS, half), :] += corner_in[3] * from_up

    for i in (0, HEIGHT - 1):
        round_cells(i, 0, WIDTH)

    @pl.loop(1, HEIGHT - 1)
    def _(i):
        round_cells(i, 0, BS)
        round_cells(i, WIDTH - BS, BS)

    writes[2].start()

    @pl.loop(0, PEERS)
    def _(k):
        for r in range(CAP):
            cot_copy(k, r).wait_send()
            patch_copy(k, r).wait_send()
            spread_copy(k, r).wait_send()
            out_copy(k, r).wait_send()

    for copy in writes:
        copy.wait()


def write_kernel(a, b, c, a_out, b_out, c_out, sem):
    quarter = HEIGHT // 4
    copies = []
    for source, target in ((a, a_out), (b, b_out)):
        for i in range(4):
            part = pl.ds(i * quarter, quarter)
            copies.append((source.at[part], target.at[part]))
    for i in range(2):
        for part in (pl.ds(0, 5), pl.ds(5, 4)):
            copies.append((c.at[i, part], c_out.at[i, part]))
    copies = [pltpu.make_async_copy(x, y, sem.at[i]) for i, (x, y) in enumerate(copies)]
    for copy in copies:
        copy.start()
    for copy in copies:
        copy.wait()


def local(fields, cotangent, kernel_bank, block_expert, owner):
    hbm = pl.BlockSpec(memory_space=pltpu.HBM)
    smem = pl.BlockSpec(memory_space=pltpu.SMEM)
    vmem = pl.BlockSpec(memory_space=pltpu.VMEM)
    dma = pltpu.SemaphoreType.DMA
    slots = NLON * CAP
    results = pl.pallas_call(
        fused_kernel,
        out_shape=(
            jax.ShapeDtypeStruct((HEIGHT, WIDTH, C), BF16),
            jax.ShapeDtypeStruct((HEIGHT, WIDTH, C), BF16),
            jax.ShapeDtypeStruct((2, 9, C, C), F32),
        ),
        in_specs=[smem, smem, hbm, hbm, hbm],
        out_specs=(hbm, hbm, hbm),
        scratch_shapes=[
            pltpu.VMEM((HEIGHT, WIDTH, C), BF16),
            pltpu.VMEM((HEIGHT, WIDTH, C), BF16),
            pltpu.VMEM((2, 9, C, C), F32),
            pltpu.SMEM((BLK,), jnp.int32),
            pltpu.SMEM((BLK,), jnp.int32),
            pltpu.SMEM((slots,), jnp.int32),
            pltpu.SMEM((BLK,), jnp.int32),
            pltpu.SMEM((NLON, 1, C), jnp.int32),
            pltpu.SMEM((slots,), jnp.int32),
            pltpu.SMEM((slots,), jnp.int32),
            pltpu.SMEM((NLON,), jnp.int32),
            pltpu.VMEM((EXT_ROWS * EXT_COLS, C), F32),
            pltpu.VMEM((EXT_ROWS, EXT_COLS, C), BF16),
            pltpu.VMEM((2, HEIGHT, C), BF16),
            pltpu.VMEM((2, HEIGHT, C), BF16),
            pltpu.VMEM((2, HEIGHT, C), F32),
            pltpu.VMEM((3 * BS, C), F32),
            pltpu.VMEM((BLK, BS, BS, C), BF16),
            pltpu.VMEM((BLK, TILES, BS, C), BF16),
            pltpu.VMEM((NLON, CAP, BS, BS, C), BF16),
            pltpu.VMEM((NLON, CAP, TILES, BS, C), BF16),
            pltpu.VMEM((NLON, 1, C), jnp.int32),
            pltpu.VMEM((slots, BS, BS, C), BF16),
            pltpu.VMEM((slots, TILES, BS, C), BF16),
            pltpu.VMEM((NLON, 1, C), jnp.int32),
            pltpu.VMEM((NLON, 9, C, C), BF16),
            pltpu.VMEM((ROWS, 2 * BS, C), F32),
            pltpu.VMEM((ROWS * BS, 3 * C), BF16),
            pltpu.VMEM((ROWS * BS, 3 * C), BF16),
            pltpu.VMEM((2, ROWS, 2 * BS, C), F32),
            pltpu.VMEM((9, C, C), F32),
            pltpu.VMEM((slots, 9, C, C), BF16),
            pltpu.VMEM((slots, BS, BS, C), BF16),
            pltpu.VMEM((slots, TILES, BS, C), BF16),
            pltpu.VMEM((slots, BS, BS, C), BF16),
            pltpu.VMEM((slots, TILES, BS, C), BF16),
            pltpu.VMEM((TILES, BS, C), BF16),
            pltpu.VMEM((NLAT, 9, C, C), BF16),
            pltpu.VMEM((NLAT, 9, C, C), BF16),
            pltpu.VMEM((RING, 2, 9, C, C), BF16),
            pltpu.VMEM((RING, 2, 9, C, C), BF16),
            pltpu.VMEM((2, WIDTH, C), F32),
            pltpu.VMEM((2, HEIGHT, C), F32),
            pltpu.VMEM((4, BS // 2, C), F32),
            dma((3,)), dma((BLK,)),
            dma((8,)), dma((8,)),
            dma((RING,)), dma((RING,)),
            dma((RING,)), dma((RING,)),
            dma((CAP, NLON)), dma((CAP, NLON)),
            dma((CAP, NLON)), dma((CAP, NLON)),
            dma((NLON,)), dma((NLON,)),
            dma((CAP, NLON)), dma((CAP, NLON)),
            dma((CAP, NLON)), dma((CAP, NLON)),
            dma((2,)),
            dma((RING,)), dma((RING,)),
            dma((8,)), dma((8,)),
            dma((5,)), dma((3,)),
        ],
        compiler_params=pltpu.CompilerParams(
            collective_id=0, has_side_effects=True, vmem_limit_bytes=62 << 20
        ),
    )(block_expert, owner, fields, cotangent, kernel_bank)
    return pl.pallas_call(
        write_kernel,
        out_shape=tuple(jax.ShapeDtypeStruct(x.shape, x.dtype) for x in results),
        in_specs=[vmem, vmem, vmem],
        out_specs=(hbm, hbm, hbm),
        scratch_shapes=[dma((12,))],
    )(*results)


def solution(mesh):
    return jax.shard_map(
        local,
        mesh=mesh,
        in_specs=(
            P("lat", "lon", None),
            P("lat", "lon", None),
            P(("lat", "lon"), None, None, None),
            P("lat", "lon"),
            P(),
        ),
        out_specs=(
            P("lat", "lon", None),
            P("lat", "lon", None),
            P(("lat", "lon"), None, None, None),
        ),
        check_vma=False,
    )
```

```python
import jax
import jax.numpy as jnp
from jax import lax
from jax.experimental import pallas as pl
from jax.experimental.pallas import tpu as pltpu
from jax.sharding import PartitionSpec as P

BS = 16
CAP = 2
C = 128
NLAT = 8
NLON = 16
RING = 4
BLK = 16
BLON = 8
HEIGHT = 32
WIDTH = 128
ROWS = BS + 2
SIDE = ROWS
CELLS = ROWS * BS
PIECE = CELLS + 40
EXT_ROWS = HEIGHT + 2
EXT_COLS = WIDTH + 2 * BS
PEERS = NLON - 1
MESH = pl.DeviceIdType.MESH
F32 = jnp.float32
BF16 = jnp.bfloat16


def turn(m):
    return lax.rem(m + 1, RING)


def torus_step(k):
    p = lax.rem(k + 1, NLON)
    i, j = p // RING, lax.rem(p, RING)
    return lax.rem(i + 2 * j, RING), j


def peer_lon(me, k):
    z, y = me // RING, lax.rem(me, RING)
    dz, dy = torus_step(k)
    return lax.rem(z + dz, RING) * RING + lax.rem(y + dy, RING)


def source_lon(me, k):
    z, y = me // RING, lax.rem(me, RING)
    dz, dy = torus_step(k)
    return lax.rem(z + RING - dz, RING) * RING + lax.rem(y + RING - dy, RING)


def greet(lat, lon, diagonal):
    barrier = pltpu.get_barrier_semaphore()

    def signal(device):
        pl.semaphore_signal(barrier, inc=1, device_id=device, device_id_type=MESH)

    @pl.loop(0, PEERS)
    def _(k):
        signal((lat, peer_lon(lon, k)))

    @pl.loop(1, NLAT)
    def _(k):
        signal((lax.rem(lat + k, NLAT), lon))

    for up, side in diagonal:
        signal((lax.rem(lat + up, NLAT), lax.rem(lon + side, NLON)))


def await_greetings(diagonal):
    pl.semaphore_wait(pltpu.get_barrier_semaphore(), NLON - 1 + NLAT - 1 + len(diagonal))


DIAGONAL = ((NLAT - 1, NLON - 1), (NLAT - 1, 1), (1, NLON - 1), (1, 1))


def index_tables(expert_ref, owner_ref, column, local, slot_block):
    for b in range(BLK):
        stored = owner_ref[expert_ref[b // BLON, b % BLON]]
        group = stored >> 1
        column[b] = group & (NLON - 1)
        local[b] = (group >> 4) * 2 + (stored & 1)

    @pl.loop(0, NLON)
    def _(c):
        first = jnp.int32(-1)
        second = jnp.int32(-1)
        for b in range(BLK):
            here = column[b] == c
            second = jnp.where(here & (first >= 0), b, second)
            first = jnp.where(here & (first < 0), b, first)
        slot_block[2 * c] = first
        slot_block[2 * c + 1] = second


def fused_kernel(
    expert_ref, owner_ref, fields, cot, bank,
    outputs_hbm, result_hbm, bank_hbm,
    outputs, result, bank_out, home, local, slot_block, block_slot, ids, rank, order, final, canvas, ext,
    col_stage, col_got, side_stage, sides, cot_in, patch_in, cot_stage, patch_stage, id_stage, got_cot, got_patch, got_id, kern,
    pad, taps, wide_cot, shift, total, running, out_stage, spread_stage, got_out, got_spread, block,
    pair_stage, got_pair, chip_stage, got_chip, row_in, col_in, corner_in,
    load_sem, cot_load, halo_send, halo_recv, bank_send, bank_recv, pass_send, pass_recv,
    cot_send, cot_recv, patch_send, patch_recv, id_send, id_recv,
    out_send, out_recv, spread_send, spread_recv, pair_sem, chip_send, chip_recv, edge_send, edge_recv,
    own_sem, write_sem,
):
    lat, lon = lax.axis_index("lat"), lax.axis_index("lon")
    core = lax.rem(lat, 2)
    chip = lat // 2
    other = lat + 1 - 2 * core

    def remote(source, target, send, recv, device):
        return pltpu.make_async_remote_copy(
            source, target, send, recv, device_id=device, device_id_type=MESH
        )

    greet(lat, lon, DIAGONAL)
    load_fields = pltpu.make_async_copy(
        fields, ext.at[pl.ds(1, HEIGHT), pl.ds(BS, WIDTH)], load_sem.at[0]
    )
    load_fields.start()
    load_bank = pltpu.make_async_copy(bank, kern.at[pl.ds(2 * lat, 2)], load_sem.at[1])
    load_bank.start()

    def step_of(t):
        return t + core * (PEERS - 1 - 2 * t)

    def load_cot(b):
        rows = pl.ds(pl.multiple_of((b // BLON) * BS, BS), BS)
        cols = pl.ds(pl.multiple_of(lax.rem(b, BLON) * BS, BS), BS)
        return pltpu.make_async_copy(cot.at[rows, cols], cot_in.at[b], cot_load.at[b])

    @pl.loop(0, BLK)
    def _(b):
        load_cot(b).start()

    index_tables(expert_ref, owner_ref, home, local, slot_block)
    for b in range(BLK):
        c = home[b]
        block_slot[b] = 2 * c + jnp.where(slot_block[2 * c + 1] == b, 1, 0)
    up, down = lax.rem(lat + NLAT - 1, NLAT), lax.rem(lat + 1, NLAT)
    left, right = lax.rem(lon + NLON - 1, NLON), lax.rem(lon + 1, NLON)
    top, bottom = pl.ds(0, 1), pl.ds(HEIGHT - 1, 1)
    first, last = pl.ds(0, BS), pl.ds(WIDTH - BS, BS)
    all_cols, mid_cols = pl.ds(0, WIDTH), pl.ds(BS, WIDTH)
    low, high = pl.ds(0, BS), pl.ds(BS + WIDTH, BS)
    zero, end = pl.ds(0, 1), pl.ds(EXT_ROWS - 1, 1)
    moves = (
        (top, all_cols, end, mid_cols, (up, lon)),
        (bottom, all_cols, zero, mid_cols, (down, lon)),
        (top, first, end, high, (up, left)),
        (top, last, end, low, (up, right)),
        (bottom, first, zero, high, (down, left)),
        (bottom, last, zero, low, (down, right)),
    )
    def bank_copy(j):
        return remote(
            bank, kern.at[pl.ds(2 * lat, 2)], bank_send.at[j], bank_recv.at[j],
            (lax.rem(lat + 2 * j, NLAT), lon),
        )

    def pass_copy(j):
        part = kern.at[pl.ds(2 * lax.rem(lat + NLAT - 2 * j, NLAT), 2)]
        return remote(part, part, pass_send.at[j], pass_recv.at[j], (other, lon))

    share_bank = remote(
        bank, kern.at[pl.ds(2 * lat, 2)], pass_send.at[0], pass_recv.at[0], (other, lon)
    )

    def cot_copy(k, r):
        dst = peer_lon(lon, k)
        return remote(
            cot_stage.at[dst, r], got_cot.at[2 * lon + r], cot_send.at[r, k], cot_recv.at[r, k], (lat, dst)
        )

    def patch_copy(k, r):
        dst = peer_lon(lon, k)
        return remote(
            patch_stage.at[dst, r], got_patch.at[2 * lon + r], patch_send.at[r, k], patch_recv.at[r, k],
            (lat, dst),
        )

    def id_copy(k):
        dst = peer_lon(lon, k)
        return remote(id_stage.at[dst], got_id.at[lon], id_send.at[k], id_recv.at[k], (lat, dst))

    def out_copy(k, r):
        dst = source_lon(lon, k)
        return remote(
            out_stage.at[2 * dst + r], got_out.at[2 * lon + r], out_send.at[r, k], out_recv.at[r, k], (lat, dst)
        )

    def spread_copy(k, r):
        dst = source_lon(lon, k)
        return remote(
            spread_stage.at[2 * dst + r], got_spread.at[2 * lon + r], spread_send.at[r, k],
            spread_recv.at[r, k], (lat, dst),
        )

    def own(source, target, i):
        return pltpu.make_async_copy(source, target, own_sem.at[i])

    own_slots = pl.ds(2 * lon, CAP)
    own_cot = own(cot_stage.at[lon], got_cot.at[own_slots], 0)
    own_patch = own(patch_stage.at[lon], got_patch.at[own_slots], 1)
    own_id = own(id_stage.at[lon], got_id.at[lon], 2)
    own_out = own(out_stage.at[own_slots], got_out.at[own_slots], 3)
    own_spread = own(spread_stage.at[own_slots], got_spread.at[own_slots], 4)

    def stage_cot(k, r):
        dst = peer_lon(lon, k)
        cot_stage[dst, r] = cot_in[jnp.maximum(slot_block[2 * dst + r], 0)]

    def column(where):
        return pl.ds(EXT_COLS + where, HEIGHT, stride=EXT_COLS)

    outer_left, inner_left, inner_right, outer_right = BS - 1, BS, BS + WIDTH - 1, BS + WIDTH
    load_fields.wait()

    def widen(r):
        canvas[pl.ds(pl.multiple_of(r * EXT_COLS, BS), EXT_COLS), :] = ext[r].astype(F32)

    @pl.loop(1, HEIGHT + 1)
    def _(r):
        widen(r)

    col_stage[0] = canvas[column(inner_left), :].astype(BF16)
    col_stage[1] = canvas[column(inner_right), :].astype(BF16)
    lane = lax.broadcasted_iota(jnp.int32, (1, C), 1)

    @pl.loop(0, NLON)
    def _(c):
        found = [slot_block[2 * c + r] for r in range(CAP)]
        named = [jnp.where(f < 0, NLON, local[jnp.maximum(f, 0)]) for f in found]
        id_stage[c] = jnp.where(lane == 0, named[0], named[1])

    @pl.loop(0, BLK)
    def _(b):
        load_cot(b).wait()

    @pl.loop(0, NLON)
    def _(k):
        for r in range(CAP):
            stage_cot(k, r)

    own_cot.start()
    own_id.start()
    await_greetings(DIAGONAL)

    @pl.loop(0, PEERS)
    def _(t):
        k = step_of(t)
        cot_copy(k, 0).start()

    halos = []
    for i, (rows, cols, to_rows, to_cols, device) in enumerate(moves):
        copy = remote(
            fields.at[rows, cols], ext.at[to_rows, to_cols], halo_send.at[i], halo_recv.at[i], device
        )
        copy.start()
        halos.append(copy)

    for i, device in enumerate(((lat, left), (lat, right))):
        copy = remote(col_stage.at[i], col_got.at[i], halo_send.at[6 + i], halo_recv.at[6 + i], device)
        copy.start()
        halos.append(copy)

    for j in range(1, RING):
        bank_copy(j).start()
    share_bank.start()

    @pl.loop(0, PEERS)
    def _(t):
        k = step_of(t)
        id_copy(k).start()
        cot_copy(k, 1).start()

    for copy in halos:
        copy.wait()

    @pl.when(lat == 0)
    def _():
        ext[0] = jnp.zeros((EXT_COLS, C), BF16)

    @pl.when(lat == NLAT - 1)
    def _():
        ext[EXT_ROWS - 1] = jnp.zeros((EXT_COLS, C), BF16)

    widen(0)
    widen(EXT_ROWS - 1)
    canvas[column(outer_right), :] = col_got[0].astype(F32)
    canvas[column(outer_left), :] = col_got[1].astype(F32)

    @pl.loop(0, BLK)
    def _(b):
        row = pl.multiple_of((b // BLON) * BS, BS)
        col = pl.multiple_of((lax.rem(b, BLON) + 1) * BS, BS)
        patch_in[b, pl.ds(0, CELLS)] = ext[pl.ds(row, ROWS), pl.ds(col, BS), :].reshape(CELLS, C)
        start = row * EXT_COLS + col
        sides[pl.ds(0, ROWS), :] = canvas[pl.ds(start - 1, ROWS, stride=EXT_COLS), :]
        sides[pl.ds(SIDE, ROWS), :] = canvas[pl.ds(start + BS, ROWS, stride=EXT_COLS), :]
        patch_in[b, pl.ds(CELLS, 40)] = sides[...].astype(BF16)

    def stage_patch(k, r):
        dst = peer_lon(lon, k)
        patch_stage[dst, r] = patch_in[jnp.maximum(slot_block[2 * dst + r], 0)]

    @pl.loop(0, PEERS)
    def _(t):
        k = step_of(t)
        stage_patch(k, 0)
        patch_copy(k, 0).start()

    @pl.loop(0, PEERS)
    def _(t):
        k = step_of(t)
        stage_patch(k, 1)
        patch_copy(k, 1).start()

    for r in range(CAP):
        stage_patch(PEERS, r)
    own_patch.start()

    load_bank.wait()
    for j in range(1, RING):
        bank_copy(j).wait()
        pass_copy(j).start()

    own_id.wait()

    @pl.loop(0, PEERS)
    def _(k):
        id_copy(k).wait()

    read_ids = pltpu.make_async_copy(got_id, ids, load_sem.at[2])
    read_ids.start()
    read_ids.wait()
    canvas[...] = jnp.zeros_like(canvas)
    wide_cot[...] = jnp.zeros_like(wide_cot)

    @pl.loop(0, NLON)
    def _(c):
        for r in range(CAP):
            mine = ids[c, 0, r]
            here = 2 * c + r
            before = jnp.int32(0)
            for s in range(NLON * CAP):
                it = ids[s // CAP, 0, s % CAP]
                before += jnp.where((it < mine) | ((it == mine) & (s < here)), 1, 0)
            rank[here] = before

    @pl.loop(0, NLON * CAP)
    def _(j):
        slot = jnp.int32(0)
        for s in range(NLON * CAP):
            slot = jnp.where(rank[s] == j, s, slot)
        order[j] = slot

    @pl.loop(0, NLON)
    def _(e):
        upto = jnp.int32(0)
        some = jnp.int32(0)
        for s in range(NLON * CAP):
            it = ids[s // CAP, 0, s % CAP]
            upto += jnp.where(it <= e, 1, 0)
            some += jnp.where(it == e, 1, 0)
        final[e] = jnp.where(some > 0, upto - 1, -1)

    share_bank.wait()
    for j in range(1, RING):
        pass_copy(j).wait()

    def build_taps(slot):
        pad[:, pl.ds(8, BS), :] = got_patch[slot, pl.ds(0, CELLS)].reshape(ROWS, BS, C).astype(F32)
        sides[...] = got_patch[slot, pl.ds(CELLS, 40)].astype(F32)
        pad[:, 7, :] = sides[pl.ds(0, ROWS), :]
        pad[:, BS + 8, :] = sides[pl.ds(SIDE, ROWS), :]
        for b in range(3):
            taps[:, pl.ds(b * C, C)] = pad[:, pl.ds(7 + b, BS), :].reshape(ROWS * BS, C).astype(BF16)

    def convolve(slot, e):
        build_taps(slot)
        cots = got_cot[slot].reshape(BS * BS, C)
        for a in range(3):
            wide_cot[pl.ds(a * BS, BS * BS), pl.ds(a * C, C)] = cots
        weights = [kern[e, pl.ds(3 * a, 3)].reshape(3 * C, C) for a in range(3)]
        sums = jnp.zeros((BS * BS, C), F32)
        for a in range(3):
            sums += jnp.dot(taps[pl.ds(a * BS, BS * BS), :], weights[a], preferred_element_type=F32)
        out_stage[slot] = sums.astype(BF16).reshape(BS, BS, C)
        grid = lax.dot_general(
            wide_cot[...], jnp.concatenate(weights, axis=1), (((1,), (1,)), ((), ())),
            preferred_element_type=F32,
        )
        shift[0, :, pl.ds(8, BS), :] = grid[:, :C].reshape(ROWS, BS, C)
        shift[1, :, pl.ds(8, BS), :] = grid[:, 2 * C:].reshape(ROWS, BS, C)
        place = lax.broadcasted_iota(jnp.int32, (ROWS, BS, C), 1)
        main = grid[:, C:2 * C].reshape(ROWS, BS, C)
        main += jnp.where(place == BS - 1, 0.0, shift[0, :, pl.ds(9, BS), :])
        main += jnp.where(place == 0, 0.0, shift[1, :, pl.ds(7, BS), :])
        spread_stage[slot, pl.ds(0, CELLS)] = main.astype(BF16).reshape(CELLS, C)
        sides[pl.ds(0, ROWS), :] = shift[0, :, 8, :]
        sides[pl.ds(SIDE, ROWS), :] = shift[1, :, BS + 7, :]
        spread_stage[slot, pl.ds(CELLS, 40)] = sides[...].astype(BF16)

    own_cot.wait()
    own_patch.wait()

    @pl.loop(0, CAP * NLON)
    def _(step):
        r, t = step // NLON, lax.rem(step, NLON)
        k = jnp.where(t < PEERS, step_of(t), t)
        source = source_lon(lon, k)

        @pl.when(k < PEERS)
        def _():
            cot_copy(k, r).wait_recv()
            patch_copy(k, r).wait_recv()

        convolve(2 * source + r, jnp.minimum(ids[source, 0, r], NLON - 1))

        @pl.when(k < PEERS)
        def _():
            spread_copy(k, r).start()

        @pl.when((k < PEERS) & (r == 0))
        def _():
            out_copy(k, r).start()

    @pl.loop(0, PEERS)
    def _(t):
        k = step_of(t)
        out_copy(k, 1).start()

    own_out.start()
    own_spread.start()

    @pl.loop(0, NLON * CAP)
    def _(j):
        slot = order[j]
        previous = order[jnp.maximum(j - 1, 0)]
        now = ids[slot >> 1, 0, slot & 1]
        same = (j > 0) & (ids[previous >> 1, 0, previous & 1] == now)
        build_taps(slot)
        cots = got_cot[slot].reshape(BS * BS, C)
        for a in range(3):
            term = lax.dot_general(
                taps[pl.ds(a * BS, BS * BS), :], cots, (((0,), (0,)), ((), ())),
                preferred_element_type=F32,
            ).reshape(3, C, C)
            sums = jnp.where(same, total[pl.ds(3 * a, 3)], 0.0) + term
            total[pl.ds(3 * a, 3)] = sums
            running[j, pl.ds(3 * a, 3)] = sums.astype(BF16)

    def gradient(e):
        at = final[e]
        return jnp.where(at < 0, 0.0, running[jnp.maximum(at, 0)].astype(F32))

    @pl.loop(0, NLAT)
    def _(i):
        e = 4 * (i // 2) + 2 * (1 - core) + lax.rem(i, 2)
        pair_stage[i] = gradient(e).astype(BF16)

    pair = remote(pair_stage, got_pair, pair_sem.at[0], pair_sem.at[1], (other, lon))
    pair.start()

    def chip_copy(j):
        to = lax.rem(chip + j, RING)
        return remote(
            chip_stage.at[to], got_chip.at[chip], chip_send.at[j], chip_recv.at[j], (2 * to + core, lon)
        )

    pair.wait()

    @pl.loop(1, RING)
    def _(j):
        to = lax.rem(chip + j, RING)
        for i in range(2):
            both = gradient(4 * to + 2 * core + i) + got_pair[2 * to + i].astype(F32)
            chip_stage[to, i] = both.astype(BF16)
        chip_copy(j).start()

    for i in range(2):
        bank_out[i] = gradient(4 * chip + 2 * core + i) + got_pair[2 * chip + i].astype(F32)

    own_spread.wait()

    @pl.loop(0, PEERS)
    def _(k):
        for r in range(CAP):
            spread_copy(k, r).wait_recv()

    @pl.loop(0, BLK)
    def _(b):
        bi, bj = b // BLON, lax.rem(b, BLON)
        base = bi * BS * EXT_COLS + (bj + 1) * BS
        block[...] = got_spread[block_slot[b]]

        for i in range(ROWS):
            at = pl.ds(pl.multiple_of(base + i * EXT_COLS, BS), BS)
            canvas[at, :] += block[pl.ds(i * BS, BS)].astype(F32)
        sides[...] = block[pl.ds(CELLS, 40)].astype(F32)
        canvas[pl.ds(base - 1, ROWS, stride=EXT_COLS), :] += sides[pl.ds(0, ROWS), :]
        canvas[pl.ds(base + BS, ROWS, stride=EXT_COLS), :] += sides[pl.ds(SIDE, ROWS), :]

    side_stage[0] = canvas[column(outer_left), :]
    side_stage[1] = canvas[column(outer_right), :]
    grid = canvas.reshape(EXT_ROWS, EXT_COLS, C)
    half = BS // 2
    edge_low, edge_high = pl.ds(half, half), pl.ds(BS + WIDTH, half)
    edges = (
        (grid.at[0, mid_cols], row_in.at[0], (up, lon)),
        (grid.at[EXT_ROWS - 1, mid_cols], row_in.at[1], (down, lon)),
        (side_stage.at[0], col_in.at[0], (lat, left)),
        (side_stage.at[1], col_in.at[1], (lat, right)),
        (grid.at[0, edge_low], corner_in.at[0], (up, left)),
        (grid.at[0, edge_high], corner_in.at[1], (up, right)),
        (grid.at[EXT_ROWS - 1, edge_low], corner_in.at[2], (down, left)),
        (grid.at[EXT_ROWS - 1, edge_high], corner_in.at[3], (down, right)),
    )
    edge_copies = []
    for i, (source, target, device) in enumerate(edges):
        copy = remote(source, target, edge_send.at[i], edge_recv.at[i], device)
        copy.start()
        edge_copies.append(copy)

    @pl.loop(1, RING)
    def _(j):
        chip_copy(j).wait()
        back = lax.rem(chip + RING - j, RING)
        for i in range(2):
            bank_out[i] += got_chip[back, i].astype(F32)

    writes = [
        pltpu.make_async_copy(x, y, write_sem.at[i])
        for i, (x, y) in enumerate(((bank_out, bank_hbm), (outputs, outputs_hbm), (result, result_hbm)))
    ]
    writes[0].start()
    own_out.wait()

    @pl.loop(0, PEERS)
    def _(k):
        for r in range(CAP):
            out_copy(k, r).wait_recv()

    @pl.loop(0, BLK)
    def _(b):
        bi, bj = b // BLON, lax.rem(b, BLON)
        outputs[
            pl.ds(pl.multiple_of(bi * BS, BS), BS), pl.ds(pl.multiple_of(bj * BS, BS), BS), :
        ] = got_out[block_slot[b]]

    writes[1].start()

    def round_cells(i, col, count):
        start = pl.multiple_of((i + 1) * EXT_COLS + BS + col, BS)
        result[i, pl.ds(col, count)] = canvas[pl.ds(start, count), :].astype(BF16)

    @pl.loop(1, HEIGHT - 1)
    def _(i):
        round_cells(i, BS, WIDTH - 2 * BS)

    for copy in edge_copies:
        copy.wait()
    from_down = jnp.where(lat < NLAT - 1, 1.0, 0.0).astype(F32)
    from_up = jnp.where(lat > 0, 1.0, 0.0).astype(F32)
    upper, lower = EXT_COLS, HEIGHT * EXT_COLS
    canvas[pl.ds(lower + BS, WIDTH), :] += row_in[0] * from_down
    canvas[pl.ds(upper + BS, WIDTH), :] += row_in[1] * from_up

    canvas[column(inner_right), :] += col_in[0]
    canvas[column(inner_left), :] += col_in[1]
    canvas[pl.ds(lower + BS + WIDTH - half, half), :] += corner_in[0] * from_down
    canvas[pl.ds(lower + BS, half), :] += corner_in[1] * from_down
    canvas[pl.ds(upper + BS + WIDTH - half, half), :] += corner_in[2] * from_up
    canvas[pl.ds(upper + BS, half), :] += corner_in[3] * from_up

    for i in (0, HEIGHT - 1):
        round_cells(i, 0, WIDTH)

    @pl.loop(1, HEIGHT - 1)
    def _(i):
        round_cells(i, 0, BS)
        round_cells(i, WIDTH - BS, BS)

    writes[2].start()

    @pl.loop(0, PEERS)
    def _(k):
        for r in range(CAP):
            cot_copy(k, r).wait_send()
            patch_copy(k, r).wait_send()
            spread_copy(k, r).wait_send()
            out_copy(k, r).wait_send()

    for copy in writes:
        copy.wait()


def write_kernel(a, b, c, a_out, b_out, c_out, sem):
    quarter = HEIGHT // 4
    copies = []
    for source, target in ((a, a_out), (b, b_out)):
        for i in range(4):
            part = pl.ds(i * quarter, quarter)
            copies.append((source.at[part], target.at[part]))
    for i in range(2):
        for part in (pl.ds(0, 5), pl.ds(5, 4)):
            copies.append((c.at[i, part], c_out.at[i, part]))
    copies = [pltpu.make_async_copy(x, y, sem.at[i]) for i, (x, y) in enumerate(copies)]
    for copy in copies:
        copy.start()
    for copy in copies:
        copy.wait()


def local(fields, cotangent, kernel_bank, block_expert, owner):
    hbm = pl.BlockSpec(memory_space=pltpu.HBM)
    smem = pl.BlockSpec(memory_space=pltpu.SMEM)
    vmem = pl.BlockSpec(memory_space=pltpu.VMEM)
    dma = pltpu.SemaphoreType.DMA
    slots = NLON * CAP
    results = pl.pallas_call(
        fused_kernel,
        out_shape=(
            jax.ShapeDtypeStruct((HEIGHT, WIDTH, C), BF16),
            jax.ShapeDtypeStruct((HEIGHT, WIDTH, C), BF16),
            jax.ShapeDtypeStruct((2, 9, C, C), F32),
        ),
        in_specs=[smem, smem, hbm, hbm, hbm],
        out_specs=(hbm, hbm, hbm),
        scratch_shapes=[
            pltpu.VMEM((HEIGHT, WIDTH, C), BF16),
            pltpu.VMEM((HEIGHT, WIDTH, C), BF16),
            pltpu.VMEM((2, 9, C, C), F32),
            pltpu.SMEM((BLK,), jnp.int32),
            pltpu.SMEM((BLK,), jnp.int32),
            pltpu.SMEM((slots,), jnp.int32),
            pltpu.SMEM((BLK,), jnp.int32),
            pltpu.SMEM((NLON, 1, C), jnp.int32),
            pltpu.SMEM((slots,), jnp.int32),
            pltpu.SMEM((slots,), jnp.int32),
            pltpu.SMEM((NLON,), jnp.int32),
            pltpu.VMEM((EXT_ROWS * EXT_COLS, C), F32),
            pltpu.VMEM((EXT_ROWS, EXT_COLS, C), BF16),
            pltpu.VMEM((2, HEIGHT, C), BF16),
            pltpu.VMEM((2, HEIGHT, C), BF16),
            pltpu.VMEM((2, HEIGHT, C), F32),
            pltpu.VMEM((40, C), F32),
            pltpu.VMEM((BLK, BS, BS, C), BF16),
            pltpu.VMEM((BLK, PIECE, C), BF16),
            pltpu.VMEM((NLON, CAP, BS, BS, C), BF16),
            pltpu.VMEM((NLON, CAP, PIECE, C), BF16),
            pltpu.VMEM((NLON, 1, C), jnp.int32),
            pltpu.VMEM((slots, BS, BS, C), BF16),
            pltpu.VMEM((slots, PIECE, C), BF16),
            pltpu.VMEM((NLON, 1, C), jnp.int32),
            pltpu.VMEM((NLON, 9, C, C), BF16),
            pltpu.VMEM((ROWS, 2 * BS, C), F32),
            pltpu.VMEM((ROWS * BS, 3 * C), BF16),
            pltpu.VMEM((ROWS * BS, 3 * C), BF16),
            pltpu.VMEM((2, ROWS, 2 * BS, C), F32),
            pltpu.VMEM((9, C, C), F32),
            pltpu.VMEM((slots, 9, C, C), BF16),
            pltpu.VMEM((slots, BS, BS, C), BF16),
            pltpu.VMEM((slots, PIECE, C), BF16),
            pltpu.VMEM((slots, BS, BS, C), BF16),
            pltpu.VMEM((slots, PIECE, C), BF16),
            pltpu.VMEM((PIECE, C), BF16),
            pltpu.VMEM((NLAT, 9, C, C), BF16),
            pltpu.VMEM((NLAT, 9, C, C), BF16),
            pltpu.VMEM((RING, 2, 9, C, C), BF16),
            pltpu.VMEM((RING, 2, 9, C, C), BF16),
            pltpu.VMEM((2, WIDTH, C), F32),
            pltpu.VMEM((2, HEIGHT, C), F32),
            pltpu.VMEM((4, BS // 2, C), F32),
            dma((3,)), dma((BLK,)),
            dma((8,)), dma((8,)),
            dma((RING,)), dma((RING,)),
            dma((RING,)), dma((RING,)),
            dma((CAP, NLON)), dma((CAP, NLON)),
            dma((CAP, NLON)), dma((CAP, NLON)),
            dma((NLON,)), dma((NLON,)),
            dma((CAP, NLON)), dma((CAP, NLON)),
            dma((CAP, NLON)), dma((CAP, NLON)),
            dma((2,)),
            dma((RING,)), dma((RING,)),
            dma((8,)), dma((8,)),
            dma((5,)), dma((3,)),
        ],
        compiler_params=pltpu.CompilerParams(
            collective_id=0, has_side_effects=True, vmem_limit_bytes=62 << 20
        ),
    )(block_expert, owner, fields, cotangent, kernel_bank)
    return pl.pallas_call(
        write_kernel,
        out_shape=tuple(jax.ShapeDtypeStruct(x.shape, x.dtype) for x in results),
        in_specs=[vmem, vmem, vmem],
        out_specs=(hbm, hbm, hbm),
        scratch_shapes=[dma((12,))],
    )(*results)


def solution(mesh):
    return jax.shard_map(
        local,
        mesh=mesh,
        in_specs=(
            P("lat", "lon", None),
            P("lat", "lon", None),
            P(("lat", "lon"), None, None, None),
            P("lat", "lon"),
            P(),
        ),
        out_specs=(
            P("lat", "lon", None),
            P("lat", "lon", None),
            P(("lat", "lon"), None, None, None),
        ),
        check_vma=False,
    )
```

```python
import jax
import jax.numpy as jnp
from jax import lax
from jax.experimental import pallas as pl
from jax.experimental.pallas import tpu as pltpu
from jax.sharding import PartitionSpec as P

BS = 16
CAP = 2
C = 128
NLAT = 8
NLON = 16
RING = 4
BLK = 16
BLON = 8
HEIGHT = 32
WIDTH = 128
ROWS = BS + 2
SIDE = ROWS
CELLS = ROWS * BS
PIECE = CELLS + 40
EXT_ROWS = HEIGHT + 2
EXT_COLS = WIDTH + 2 * BS
PEERS = NLON - 1
MESH = pl.DeviceIdType.MESH
F32 = jnp.float32
BF16 = jnp.bfloat16


def turn(m):
    return lax.rem(m + 1, RING)


def torus_step(k):
    p = lax.rem(k + 1, NLON)
    i, j = p // RING, lax.rem(p, RING)
    a, b = lax.rem(i + 2 * j, RING), j
    swap = lax.rem(lax.axis_index("lat"), 2)
    return a + swap * (b - a), b + swap * (a - b)


def peer_lon(me, k):
    z, y = me // RING, lax.rem(me, RING)
    dz, dy = torus_step(k)
    return lax.rem(z + dz, RING) * RING + lax.rem(y + dy, RING)


def source_lon(me, k):
    z, y = me // RING, lax.rem(me, RING)
    dz, dy = torus_step(k)
    return lax.rem(z + RING - dz, RING) * RING + lax.rem(y + RING - dy, RING)


def greet(lat, lon, diagonal):
    barrier = pltpu.get_barrier_semaphore()

    def signal(device):
        pl.semaphore_signal(barrier, inc=1, device_id=device, device_id_type=MESH)

    @pl.loop(0, PEERS)
    def _(k):
        signal((lat, peer_lon(lon, k)))

    @pl.loop(1, NLAT)
    def _(k):
        signal((lax.rem(lat + k, NLAT), lon))

    for up, side in diagonal:
        signal((lax.rem(lat + up, NLAT), lax.rem(lon + side, NLON)))


def await_greetings(diagonal):
    pl.semaphore_wait(pltpu.get_barrier_semaphore(), NLON - 1 + NLAT - 1 + len(diagonal))


DIAGONAL = ((NLAT - 1, NLON - 1), (NLAT - 1, 1), (1, NLON - 1), (1, 1))


def index_tables(expert_ref, owner_ref, column, local, slot_block):
    for b in range(BLK):
        stored = owner_ref[expert_ref[b // BLON, b % BLON]]
        group = stored >> 1
        column[b] = group & (NLON - 1)
        local[b] = (group >> 4) * 2 + (stored & 1)

    @pl.loop(0, NLON)
    def _(c):
        first = jnp.int32(-1)
        second = jnp.int32(-1)
        for b in range(BLK):
            here = column[b] == c
            second = jnp.where(here & (first >= 0), b, second)
            first = jnp.where(here & (first < 0), b, first)
        slot_block[2 * c] = first
        slot_block[2 * c + 1] = second


def fused_kernel(
    expert_ref, owner_ref, fields, cot, bank,
    outputs_hbm, result_hbm, bank_hbm,
    outputs, result, bank_out, home, local, slot_block, block_slot, ids, rank, order, final, canvas, ext,
    col_stage, col_got, side_stage, sides, cot_in, patch_in, cot_stage, patch_stage, id_stage, got_cot, got_patch, got_id, kern,
    pad, taps, wide_cot, shift, total, running, out_stage, spread_stage, got_out, got_spread, block,
    pair_stage, got_pair, chip_stage, got_chip, row_in, col_in, corner_in,
    load_sem, cot_load, halo_send, halo_recv, bank_send, bank_recv, pass_send, pass_recv,
    cot_send, cot_recv, patch_send, patch_recv, id_send, id_recv,
    out_send, out_recv, spread_send, spread_recv, pair_sem, chip_send, chip_recv, edge_send, edge_recv,
    own_sem, write_sem,
):
    lat, lon = lax.axis_index("lat"), lax.axis_index("lon")
    core = lax.rem(lat, 2)
    chip = lat // 2
    other = lat + 1 - 2 * core

    def remote(source, target, send, recv, device):
        return pltpu.make_async_remote_copy(
            source, target, send, recv, device_id=device, device_id_type=MESH
        )

    greet(lat, lon, DIAGONAL)
    load_fields = pltpu.make_async_copy(
        fields, ext.at[pl.ds(1, HEIGHT), pl.ds(BS, WIDTH)], load_sem.at[0]
    )
    load_fields.start()
    load_bank = pltpu.make_async_copy(bank, kern.at[pl.ds(2 * lat, 2)], load_sem.at[1])
    load_bank.start()

    def load_cot(b):
        rows = pl.ds(pl.multiple_of((b // BLON) * BS, BS), BS)
        cols = pl.ds(pl.multiple_of(lax.rem(b, BLON) * BS, BS), BS)
        return pltpu.make_async_copy(cot.at[rows, cols], cot_in.at[b], cot_load.at[b])

    @pl.loop(0, BLK)
    def _(b):
        load_cot(b).start()

    index_tables(expert_ref, owner_ref, home, local, slot_block)
    for b in range(BLK):
        c = home[b]
        block_slot[b] = 2 * c + jnp.where(slot_block[2 * c + 1] == b, 1, 0)
    up, down = lax.rem(lat + NLAT - 1, NLAT), lax.rem(lat + 1, NLAT)
    left, right = lax.rem(lon + NLON - 1, NLON), lax.rem(lon + 1, NLON)
    top, bottom = pl.ds(0, 1), pl.ds(HEIGHT - 1, 1)
    first, last = pl.ds(0, BS), pl.ds(WIDTH - BS, BS)
    all_cols, mid_cols = pl.ds(0, WIDTH), pl.ds(BS, WIDTH)
    low, high = pl.ds(0, BS), pl.ds(BS + WIDTH, BS)
    zero, end = pl.ds(0, 1), pl.ds(EXT_ROWS - 1, 1)
    moves = (
        (top, all_cols, end, mid_cols, (up, lon)),
        (bottom, all_cols, zero, mid_cols, (down, lon)),
        (top, first, end, high, (up, left)),
        (top, last, end, low, (up, right)),
        (bottom, first, zero, high, (down, left)),
        (bottom, last, zero, low, (down, right)),
    )
    def bank_copy(j):
        return remote(
            bank, kern.at[pl.ds(2 * lat, 2)], bank_send.at[j], bank_recv.at[j],
            (lax.rem(lat + 2 * j, NLAT), lon),
        )

    def pass_copy(j):
        part = kern.at[pl.ds(2 * lax.rem(lat + NLAT - 2 * j, NLAT), 2)]
        return remote(part, part, pass_send.at[j], pass_recv.at[j], (other, lon))

    share_bank = remote(
        bank, kern.at[pl.ds(2 * lat, 2)], pass_send.at[0], pass_recv.at[0], (other, lon)
    )

    def cot_copy(k, r):
        dst = peer_lon(lon, k)
        return remote(
            cot_stage.at[dst, r], got_cot.at[2 * lon + r], cot_send.at[r, k], cot_recv.at[r, k], (lat, dst)
        )

    def patch_copy(k, r):
        dst = peer_lon(lon, k)
        return remote(
            patch_stage.at[dst, r], got_patch.at[2 * lon + r], patch_send.at[r, k], patch_recv.at[r, k],
            (lat, dst),
        )

    def id_copy(k):
        dst = peer_lon(lon, k)
        return remote(id_stage.at[dst], got_id.at[lon], id_send.at[k], id_recv.at[k], (lat, dst))

    def out_copy(k, r):
        dst = source_lon(lon, k)
        return remote(
            out_stage.at[2 * dst + r], got_out.at[2 * lon + r], out_send.at[r, k], out_recv.at[r, k], (lat, dst)
        )

    def spread_copy(k, r):
        dst = source_lon(lon, k)
        return remote(
            spread_stage.at[2 * dst + r], got_spread.at[2 * lon + r], spread_send.at[r, k],
            spread_recv.at[r, k], (lat, dst),
        )

    def own(source, target, i):
        return pltpu.make_async_copy(source, target, own_sem.at[i])

    own_slots = pl.ds(2 * lon, CAP)
    own_cot = own(cot_stage.at[lon], got_cot.at[own_slots], 0)
    own_patch = own(patch_stage.at[lon], got_patch.at[own_slots], 1)
    own_id = own(id_stage.at[lon], got_id.at[lon], 2)
    own_out = own(out_stage.at[own_slots], got_out.at[own_slots], 3)
    own_spread = own(spread_stage.at[own_slots], got_spread.at[own_slots], 4)

    def stage_cot(k, r):
        dst = peer_lon(lon, k)
        cot_stage[dst, r] = cot_in[jnp.maximum(slot_block[2 * dst + r], 0)]

    def column(where):
        return pl.ds(EXT_COLS + where, HEIGHT, stride=EXT_COLS)

    outer_left, inner_left, inner_right, outer_right = BS - 1, BS, BS + WIDTH - 1, BS + WIDTH
    load_fields.wait()

    def widen(r):
        canvas[pl.ds(pl.multiple_of(r * EXT_COLS, BS), EXT_COLS), :] = ext[r].astype(F32)

    @pl.loop(1, HEIGHT + 1)
    def _(r):
        widen(r)

    col_stage[0] = canvas[column(inner_left), :].astype(BF16)
    col_stage[1] = canvas[column(inner_right), :].astype(BF16)
    lane = lax.broadcasted_iota(jnp.int32, (1, C), 1)

    @pl.loop(0, NLON)
    def _(c):
        found = [slot_block[2 * c + r] for r in range(CAP)]
        named = [jnp.where(f < 0, NLON, local[jnp.maximum(f, 0)]) for f in found]
        id_stage[c] = jnp.where(lane == 0, named[0], named[1])

    @pl.loop(0, BLK)
    def _(b):
        load_cot(b).wait()

    @pl.loop(0, NLON)
    def _(k):
        for r in range(CAP):
            stage_cot(k, r)

    own_cot.start()
    own_id.start()
    await_greetings(DIAGONAL)

    @pl.loop(0, PEERS)
    def _(k):
        cot_copy(k, 0).start()

    halos = []
    for i, (rows, cols, to_rows, to_cols, device) in enumerate(moves):
        copy = remote(
            fields.at[rows, cols], ext.at[to_rows, to_cols], halo_send.at[i], halo_recv.at[i], device
        )
        copy.start()
        halos.append(copy)

    for i, device in enumerate(((lat, left), (lat, right))):
        copy = remote(col_stage.at[i], col_got.at[i], halo_send.at[6 + i], halo_recv.at[6 + i], device)
        copy.start()
        halos.append(copy)

    for j in range(1, RING):
        bank_copy(j).start()
    share_bank.start()

    @pl.loop(0, PEERS)
    def _(k):
        id_copy(k).start()
        cot_copy(k, 1).start()

    for copy in halos:
        copy.wait()

    @pl.when(lat == 0)
    def _():
        ext[0] = jnp.zeros((EXT_COLS, C), BF16)

    @pl.when(lat == NLAT - 1)
    def _():
        ext[EXT_ROWS - 1] = jnp.zeros((EXT_COLS, C), BF16)

    widen(0)
    widen(EXT_ROWS - 1)
    canvas[column(outer_right), :] = col_got[0].astype(F32)
    canvas[column(outer_left), :] = col_got[1].astype(F32)

    @pl.loop(0, BLK)
    def _(b):
        row = pl.multiple_of((b // BLON) * BS, BS)
        col = pl.multiple_of((lax.rem(b, BLON) + 1) * BS, BS)
        patch_in[b, pl.ds(0, CELLS)] = ext[pl.ds(row, ROWS), pl.ds(col, BS), :].reshape(CELLS, C)
        start = row * EXT_COLS + col
        sides[pl.ds(0, ROWS), :] = canvas[pl.ds(start - 1, ROWS, stride=EXT_COLS), :]
        sides[pl.ds(SIDE, ROWS), :] = canvas[pl.ds(start + BS, ROWS, stride=EXT_COLS), :]
        patch_in[b, pl.ds(CELLS, 40)] = sides[...].astype(BF16)

    def stage_patch(k, r):
        dst = peer_lon(lon, k)
        patch_stage[dst, r] = patch_in[jnp.maximum(slot_block[2 * dst + r], 0)]

    @pl.loop(0, PEERS)
    def _(k):
        stage_patch(k, 0)
        patch_copy(k, 0).start()

    @pl.loop(0, PEERS)
    def _(k):
        stage_patch(k, 1)
        patch_copy(k, 1).start()

    for r in range(CAP):
        stage_patch(PEERS, r)
    own_patch.start()

    load_bank.wait()
    for j in range(1, RING):
        bank_copy(j).wait()
        pass_copy(j).start()

    own_id.wait()

    @pl.loop(0, PEERS)
    def _(k):
        id_copy(k).wait()

    read_ids = pltpu.make_async_copy(got_id, ids, load_sem.at[2])
    read_ids.start()
    read_ids.wait()
    canvas[...] = jnp.zeros_like(canvas)
    wide_cot[...] = jnp.zeros_like(wide_cot)

    @pl.loop(0, NLON)
    def _(c):
        for r in range(CAP):
            mine = ids[c, 0, r]
            here = 2 * c + r
            before = jnp.int32(0)
            for s in range(NLON * CAP):
                it = ids[s // CAP, 0, s % CAP]
                before += jnp.where((it < mine) | ((it == mine) & (s < here)), 1, 0)
            rank[here] = before

    @pl.loop(0, NLON * CAP)
    def _(j):
        slot = jnp.int32(0)
        for s in range(NLON * CAP):
            slot = jnp.where(rank[s] == j, s, slot)
        order[j] = slot

    @pl.loop(0, NLON)
    def _(e):
        upto = jnp.int32(0)
        some = jnp.int32(0)
        for s in range(NLON * CAP):
            it = ids[s // CAP, 0, s % CAP]
            upto += jnp.where(it <= e, 1, 0)
            some += jnp.where(it == e, 1, 0)
        final[e] = jnp.where(some > 0, upto - 1, -1)

    share_bank.wait()
    for j in range(1, RING):
        pass_copy(j).wait()

    def build_taps(slot):
        pad[:, pl.ds(8, BS), :] = got_patch[slot, pl.ds(0, CELLS)].reshape(ROWS, BS, C).astype(F32)
        sides[...] = got_patch[slot, pl.ds(CELLS, 40)].astype(F32)
        pad[:, 7, :] = sides[pl.ds(0, ROWS), :]
        pad[:, BS + 8, :] = sides[pl.ds(SIDE, ROWS), :]
        for b in range(3):
            taps[:, pl.ds(b * C, C)] = pad[:, pl.ds(7 + b, BS), :].reshape(ROWS * BS, C).astype(BF16)

    def convolve(slot, e):
        build_taps(slot)
        cots = got_cot[slot].reshape(BS * BS, C)
        for a in range(3):
            wide_cot[pl.ds(a * BS, BS * BS), pl.ds(a * C, C)] = cots
        weights = [kern[e, pl.ds(3 * a, 3)].reshape(3 * C, C) for a in range(3)]
        sums = jnp.zeros((BS * BS, C), F32)
        for a in range(3):
            sums += jnp.dot(taps[pl.ds(a * BS, BS * BS), :], weights[a], preferred_element_type=F32)
        out_stage[slot] = sums.astype(BF16).reshape(BS, BS, C)
        grid = lax.dot_general(
            wide_cot[...], jnp.concatenate(weights, axis=1), (((1,), (1,)), ((), ())),
            preferred_element_type=F32,
        )
        shift[0, :, pl.ds(8, BS), :] = grid[:, :C].reshape(ROWS, BS, C)
        shift[1, :, pl.ds(8, BS), :] = grid[:, 2 * C:].reshape(ROWS, BS, C)
        place = lax.broadcasted_iota(jnp.int32, (ROWS, BS, C), 1)
        main = grid[:, C:2 * C].reshape(ROWS, BS, C)
        main += jnp.where(place == BS - 1, 0.0, shift[0, :, pl.ds(9, BS), :])
        main += jnp.where(place == 0, 0.0, shift[1, :, pl.ds(7, BS), :])
        spread_stage[slot, pl.ds(0, CELLS)] = main.astype(BF16).reshape(CELLS, C)
        sides[pl.ds(0, ROWS), :] = shift[0, :, 8, :]
        sides[pl.ds(SIDE, ROWS), :] = shift[1, :, BS + 7, :]
        spread_stage[slot, pl.ds(CELLS, 40)] = sides[...].astype(BF16)

    own_cot.wait()
    own_patch.wait()

    @pl.loop(0, CAP * NLON)
    def _(step):
        r, k = step // NLON, lax.rem(step, NLON)
        source = source_lon(lon, k)

        @pl.when(k < PEERS)
        def _():
            cot_copy(k, r).wait_recv()
            patch_copy(k, r).wait_recv()

        convolve(2 * source + r, jnp.minimum(ids[source, 0, r], NLON - 1))

        @pl.when(k < PEERS)
        def _():
            spread_copy(k, r).start()

        @pl.when((k < PEERS) & (r == 0))
        def _():
            out_copy(k, r).start()

    @pl.loop(0, PEERS)
    def _(k):
        out_copy(k, 1).start()

    own_out.start()
    own_spread.start()

    @pl.loop(0, NLON * CAP)
    def _(j):
        slot = order[j]
        previous = order[jnp.maximum(j - 1, 0)]
        now = ids[slot >> 1, 0, slot & 1]
        same = (j > 0) & (ids[previous >> 1, 0, previous & 1] == now)
        build_taps(slot)
        cots = got_cot[slot].reshape(BS * BS, C)
        for a in range(3):
            term = lax.dot_general(
                taps[pl.ds(a * BS, BS * BS), :], cots, (((0,), (0,)), ((), ())),
                preferred_element_type=F32,
            ).reshape(3, C, C)
            sums = jnp.where(same, total[pl.ds(3 * a, 3)], 0.0) + term
            total[pl.ds(3 * a, 3)] = sums
            running[j, pl.ds(3 * a, 3)] = sums.astype(BF16)

    def gradient(e):
        at = final[e]
        return jnp.where(at < 0, 0.0, running[jnp.maximum(at, 0)].astype(F32))

    @pl.loop(0, NLAT)
    def _(i):
        e = 4 * (i // 2) + 2 * (1 - core) + lax.rem(i, 2)
        pair_stage[i] = gradient(e).astype(BF16)

    pair = remote(pair_stage, got_pair, pair_sem.at[0], pair_sem.at[1], (other, lon))
    pair.start()

    def chip_copy(j):
        to = lax.rem(chip + j, RING)
        return remote(
            chip_stage.at[to], got_chip.at[chip], chip_send.at[j], chip_recv.at[j], (2 * to + core, lon)
        )

    pair.wait()

    @pl.loop(1, RING)
    def _(j):
        to = lax.rem(chip + j, RING)
        for i in range(2):
            both = gradient(4 * to + 2 * core + i) + got_pair[2 * to + i].astype(F32)
            chip_stage[to, i] = both.astype(BF16)
        chip_copy(j).start()

    for i in range(2):
        bank_out[i] = gradient(4 * chip + 2 * core + i) + got_pair[2 * chip + i].astype(F32)

    own_spread.wait()

    @pl.loop(0, PEERS)
    def _(k):
        for r in range(CAP):
            spread_copy(k, r).wait_recv()

    @pl.loop(0, BLK)
    def _(b):
        bi, bj = b // BLON, lax.rem(b, BLON)
        base = bi * BS * EXT_COLS + (bj + 1) * BS
        block[...] = got_spread[block_slot[b]]

        for i in range(ROWS):
            at = pl.ds(pl.multiple_of(base + i * EXT_COLS, BS), BS)
            canvas[at, :] += block[pl.ds(i * BS, BS)].astype(F32)
        sides[...] = block[pl.ds(CELLS, 40)].astype(F32)
        canvas[pl.ds(base - 1, ROWS, stride=EXT_COLS), :] += sides[pl.ds(0, ROWS), :]
        canvas[pl.ds(base + BS, ROWS, stride=EXT_COLS), :] += sides[pl.ds(SIDE, ROWS), :]

    side_stage[0] = canvas[column(outer_left), :]
    side_stage[1] = canvas[column(outer_right), :]
    grid = canvas.reshape(EXT_ROWS, EXT_COLS, C)
    half = BS // 2
    edge_low, edge_high = pl.ds(half, half), pl.ds(BS + WIDTH, half)
    edges = (
        (grid.at[0, mid_cols], row_in.at[0], (up, lon)),
        (grid.at[EXT_ROWS - 1, mid_cols], row_in.at[1], (down, lon)),
        (side_stage.at[0], col_in.at[0], (lat, left)),
        (side_stage.at[1], col_in.at[1], (lat, right)),
        (grid.at[0, edge_low], corner_in.at[0], (up, left)),
        (grid.at[0, edge_high], corner_in.at[1], (up, right)),
        (grid.at[EXT_ROWS - 1, edge_low], corner_in.at[2], (down, left)),
        (grid.at[EXT_ROWS - 1, edge_high], corner_in.at[3], (down, right)),
    )
    edge_copies = []
    for i, (source, target, device) in enumerate(edges):
        copy = remote(source, target, edge_send.at[i], edge_recv.at[i], device)
        copy.start()
        edge_copies.append(copy)

    @pl.loop(1, RING)
    def _(j):
        chip_copy(j).wait()
        back = lax.rem(chip + RING - j, RING)
        for i in range(2):
            bank_out[i] += got_chip[back, i].astype(F32)

    writes = [
        pltpu.make_async_copy(x, y, write_sem.at[i])
        for i, (x, y) in enumerate(((bank_out, bank_hbm), (outputs, outputs_hbm), (result, result_hbm)))
    ]
    writes[0].start()
    own_out.wait()

    @pl.loop(0, PEERS)
    def _(k):
        for r in range(CAP):
            out_copy(k, r).wait_recv()

    @pl.loop(0, BLK)
    def _(b):
        bi, bj = b // BLON, lax.rem(b, BLON)
        outputs[
            pl.ds(pl.multiple_of(bi * BS, BS), BS), pl.ds(pl.multiple_of(bj * BS, BS), BS), :
        ] = got_out[block_slot[b]]

    writes[1].start()

    def round_cells(i, col, count):
        start = pl.multiple_of((i + 1) * EXT_COLS + BS + col, BS)
        result[i, pl.ds(col, count)] = canvas[pl.ds(start, count), :].astype(BF16)

    @pl.loop(1, HEIGHT - 1)
    def _(i):
        round_cells(i, BS, WIDTH - 2 * BS)

    for copy in edge_copies:
        copy.wait()
    from_down = jnp.where(lat < NLAT - 1, 1.0, 0.0).astype(F32)
    from_up = jnp.where(lat > 0, 1.0, 0.0).astype(F32)
    upper, lower = EXT_COLS, HEIGHT * EXT_COLS
    canvas[pl.ds(lower + BS, WIDTH), :] += row_in[0] * from_down
    canvas[pl.ds(upper + BS, WIDTH), :] += row_in[1] * from_up

    canvas[column(inner_right), :] += col_in[0]
    canvas[column(inner_left), :] += col_in[1]
    canvas[pl.ds(lower + BS + WIDTH - half, half), :] += corner_in[0] * from_down
    canvas[pl.ds(lower + BS, half), :] += corner_in[1] * from_down
    canvas[pl.ds(upper + BS + WIDTH - half, half), :] += corner_in[2] * from_up
    canvas[pl.ds(upper + BS, half), :] += corner_in[3] * from_up

    for i in (0, HEIGHT - 1):
        round_cells(i, 0, WIDTH)

    @pl.loop(1, HEIGHT - 1)
    def _(i):
        round_cells(i, 0, BS)
        round_cells(i, WIDTH - BS, BS)

    writes[2].start()

    @pl.loop(0, PEERS)
    def _(k):
        for r in range(CAP):
            cot_copy(k, r).wait_send()
            patch_copy(k, r).wait_send()
            spread_copy(k, r).wait_send()
            out_copy(k, r).wait_send()

    for copy in writes:
        copy.wait()


def write_kernel(a, b, c, a_out, b_out, c_out, sem):
    quarter = HEIGHT // 4
    copies = []
    for source, target in ((a, a_out), (b, b_out)):
        for i in range(4):
            part = pl.ds(i * quarter, quarter)
            copies.append((source.at[part], target.at[part]))
    for i in range(2):
        for part in (pl.ds(0, 5), pl.ds(5, 4)):
            copies.append((c.at[i, part], c_out.at[i, part]))
    copies = [pltpu.make_async_copy(x, y, sem.at[i]) for i, (x, y) in enumerate(copies)]
    for copy in copies:
        copy.start()
    for copy in copies:
        copy.wait()


def local(fields, cotangent, kernel_bank, block_expert, owner):
    hbm = pl.BlockSpec(memory_space=pltpu.HBM)
    smem = pl.BlockSpec(memory_space=pltpu.SMEM)
    vmem = pl.BlockSpec(memory_space=pltpu.VMEM)
    dma = pltpu.SemaphoreType.DMA
    slots = NLON * CAP
    results = pl.pallas_call(
        fused_kernel,
        out_shape=(
            jax.ShapeDtypeStruct((HEIGHT, WIDTH, C), BF16),
            jax.ShapeDtypeStruct((HEIGHT, WIDTH, C), BF16),
            jax.ShapeDtypeStruct((2, 9, C, C), F32),
        ),
        in_specs=[smem, smem, hbm, hbm, hbm],
        out_specs=(hbm, hbm, hbm),
        scratch_shapes=[
            pltpu.VMEM((HEIGHT, WIDTH, C), BF16),
            pltpu.VMEM((HEIGHT, WIDTH, C), BF16),
            pltpu.VMEM((2, 9, C, C), F32),
            pltpu.SMEM((BLK,), jnp.int32),
            pltpu.SMEM((BLK,), jnp.int32),
            pltpu.SMEM((slots,), jnp.int32),
            pltpu.SMEM((BLK,), jnp.int32),
            pltpu.SMEM((NLON, 1, C), jnp.int32),
            pltpu.SMEM((slots,), jnp.int32),
            pltpu.SMEM((slots,), jnp.int32),
            pltpu.SMEM((NLON,), jnp.int32),
            pltpu.VMEM((EXT_ROWS * EXT_COLS, C), F32),
            pltpu.VMEM((EXT_ROWS, EXT_COLS, C), BF16),
            pltpu.VMEM((2, HEIGHT, C), BF16),
            pltpu.VMEM((2, HEIGHT, C), BF16),
            pltpu.VMEM((2, HEIGHT, C), F32),
            pltpu.VMEM((40, C), F32),
            pltpu.VMEM((BLK, BS, BS, C), BF16),
            pltpu.VMEM((BLK, PIECE, C), BF16),
            pltpu.VMEM((NLON, CAP, BS, BS, C), BF16),
            pltpu.VMEM((NLON, CAP, PIECE, C), BF16),
            pltpu.VMEM((NLON, 1, C), jnp.int32),
            pltpu.VMEM((slots, BS, BS, C), BF16),
            pltpu.VMEM((slots, PIECE, C), BF16),
            pltpu.VMEM((NLON, 1, C), jnp.int32),
            pltpu.VMEM((NLON, 9, C, C), BF16),
            pltpu.VMEM((ROWS, 2 * BS, C), F32),
            pltpu.VMEM((ROWS * BS, 3 * C), BF16),
            pltpu.VMEM((ROWS * BS, 3 * C), BF16),
            pltpu.VMEM((2, ROWS, 2 * BS, C), F32),
            pltpu.VMEM((9, C, C), F32),
            pltpu.VMEM((slots, 9, C, C), BF16),
            pltpu.VMEM((slots, BS, BS, C), BF16),
            pltpu.VMEM((slots, PIECE, C), BF16),
            pltpu.VMEM((slots, BS, BS, C), BF16),
            pltpu.VMEM((slots, PIECE, C), BF16),
            pltpu.VMEM((PIECE, C), BF16),
            pltpu.VMEM((NLAT, 9, C, C), BF16),
            pltpu.VMEM((NLAT, 9, C, C), BF16),
            pltpu.VMEM((RING, 2, 9, C, C), BF16),
            pltpu.VMEM((RING, 2, 9, C, C), BF16),
            pltpu.VMEM((2, WIDTH, C), F32),
            pltpu.VMEM((2, HEIGHT, C), F32),
            pltpu.VMEM((4, BS // 2, C), F32),
            dma((3,)), dma((BLK,)),
            dma((8,)), dma((8,)),
            dma((RING,)), dma((RING,)),
            dma((RING,)), dma((RING,)),
            dma((CAP, NLON)), dma((CAP, NLON)),
            dma((CAP, NLON)), dma((CAP, NLON)),
            dma((NLON,)), dma((NLON,)),
            dma((CAP, NLON)), dma((CAP, NLON)),
            dma((CAP, NLON)), dma((CAP, NLON)),
            dma((2,)),
            dma((RING,)), dma((RING,)),
            dma((8,)), dma((8,)),
            dma((5,)), dma((3,)),
        ],
        compiler_params=pltpu.CompilerParams(
            collective_id=0, has_side_effects=True, vmem_limit_bytes=62 << 20
        ),
    )(block_expert, owner, fields, cotangent, kernel_bank)
    return pl.pallas_call(
        write_kernel,
        out_shape=tuple(jax.ShapeDtypeStruct(x.shape, x.dtype) for x in results),
        in_specs=[vmem, vmem, vmem],
        out_specs=(hbm, hbm, hbm),
        scratch_shapes=[dma((12,))],
    )(*results)


def solution(mesh):
    return jax.shard_map(
        local,
        mesh=mesh,
        in_specs=(
            P("lat", "lon", None),
            P("lat", "lon", None),
            P(("lat", "lon"), None, None, None),
            P("lat", "lon"),
            P(),
        ),
        out_specs=(
            P("lat", "lon", None),
            P("lat", "lon", None),
            P(("lat", "lon"), None, None, None),
        ),
        check_vma=False,
    )
```

```python
import jax
import jax.numpy as jnp
from jax import lax
from jax.experimental import pallas as pl
from jax.experimental.pallas import tpu as pltpu
from jax.sharding import PartitionSpec as P

BS = 16
CAP = 2
C = 128
NLAT = 8
NLON = 16
RING = 4
BLK = 16
BLON = 8
HEIGHT = 32
WIDTH = 128
ROWS = BS + 2
SIDE = ROWS
CELLS = ROWS * BS
PIECE = CELLS + 40
EXT_ROWS = HEIGHT + 2
EXT_COLS = WIDTH + 2 * BS
PEERS = NLON - 1
MESH = pl.DeviceIdType.MESH
F32 = jnp.float32
BF16 = jnp.bfloat16


def turn(m):
    return lax.rem(m + 1, RING)


def torus_step(k):
    p = lax.rem(k + 1, NLON)
    i, j = p // RING, lax.rem(p, RING)
    a, b = lax.rem(i + j, RING), j
    swap = lax.rem(lax.axis_index("lat"), 2)
    return a + swap * (b - a), b + swap * (a - b)


def peer_lon(me, k):
    z, y = me // RING, lax.rem(me, RING)
    dz, dy = torus_step(k)
    return lax.rem(z + dz, RING) * RING + lax.rem(y + dy, RING)


def source_lon(me, k):
    z, y = me // RING, lax.rem(me, RING)
    dz, dy = torus_step(k)
    return lax.rem(z + RING - dz, RING) * RING + lax.rem(y + RING - dy, RING)


def greet(lat, lon, diagonal):
    barrier = pltpu.get_barrier_semaphore()

    def signal(device):
        pl.semaphore_signal(barrier, inc=1, device_id=device, device_id_type=MESH)

    @pl.loop(0, PEERS)
    def _(k):
        signal((lat, peer_lon(lon, k)))

    @pl.loop(1, NLAT)
    def _(k):
        signal((lax.rem(lat + k, NLAT), lon))

    for up, side in diagonal:
        signal((lax.rem(lat + up, NLAT), lax.rem(lon + side, NLON)))


def await_greetings(diagonal):
    pl.semaphore_wait(pltpu.get_barrier_semaphore(), NLON - 1 + NLAT - 1 + len(diagonal))


DIAGONAL = ((NLAT - 1, NLON - 1), (NLAT - 1, 1), (1, NLON - 1), (1, 1))


def index_tables(expert_ref, owner_ref, column, local, slot_block):
    for b in range(BLK):
        stored = owner_ref[expert_ref[b // BLON, b % BLON]]
        group = stored >> 1
        column[b] = group & (NLON - 1)
        local[b] = (group >> 4) * 2 + (stored & 1)

    @pl.loop(0, NLON)
    def _(c):
        first = jnp.int32(-1)
        second = jnp.int32(-1)
        for b in range(BLK):
            here = column[b] == c
            second = jnp.where(here & (first >= 0), b, second)
            first = jnp.where(here & (first < 0), b, first)
        slot_block[2 * c] = first
        slot_block[2 * c + 1] = second


def fused_kernel(
    expert_ref, owner_ref, fields, cot, bank,
    outputs_hbm, result_hbm, bank_hbm,
    outputs, result, bank_out, home, local, slot_block, block_slot, ids, rank, order, final, canvas, ext,
    col_stage, col_got, side_stage, sides, cot_in, patch_in, cot_stage, patch_stage, id_stage, got_cot, got_patch, got_id, kern,
    pad, taps, wide_cot, shift, total, running, out_stage, spread_stage, got_out, got_spread, block,
    pair_stage, got_pair, chip_stage, got_chip, row_in, col_in, corner_in,
    load_sem, cot_load, halo_send, halo_recv, bank_send, bank_recv, pass_send, pass_recv,
    cot_send, cot_recv, patch_send, patch_recv, id_send, id_recv,
    out_send, out_recv, spread_send, spread_recv, pair_sem, chip_send, chip_recv, edge_send, edge_recv,
    own_sem, write_sem,
):
    lat, lon = lax.axis_index("lat"), lax.axis_index("lon")
    core = lax.rem(lat, 2)
    chip = lat // 2
    other = lat + 1 - 2 * core

    def remote(source, target, send, recv, device):
        return pltpu.make_async_remote_copy(
            source, target, send, recv, device_id=device, device_id_type=MESH
        )

    greet(lat, lon, DIAGONAL)
    load_fields = pltpu.make_async_copy(
        fields, ext.at[pl.ds(1, HEIGHT), pl.ds(BS, WIDTH)], load_sem.at[0]
    )
    load_fields.start()
    load_bank = pltpu.make_async_copy(bank, kern.at[pl.ds(2 * lat, 2)], load_sem.at[1])
    load_bank.start()

    def load_cot(b):
        rows = pl.ds(pl.multiple_of((b // BLON) * BS, BS), BS)
        cols = pl.ds(pl.multiple_of(lax.rem(b, BLON) * BS, BS), BS)
        return pltpu.make_async_copy(cot.at[rows, cols], cot_in.at[b], cot_load.at[b])

    @pl.loop(0, BLK)
    def _(b):
        load_cot(b).start()

    index_tables(expert_ref, owner_ref, home, local, slot_block)
    for b in range(BLK):
        c = home[b]
        block_slot[b] = 2 * c + jnp.where(slot_block[2 * c + 1] == b, 1, 0)
    up, down = lax.rem(lat + NLAT - 1, NLAT), lax.rem(lat + 1, NLAT)
    left, right = lax.rem(lon + NLON - 1, NLON), lax.rem(lon + 1, NLON)
    top, bottom = pl.ds(0, 1), pl.ds(HEIGHT - 1, 1)
    first, last = pl.ds(0, BS), pl.ds(WIDTH - BS, BS)
    all_cols, mid_cols = pl.ds(0, WIDTH), pl.ds(BS, WIDTH)
    low, high = pl.ds(0, BS), pl.ds(BS + WIDTH, BS)
    zero, end = pl.ds(0, 1), pl.ds(EXT_ROWS - 1, 1)
    moves = (
        (top, all_cols, end, mid_cols, (up, lon)),
        (bottom, all_cols, zero, mid_cols, (down, lon)),
        (top, first, end, high, (up, left)),
        (top, last, end, low, (up, right)),
        (bottom, first, zero, high, (down, left)),
        (bottom, last, zero, low, (down, right)),
    )
    def bank_copy(j):
        return remote(
            bank, kern.at[pl.ds(2 * lat, 2)], bank_send.at[j], bank_recv.at[j],
            (lax.rem(lat + 2 * j, NLAT), lon),
        )

    def pass_copy(j):
        part = kern.at[pl.ds(2 * lax.rem(lat + NLAT - 2 * j, NLAT), 2)]
        return remote(part, part, pass_send.at[j], pass_recv.at[j], (other, lon))

    share_bank = remote(
        bank, kern.at[pl.ds(2 * lat, 2)], pass_send.at[0], pass_recv.at[0], (other, lon)
    )

    def cot_copy(k, r):
        dst = peer_lon(lon, k)
        return remote(
            cot_stage.at[dst, r], got_cot.at[2 * lon + r], cot_send.at[r, k], cot_recv.at[r, k], (lat, dst)
        )

    def patch_copy(k, r):
        dst = peer_lon(lon, k)
        return remote(
            patch_stage.at[dst, r], got_patch.at[2 * lon + r], patch_send.at[r, k], patch_recv.at[r, k],
            (lat, dst),
        )

    def id_copy(k):
        dst = peer_lon(lon, k)
        return remote(id_stage.at[dst], got_id.at[lon], id_send.at[k], id_recv.at[k], (lat, dst))

    def out_copy(k, r):
        dst = source_lon(lon, k)
        return remote(
            out_stage.at[2 * dst + r], got_out.at[2 * lon + r], out_send.at[r, k], out_recv.at[r, k], (lat, dst)
        )

    def spread_copy(k, r):
        dst = source_lon(lon, k)
        return remote(
            spread_stage.at[2 * dst + r], got_spread.at[2 * lon + r], spread_send.at[r, k],
            spread_recv.at[r, k], (lat, dst),
        )

    def own(source, target, i):
        return pltpu.make_async_copy(source, target, own_sem.at[i])

    own_slots = pl.ds(2 * lon, CAP)
    own_cot = own(cot_stage.at[lon], got_cot.at[own_slots], 0)
    own_patch = own(patch_stage.at[lon], got_patch.at[own_slots], 1)
    own_id = own(id_stage.at[lon], got_id.at[lon], 2)
    own_out = own(out_stage.at[own_slots], got_out.at[own_slots], 3)
    own_spread = own(spread_stage.at[own_slots], got_spread.at[own_slots], 4)

    def stage_cot(k, r):
        dst = peer_lon(lon, k)
        cot_stage[dst, r] = cot_in[jnp.maximum(slot_block[2 * dst + r], 0)]

    def column(where):
        return pl.ds(EXT_COLS + where, HEIGHT, stride=EXT_COLS)

    outer_left, inner_left, inner_right, outer_right = BS - 1, BS, BS + WIDTH - 1, BS + WIDTH
    load_fields.wait()

    def widen(r):
        canvas[pl.ds(pl.multiple_of(r * EXT_COLS, BS), EXT_COLS), :] = ext[r].astype(F32)

    @pl.loop(1, HEIGHT + 1)
    def _(r):
        widen(r)

    col_stage[0] = canvas[column(inner_left), :].astype(BF16)
    col_stage[1] = canvas[column(inner_right), :].astype(BF16)
    lane = lax.broadcasted_iota(jnp.int32, (1, C), 1)

    @pl.loop(0, NLON)
    def _(c):
        found = [slot_block[2 * c + r] for r in range(CAP)]
        named = [jnp.where(f < 0, NLON, local[jnp.maximum(f, 0)]) for f in found]
        id_stage[c] = jnp.where(lane == 0, named[0], named[1])

    @pl.loop(0, BLK)
    def _(b):
        load_cot(b).wait()

    @pl.loop(0, NLON)
    def _(k):
        for r in range(CAP):
            stage_cot(k, r)

    own_cot.start()
    own_id.start()
    await_greetings(DIAGONAL)

    @pl.loop(0, PEERS)
    def _(k):
        cot_copy(k, 0).start()

    halos = []
    for i, (rows, cols, to_rows, to_cols, device) in enumerate(moves):
        copy = remote(
            fields.at[rows, cols], ext.at[to_rows, to_cols], halo_send.at[i], halo_recv.at[i], device
        )
        copy.start()
        halos.append(copy)

    for i, device in enumerate(((lat, left), (lat, right))):
        copy = remote(col_stage.at[i], col_got.at[i], halo_send.at[6 + i], halo_recv.at[6 + i], device)
        copy.start()
        halos.append(copy)

    for j in range(1, RING):
        bank_copy(j).start()
    share_bank.start()

    @pl.loop(0, PEERS)
    def _(k):
        id_copy(k).start()
        cot_copy(k, 1).start()

    for copy in halos:
        copy.wait()

    @pl.when(lat == 0)
    def _():
        ext[0] = jnp.zeros((EXT_COLS, C), BF16)

    @pl.when(lat == NLAT - 1)
    def _():
        ext[EXT_ROWS - 1] = jnp.zeros((EXT_COLS, C), BF16)

    widen(0)
    widen(EXT_ROWS - 1)
    canvas[column(outer_right), :] = col_got[0].astype(F32)
    canvas[column(outer_left), :] = col_got[1].astype(F32)

    @pl.loop(0, BLK)
    def _(b):
        row = pl.multiple_of((b // BLON) * BS, BS)
        col = pl.multiple_of((lax.rem(b, BLON) + 1) * BS, BS)
        patch_in[b, pl.ds(0, CELLS)] = ext[pl.ds(row, ROWS), pl.ds(col, BS), :].reshape(CELLS, C)
        start = row * EXT_COLS + col
        sides[pl.ds(0, ROWS), :] = canvas[pl.ds(start - 1, ROWS, stride=EXT_COLS), :]
        sides[pl.ds(SIDE, ROWS), :] = canvas[pl.ds(start + BS, ROWS, stride=EXT_COLS), :]
        patch_in[b, pl.ds(CELLS, 40)] = sides[...].astype(BF16)

    def stage_patch(k, r):
        dst = peer_lon(lon, k)
        patch_stage[dst, r] = patch_in[jnp.maximum(slot_block[2 * dst + r], 0)]

    @pl.loop(0, PEERS)
    def _(k):
        stage_patch(k, 0)
        patch_copy(k, 0).start()

    @pl.loop(0, PEERS)
    def _(k):
        stage_patch(k, 1)
        patch_copy(k, 1).start()

    for r in range(CAP):
        stage_patch(PEERS, r)
    own_patch.start()

    load_bank.wait()
    for j in range(1, RING):
        bank_copy(j).wait()
        pass_copy(j).start()

    own_id.wait()

    @pl.loop(0, PEERS)
    def _(k):
        id_copy(k).wait()

    read_ids = pltpu.make_async_copy(got_id, ids, load_sem.at[2])
    read_ids.start()
    read_ids.wait()
    canvas[...] = jnp.zeros_like(canvas)
    wide_cot[...] = jnp.zeros_like(wide_cot)

    @pl.loop(0, NLON)
    def _(c):
        for r in range(CAP):
            mine = ids[c, 0, r]
            here = 2 * c + r
            before = jnp.int32(0)
            for s in range(NLON * CAP):
                it = ids[s // CAP, 0, s % CAP]
                before += jnp.where((it < mine) | ((it == mine) & (s < here)), 1, 0)
            rank[here] = before

    @pl.loop(0, NLON * CAP)
    def _(j):
        slot = jnp.int32(0)
        for s in range(NLON * CAP):
            slot = jnp.where(rank[s] == j, s, slot)
        order[j] = slot

    @pl.loop(0, NLON)
    def _(e):
        upto = jnp.int32(0)
        some = jnp.int32(0)
        for s in range(NLON * CAP):
            it = ids[s // CAP, 0, s % CAP]
            upto += jnp.where(it <= e, 1, 0)
            some += jnp.where(it == e, 1, 0)
        final[e] = jnp.where(some > 0, upto - 1, -1)

    share_bank.wait()
    for j in range(1, RING):
        pass_copy(j).wait()

    def build_taps(slot):
        pad[:, pl.ds(8, BS), :] = got_patch[slot, pl.ds(0, CELLS)].reshape(ROWS, BS, C).astype(F32)
        sides[...] = got_patch[slot, pl.ds(CELLS, 40)].astype(F32)
        pad[:, 7, :] = sides[pl.ds(0, ROWS), :]
        pad[:, BS + 8, :] = sides[pl.ds(SIDE, ROWS), :]
        for b in range(3):
            taps[:, pl.ds(b * C, C)] = pad[:, pl.ds(7 + b, BS), :].reshape(ROWS * BS, C).astype(BF16)

    def convolve(slot, e):
        build_taps(slot)
        cots = got_cot[slot].reshape(BS * BS, C)
        for a in range(3):
            wide_cot[pl.ds(a * BS, BS * BS), pl.ds(a * C, C)] = cots
        weights = [kern[e, pl.ds(3 * a, 3)].reshape(3 * C, C) for a in range(3)]
        sums = jnp.zeros((BS * BS, C), F32)
        for a in range(3):
            sums += jnp.dot(taps[pl.ds(a * BS, BS * BS), :], weights[a], preferred_element_type=F32)
        out_stage[slot] = sums.astype(BF16).reshape(BS, BS, C)
        grid = lax.dot_general(
            wide_cot[...], jnp.concatenate(weights, axis=1), (((1,), (1,)), ((), ())),
            preferred_element_type=F32,
        )
        shift[0, :, pl.ds(8, BS), :] = grid[:, :C].reshape(ROWS, BS, C)
        shift[1, :, pl.ds(8, BS), :] = grid[:, 2 * C:].reshape(ROWS, BS, C)
        place = lax.broadcasted_iota(jnp.int32, (ROWS, BS, C), 1)
        main = grid[:, C:2 * C].reshape(ROWS, BS, C)
        main += jnp.where(place == BS - 1, 0.0, shift[0, :, pl.ds(9, BS), :])
        main += jnp.where(place == 0, 0.0, shift[1, :, pl.ds(7, BS), :])
        spread_stage[slot, pl.ds(0, CELLS)] = main.astype(BF16).reshape(CELLS, C)
        sides[pl.ds(0, ROWS), :] = shift[0, :, 8, :]
        sides[pl.ds(SIDE, ROWS), :] = shift[1, :, BS + 7, :]
        spread_stage[slot, pl.ds(CELLS, 40)] = sides[...].astype(BF16)

    own_cot.wait()
    own_patch.wait()

    @pl.loop(0, CAP * NLON)
    def _(step):
        r, k = step // NLON, lax.rem(step, NLON)
        source = source_lon(lon, k)

        @pl.when(k < PEERS)
        def _():
            cot_copy(k, r).wait_recv()
            patch_copy(k, r).wait_recv()

        convolve(2 * source + r, jnp.minimum(ids[source, 0, r], NLON - 1))

        @pl.when(k < PEERS)
        def _():
            spread_copy(k, r).start()

        @pl.when((k < PEERS) & (r == 0))
        def _():
            out_copy(k, r).start()

    @pl.loop(0, PEERS)
    def _(k):
        out_copy(k, 1).start()

    own_out.start()
    own_spread.start()

    @pl.loop(0, NLON * CAP)
    def _(j):
        slot = order[j]
        previous = order[jnp.maximum(j - 1, 0)]
        now = ids[slot >> 1, 0, slot & 1]
        same = (j > 0) & (ids[previous >> 1, 0, previous & 1] == now)
        build_taps(slot)
        cots = got_cot[slot].reshape(BS * BS, C)
        for a in range(3):
            term = lax.dot_general(
                taps[pl.ds(a * BS, BS * BS), :], cots, (((0,), (0,)), ((), ())),
                preferred_element_type=F32,
            ).reshape(3, C, C)
            sums = jnp.where(same, total[pl.ds(3 * a, 3)], 0.0) + term
            total[pl.ds(3 * a, 3)] = sums
            running[j, pl.ds(3 * a, 3)] = sums.astype(BF16)

    def gradient(e):
        at = final[e]
        return jnp.where(at < 0, 0.0, running[jnp.maximum(at, 0)].astype(F32))

    @pl.loop(0, NLAT)
    def _(i):
        e = 4 * (i // 2) + 2 * (1 - core) + lax.rem(i, 2)
        pair_stage[i] = gradient(e).astype(BF16)

    pair = remote(pair_stage, got_pair, pair_sem.at[0], pair_sem.at[1], (other, lon))
    pair.start()

    def chip_copy(j):
        to = lax.rem(chip + j, RING)
        return remote(
            chip_stage.at[to], got_chip.at[chip], chip_send.at[j], chip_recv.at[j], (2 * to + core, lon)
        )

    pair.wait()

    @pl.loop(1, RING)
    def _(j):
        to = lax.rem(chip + j, RING)
        for i in range(2):
            both = gradient(4 * to + 2 * core + i) + got_pair[2 * to + i].astype(F32)
            chip_stage[to, i] = both.astype(BF16)
        chip_copy(j).start()

    for i in range(2):
        bank_out[i] = gradient(4 * chip + 2 * core + i) + got_pair[2 * chip + i].astype(F32)

    own_spread.wait()

    @pl.loop(0, PEERS)
    def _(k):
        for r in range(CAP):
            spread_copy(k, r).wait_recv()

    @pl.loop(0, BLK)
    def _(b):
        bi, bj = b // BLON, lax.rem(b, BLON)
        base = bi * BS * EXT_COLS + (bj + 1) * BS
        block[...] = got_spread[block_slot[b]]

        for i in range(ROWS):
            at = pl.ds(pl.multiple_of(base + i * EXT_COLS, BS), BS)
            canvas[at, :] += block[pl.ds(i * BS, BS)].astype(F32)
        sides[...] = block[pl.ds(CELLS, 40)].astype(F32)
        canvas[pl.ds(base - 1, ROWS, stride=EXT_COLS), :] += sides[pl.ds(0, ROWS), :]
        canvas[pl.ds(base + BS, ROWS, stride=EXT_COLS), :] += sides[pl.ds(SIDE, ROWS), :]

    side_stage[0] = canvas[column(outer_left), :]
    side_stage[1] = canvas[column(outer_right), :]
    grid = canvas.reshape(EXT_ROWS, EXT_COLS, C)
    half = BS // 2
    edge_low, edge_high = pl.ds(half, half), pl.ds(BS + WIDTH, half)
    edges = (
        (grid.at[0, mid_cols], row_in.at[0], (up, lon)),
        (grid.at[EXT_ROWS - 1, mid_cols], row_in.at[1], (down, lon)),
        (side_stage.at[0], col_in.at[0], (lat, left)),
        (side_stage.at[1], col_in.at[1], (lat, right)),
        (grid.at[0, edge_low], corner_in.at[0], (up, left)),
        (grid.at[0, edge_high], corner_in.at[1], (up, right)),
        (grid.at[EXT_ROWS - 1, edge_low], corner_in.at[2], (down, left)),
        (grid.at[EXT_ROWS - 1, edge_high], corner_in.at[3], (down, right)),
    )
    edge_copies = []
    for i, (source, target, device) in enumerate(edges):
        copy = remote(source, target, edge_send.at[i], edge_recv.at[i], device)
        copy.start()
        edge_copies.append(copy)

    @pl.loop(1, RING)
    def _(j):
        chip_copy(j).wait()
        back = lax.rem(chip + RING - j, RING)
        for i in range(2):
            bank_out[i] += got_chip[back, i].astype(F32)

    writes = [
        pltpu.make_async_copy(x, y, write_sem.at[i])
        for i, (x, y) in enumerate(((bank_out, bank_hbm), (outputs, outputs_hbm), (result, result_hbm)))
    ]
    writes[0].start()
    own_out.wait()

    @pl.loop(0, PEERS)
    def _(k):
        for r in range(CAP):
            out_copy(k, r).wait_recv()

    @pl.loop(0, BLK)
    def _(b):
        bi, bj = b // BLON, lax.rem(b, BLON)
        outputs[
            pl.ds(pl.multiple_of(bi * BS, BS), BS), pl.ds(pl.multiple_of(bj * BS, BS), BS), :
        ] = got_out[block_slot[b]]

    writes[1].start()

    def round_cells(i, col, count):
        start = pl.multiple_of((i + 1) * EXT_COLS + BS + col, BS)
        result[i, pl.ds(col, count)] = canvas[pl.ds(start, count), :].astype(BF16)

    @pl.loop(1, HEIGHT - 1)
    def _(i):
        round_cells(i, BS, WIDTH - 2 * BS)

    for copy in edge_copies:
        copy.wait()
    from_down = jnp.where(lat < NLAT - 1, 1.0, 0.0).astype(F32)
    from_up = jnp.where(lat > 0, 1.0, 0.0).astype(F32)
    upper, lower = EXT_COLS, HEIGHT * EXT_COLS
    canvas[pl.ds(lower + BS, WIDTH), :] += row_in[0] * from_down
    canvas[pl.ds(upper + BS, WIDTH), :] += row_in[1] * from_up

    canvas[column(inner_right), :] += col_in[0]
    canvas[column(inner_left), :] += col_in[1]
    canvas[pl.ds(lower + BS + WIDTH - half, half), :] += corner_in[0] * from_down
    canvas[pl.ds(lower + BS, half), :] += corner_in[1] * from_down
    canvas[pl.ds(upper + BS + WIDTH - half, half), :] += corner_in[2] * from_up
    canvas[pl.ds(upper + BS, half), :] += corner_in[3] * from_up

    for i in (0, HEIGHT - 1):
        round_cells(i, 0, WIDTH)

    @pl.loop(1, HEIGHT - 1)
    def _(i):
        round_cells(i, 0, BS)
        round_cells(i, WIDTH - BS, BS)

    writes[2].start()

    @pl.loop(0, PEERS)
    def _(k):
        for r in range(CAP):
            cot_copy(k, r).wait_send()
            patch_copy(k, r).wait_send()
            spread_copy(k, r).wait_send()
            out_copy(k, r).wait_send()

    for copy in writes:
        copy.wait()


def write_kernel(a, b, c, a_out, b_out, c_out, sem):
    quarter = HEIGHT // 4
    copies = []
    for source, target in ((a, a_out), (b, b_out)):
        for i in range(4):
            part = pl.ds(i * quarter, quarter)
            copies.append((source.at[part], target.at[part]))
    for i in range(2):
        for part in (pl.ds(0, 5), pl.ds(5, 4)):
            copies.append((c.at[i, part], c_out.at[i, part]))
    copies = [pltpu.make_async_copy(x, y, sem.at[i]) for i, (x, y) in enumerate(copies)]
    for copy in copies:
        copy.start()
    for copy in copies:
        copy.wait()


def local(fields, cotangent, kernel_bank, block_expert, owner):
    hbm = pl.BlockSpec(memory_space=pltpu.HBM)
    smem = pl.BlockSpec(memory_space=pltpu.SMEM)
    vmem = pl.BlockSpec(memory_space=pltpu.VMEM)
    dma = pltpu.SemaphoreType.DMA
    slots = NLON * CAP
    results = pl.pallas_call(
        fused_kernel,
        out_shape=(
            jax.ShapeDtypeStruct((HEIGHT, WIDTH, C), BF16),
            jax.ShapeDtypeStruct((HEIGHT, WIDTH, C), BF16),
            jax.ShapeDtypeStruct((2, 9, C, C), F32),
        ),
        in_specs=[smem, smem, hbm, hbm, hbm],
        out_specs=(hbm, hbm, hbm),
        scratch_shapes=[
            pltpu.VMEM((HEIGHT, WIDTH, C), BF16),
            pltpu.VMEM((HEIGHT, WIDTH, C), BF16),
            pltpu.VMEM((2, 9, C, C), F32),
            pltpu.SMEM((BLK,), jnp.int32),
            pltpu.SMEM((BLK,), jnp.int32),
            pltpu.SMEM((slots,), jnp.int32),
            pltpu.SMEM((BLK,), jnp.int32),
            pltpu.SMEM((NLON, 1, C), jnp.int32),
            pltpu.SMEM((slots,), jnp.int32),
            pltpu.SMEM((slots,), jnp.int32),
            pltpu.SMEM((NLON,), jnp.int32),
            pltpu.VMEM((EXT_ROWS * EXT_COLS, C), F32),
            pltpu.VMEM((EXT_ROWS, EXT_COLS, C), BF16),
            pltpu.VMEM((2, HEIGHT, C), BF16),
            pltpu.VMEM((2, HEIGHT, C), BF16),
            pltpu.VMEM((2, HEIGHT, C), F32),
            pltpu.VMEM((40, C), F32),
            pltpu.VMEM((BLK, BS, BS, C), BF16),
            pltpu.VMEM((BLK, PIECE, C), BF16),
            pltpu.VMEM((NLON, CAP, BS, BS, C), BF16),
            pltpu.VMEM((NLON, CAP, PIECE, C), BF16),
            pltpu.VMEM((NLON, 1, C), jnp.int32),
            pltpu.VMEM((slots, BS, BS, C), BF16),
            pltpu.VMEM((slots, PIECE, C), BF16),
            pltpu.VMEM((NLON, 1, C), jnp.int32),
            pltpu.VMEM((NLON, 9, C, C), BF16),
            pltpu.VMEM((ROWS, 2 * BS, C), F32),
            pltpu.VMEM((ROWS * BS, 3 * C), BF16),
            pltpu.VMEM((ROWS * BS, 3 * C), BF16),
            pltpu.VMEM((2, ROWS, 2 * BS, C), F32),
            pltpu.VMEM((9, C, C), F32),
            pltpu.VMEM((slots, 9, C, C), BF16),
            pltpu.VMEM((slots, BS, BS, C), BF16),
            pltpu.VMEM((slots, PIECE, C), BF16),
            pltpu.VMEM((slots, BS, BS, C), BF16),
            pltpu.VMEM((slots, PIECE, C), BF16),
            pltpu.VMEM((PIECE, C), BF16),
            pltpu.VMEM((NLAT, 9, C, C), BF16),
            pltpu.VMEM((NLAT, 9, C, C), BF16),
            pltpu.VMEM((RING, 2, 9, C, C), BF16),
            pltpu.VMEM((RING, 2, 9, C, C), BF16),
            pltpu.VMEM((2, WIDTH, C), F32),
            pltpu.VMEM((2, HEIGHT, C), F32),
            pltpu.VMEM((4, BS // 2, C), F32),
            dma((3,)), dma((BLK,)),
            dma((8,)), dma((8,)),
            dma((RING,)), dma((RING,)),
            dma((RING,)), dma((RING,)),
            dma((CAP, NLON)), dma((CAP, NLON)),
            dma((CAP, NLON)), dma((CAP, NLON)),
            dma((NLON,)), dma((NLON,)),
            dma((CAP, NLON)), dma((CAP, NLON)),
            dma((CAP, NLON)), dma((CAP, NLON)),
            dma((2,)),
            dma((RING,)), dma((RING,)),
            dma((8,)), dma((8,)),
            dma((5,)), dma((3,)),
        ],
        compiler_params=pltpu.CompilerParams(
            collective_id=0, has_side_effects=True, vmem_limit_bytes=62 << 20
        ),
    )(block_expert, owner, fields, cotangent, kernel_bank)
    return pl.pallas_call(
        write_kernel,
        out_shape=tuple(jax.ShapeDtypeStruct(x.shape, x.dtype) for x in results),
        in_specs=[vmem, vmem, vmem],
        out_specs=(hbm, hbm, hbm),
        scratch_shapes=[dma((12,))],
    )(*results)


def solution(mesh):
    return jax.shard_map(
        local,
        mesh=mesh,
        in_specs=(
            P("lat", "lon", None),
            P("lat", "lon", None),
            P(("lat", "lon"), None, None, None),
            P("lat", "lon"),
            P(),
        ),
        out_specs=(
            P("lat", "lon", None),
            P("lat", "lon", None),
            P(("lat", "lon"), None, None, None),
        ),
        check_vma=False,
    )
```

```python
import jax
import jax.numpy as jnp
from jax import lax
from jax.experimental import pallas as pl
from jax.experimental.pallas import tpu as pltpu
from jax.sharding import PartitionSpec as P

BS = 16
CAP = 2
C = 128
NLAT = 8
NLON = 16
RING = 4
BLK = 16
BLON = 8
HEIGHT = 32
WIDTH = 128
ROWS = BS + 2
SIDE = ROWS
CELLS = ROWS * BS
PIECE = CELLS + 40
EXT_ROWS = HEIGHT + 2
EXT_COLS = WIDTH + 2 * BS
PEERS = NLON - 1
MESH = pl.DeviceIdType.MESH
F32 = jnp.float32
BF16 = jnp.bfloat16


def turn(m):
    return lax.rem(m + 1, RING)


def torus_step(k):
    p = lax.rem(k + 1, NLON)
    i, j = p // RING, lax.rem(p, RING)
    a, b = lax.rem(i + 2 * j, RING), j
    swap = lax.rem(lax.axis_index("lat"), 2)
    c, d = lax.rem(RING - a, RING), lax.rem(RING - b, RING)
    return a + swap * (d - a), b + swap * (c - b)


def peer_lon(me, k):
    z, y = me // RING, lax.rem(me, RING)
    dz, dy = torus_step(k)
    return lax.rem(z + dz, RING) * RING + lax.rem(y + dy, RING)


def source_lon(me, k):
    z, y = me // RING, lax.rem(me, RING)
    dz, dy = torus_step(k)
    return lax.rem(z + RING - dz, RING) * RING + lax.rem(y + RING - dy, RING)


def greet(lat, lon, diagonal):
    barrier = pltpu.get_barrier_semaphore()

    def signal(device):
        pl.semaphore_signal(barrier, inc=1, device_id=device, device_id_type=MESH)

    @pl.loop(0, PEERS)
    def _(k):
        signal((lat, peer_lon(lon, k)))

    @pl.loop(1, NLAT)
    def _(k):
        signal((lax.rem(lat + k, NLAT), lon))

    for up, side in diagonal:
        signal((lax.rem(lat + up, NLAT), lax.rem(lon + side, NLON)))


def await_greetings(diagonal):
    pl.semaphore_wait(pltpu.get_barrier_semaphore(), NLON - 1 + NLAT - 1 + len(diagonal))


DIAGONAL = ((NLAT - 1, NLON - 1), (NLAT - 1, 1), (1, NLON - 1), (1, 1))


def index_tables(expert_ref, owner_ref, column, local, slot_block):
    for b in range(BLK):
        stored = owner_ref[expert_ref[b // BLON, b % BLON]]
        group = stored >> 1
        column[b] = group & (NLON - 1)
        local[b] = (group >> 4) * 2 + (stored & 1)

    @pl.loop(0, NLON)
    def _(c):
        first = jnp.int32(-1)
        second = jnp.int32(-1)
        for b in range(BLK):
            here = column[b] == c
            second = jnp.where(here & (first >= 0), b, second)
            first = jnp.where(here & (first < 0), b, first)
        slot_block[2 * c] = first
        slot_block[2 * c + 1] = second


def fused_kernel(
    expert_ref, owner_ref, fields, cot, bank,
    outputs_hbm, result_hbm, bank_hbm,
    outputs, result, bank_out, home, local, slot_block, block_slot, ids, rank, order, final, canvas, ext,
    col_stage, col_got, side_stage, sides, cot_in, patch_in, cot_stage, patch_stage, id_stage, got_cot, got_patch, got_id, kern,
    pad, taps, wide_cot, shift, total, running, out_stage, spread_stage, got_out, got_spread, block,
    pair_stage, got_pair, chip_stage, got_chip, row_in, col_in, corner_in,
    load_sem, cot_load, halo_send, halo_recv, bank_send, bank_recv, pass_send, pass_recv,
    cot_send, cot_recv, patch_send, patch_recv, id_send, id_recv,
    out_send, out_recv, spread_send, spread_recv, pair_sem, chip_send, chip_recv, edge_send, edge_recv,
    own_sem, write_sem,
):
    lat, lon = lax.axis_index("lat"), lax.axis_index("lon")
    core = lax.rem(lat, 2)
    chip = lat // 2
    other = lat + 1 - 2 * core

    def remote(source, target, send, recv, device):
        return pltpu.make_async_remote_copy(
            source, target, send, recv, device_id=device, device_id_type=MESH
        )

    greet(lat, lon, DIAGONAL)
    load_fields = pltpu.make_async_copy(
        fields, ext.at[pl.ds(1, HEIGHT), pl.ds(BS, WIDTH)], load_sem.at[0]
    )
    load_fields.start()
    load_bank = pltpu.make_async_copy(bank, kern.at[pl.ds(2 * lat, 2)], load_sem.at[1])
    load_bank.start()

    def load_cot(b):
        rows = pl.ds(pl.multiple_of((b // BLON) * BS, BS), BS)
        cols = pl.ds(pl.multiple_of(lax.rem(b, BLON) * BS, BS), BS)
        return pltpu.make_async_copy(cot.at[rows, cols], cot_in.at[b], cot_load.at[b])

    @pl.loop(0, BLK)
    def _(b):
        load_cot(b).start()

    index_tables(expert_ref, owner_ref, home, local, slot_block)
    for b in range(BLK):
        c = home[b]
        block_slot[b] = 2 * c + jnp.where(slot_block[2 * c + 1] == b, 1, 0)
    up, down = lax.rem(lat + NLAT - 1, NLAT), lax.rem(lat + 1, NLAT)
    left, right = lax.rem(lon + NLON - 1, NLON), lax.rem(lon + 1, NLON)
    top, bottom = pl.ds(0, 1), pl.ds(HEIGHT - 1, 1)
    first, last = pl.ds(0, BS), pl.ds(WIDTH - BS, BS)
    all_cols, mid_cols = pl.ds(0, WIDTH), pl.ds(BS, WIDTH)
    low, high = pl.ds(0, BS), pl.ds(BS + WIDTH, BS)
    zero, end = pl.ds(0, 1), pl.ds(EXT_ROWS - 1, 1)
    moves = (
        (top, all_cols, end, mid_cols, (up, lon)),
        (bottom, all_cols, zero, mid_cols, (down, lon)),
        (top, first, end, high, (up, left)),
        (top, last, end, low, (up, right)),
        (bottom, first, zero, high, (down, left)),
        (bottom, last, zero, low, (down, right)),
    )
    def bank_copy(j):
        return remote(
            bank, kern.at[pl.ds(2 * lat, 2)], bank_send.at[j], bank_recv.at[j],
            (lax.rem(lat + 2 * j, NLAT), lon),
        )

    def pass_copy(j):
        part = kern.at[pl.ds(2 * lax.rem(lat + NLAT - 2 * j, NLAT), 2)]
        return remote(part, part, pass_send.at[j], pass_recv.at[j], (other, lon))

    share_bank = remote(
        bank, kern.at[pl.ds(2 * lat, 2)], pass_send.at[0], pass_recv.at[0], (other, lon)
    )

    def cot_copy(k, r):
        dst = peer_lon(lon, k)
        return remote(
            cot_stage.at[dst, r], got_cot.at[2 * lon + r], cot_send.at[r, k], cot_recv.at[r, k], (lat, dst)
        )

    def patch_copy(k, r):
        dst = peer_lon(lon, k)
        return remote(
            patch_stage.at[dst, r], got_patch.at[2 * lon + r], patch_send.at[r, k], patch_recv.at[r, k],
            (lat, dst),
        )

    def id_copy(k):
        dst = peer_lon(lon, k)
        return remote(id_stage.at[dst], got_id.at[lon], id_send.at[k], id_recv.at[k], (lat, dst))

    def out_copy(k, r):
        dst = source_lon(lon, k)
        return remote(
            out_stage.at[2 * dst + r], got_out.at[2 * lon + r], out_send.at[r, k], out_recv.at[r, k], (lat, dst)
        )

    def spread_copy(k, r):
        dst = source_lon(lon, k)
        return remote(
            spread_stage.at[2 * dst + r], got_spread.at[2 * lon + r], spread_send.at[r, k],
            spread_recv.at[r, k], (lat, dst),
        )

    def own(source, target, i):
        return pltpu.make_async_copy(source, target, own_sem.at[i])

    own_slots = pl.ds(2 * lon, CAP)
    own_cot = own(cot_stage.at[lon], got_cot.at[own_slots], 0)
    own_patch = own(patch_stage.at[lon], got_patch.at[own_slots], 1)
    own_id = own(id_stage.at[lon], got_id.at[lon], 2)
    own_out = own(out_stage.at[own_slots], got_out.at[own_slots], 3)
    own_spread = own(spread_stage.at[own_slots], got_spread.at[own_slots], 4)

    def stage_cot(k, r):
        dst = peer_lon(lon, k)
        cot_stage[dst, r] = cot_in[jnp.maximum(slot_block[2 * dst + r], 0)]

    def column(where):
        return pl.ds(EXT_COLS + where, HEIGHT, stride=EXT_COLS)

    outer_left, inner_left, inner_right, outer_right = BS - 1, BS, BS + WIDTH - 1, BS + WIDTH
    load_fields.wait()

    def widen(r):
        canvas[pl.ds(pl.multiple_of(r * EXT_COLS, BS), EXT_COLS), :] = ext[r].astype(F32)

    @pl.loop(1, HEIGHT + 1)
    def _(r):
        widen(r)

    col_stage[0] = canvas[column(inner_left), :].astype(BF16)
    col_stage[1] = canvas[column(inner_right), :].astype(BF16)
    lane = lax.broadcasted_iota(jnp.int32, (1, C), 1)

    @pl.loop(0, NLON)
    def _(c):
        found = [slot_block[2 * c + r] for r in range(CAP)]
        named = [jnp.where(f < 0, NLON, local[jnp.maximum(f, 0)]) for f in found]
        id_stage[c] = jnp.where(lane == 0, named[0], named[1])

    @pl.loop(0, BLK)
    def _(b):
        load_cot(b).wait()

    @pl.loop(0, NLON)
    def _(k):
        for r in range(CAP):
            stage_cot(k, r)

    own_cot.start()
    own_id.start()
    await_greetings(DIAGONAL)

    @pl.loop(0, PEERS)
    def _(k):
        cot_copy(k, 0).start()

    halos = []
    for i, (rows, cols, to_rows, to_cols, device) in enumerate(moves):
        copy = remote(
            fields.at[rows, cols], ext.at[to_rows, to_cols], halo_send.at[i], halo_recv.at[i], device
        )
        copy.start()
        halos.append(copy)

    for i, device in enumerate(((lat, left), (lat, right))):
        copy = remote(col_stage.at[i], col_got.at[i], halo_send.at[6 + i], halo_recv.at[6 + i], device)
        copy.start()
        halos.append(copy)

    for j in range(1, RING):
        bank_copy(j).start()
    share_bank.start()

    @pl.loop(0, PEERS)
    def _(k):
        id_copy(k).start()
        cot_copy(k, 1).start()

    for copy in halos:
        copy.wait()

    @pl.when(lat == 0)
    def _():
        ext[0] = jnp.zeros((EXT_COLS, C), BF16)

    @pl.when(lat == NLAT - 1)
    def _():
        ext[EXT_ROWS - 1] = jnp.zeros((EXT_COLS, C), BF16)

    widen(0)
    widen(EXT_ROWS - 1)
    canvas[column(outer_right), :] = col_got[0].astype(F32)
    canvas[column(outer_left), :] = col_got[1].astype(F32)

    @pl.loop(0, BLK)
    def _(b):
        row = pl.multiple_of((b // BLON) * BS, BS)
        col = pl.multiple_of((lax.rem(b, BLON) + 1) * BS, BS)
        patch_in[b, pl.ds(0, CELLS)] = ext[pl.ds(row, ROWS), pl.ds(col, BS), :].reshape(CELLS, C)
        start = row * EXT_COLS + col
        sides[pl.ds(0, ROWS), :] = canvas[pl.ds(start - 1, ROWS, stride=EXT_COLS), :]
        sides[pl.ds(SIDE, ROWS), :] = canvas[pl.ds(start + BS, ROWS, stride=EXT_COLS), :]
        patch_in[b, pl.ds(CELLS, 40)] = sides[...].astype(BF16)

    def stage_patch(k, r):
        dst = peer_lon(lon, k)
        patch_stage[dst, r] = patch_in[jnp.maximum(slot_block[2 * dst + r], 0)]

    @pl.loop(0, PEERS)
    def _(k):
        stage_patch(k, 0)
        patch_copy(k, 0).start()

    @pl.loop(0, PEERS)
    def _(k):
        stage_patch(k, 1)
        patch_copy(k, 1).start()

    for r in range(CAP):
        stage_patch(PEERS, r)
    own_patch.start()

    load_bank.wait()
    for j in range(1, RING):
        bank_copy(j).wait()
        pass_copy(j).start()

    own_id.wait()

    @pl.loop(0, PEERS)
    def _(k):
        id_copy(k).wait()

    read_ids = pltpu.make_async_copy(got_id, ids, load_sem.at[2])
    read_ids.start()
    read_ids.wait()
    canvas[...] = jnp.zeros_like(canvas)
    wide_cot[...] = jnp.zeros_like(wide_cot)

    @pl.loop(0, NLON)
    def _(c):
        for r in range(CAP):
            mine = ids[c, 0, r]
            here = 2 * c + r
            before = jnp.int32(0)
            for s in range(NLON * CAP):
                it = ids[s // CAP, 0, s % CAP]
                before += jnp.where((it < mine) | ((it == mine) & (s < here)), 1, 0)
            rank[here] = before

    @pl.loop(0, NLON * CAP)
    def _(j):
        slot = jnp.int32(0)
        for s in range(NLON * CAP):
            slot = jnp.where(rank[s] == j, s, slot)
        order[j] = slot

    @pl.loop(0, NLON)
    def _(e):
        upto = jnp.int32(0)
        some = jnp.int32(0)
        for s in range(NLON * CAP):
            it = ids[s // CAP, 0, s % CAP]
            upto += jnp.where(it <= e, 1, 0)
            some += jnp.where(it == e, 1, 0)
        final[e] = jnp.where(some > 0, upto - 1, -1)

    share_bank.wait()
    for j in range(1, RING):
        pass_copy(j).wait()

    def build_taps(slot):
        pad[:, pl.ds(8, BS), :] = got_patch[slot, pl.ds(0, CELLS)].reshape(ROWS, BS, C).astype(F32)
        sides[...] = got_patch[slot, pl.ds(CELLS, 40)].astype(F32)
        pad[:, 7, :] = sides[pl.ds(0, ROWS), :]
        pad[:, BS + 8, :] = sides[pl.ds(SIDE, ROWS), :]
        for b in range(3):
            taps[:, pl.ds(b * C, C)] = pad[:, pl.ds(7 + b, BS), :].reshape(ROWS * BS, C).astype(BF16)

    def convolve(slot, e):
        build_taps(slot)
        cots = got_cot[slot].reshape(BS * BS, C)
        for a in range(3):
            wide_cot[pl.ds(a * BS, BS * BS), pl.ds(a * C, C)] = cots
        weights = [kern[e, pl.ds(3 * a, 3)].reshape(3 * C, C) for a in range(3)]
        sums = jnp.zeros((BS * BS, C), F32)
        for a in range(3):
            sums += jnp.dot(taps[pl.ds(a * BS, BS * BS), :], weights[a], preferred_element_type=F32)
        out_stage[slot] = sums.astype(BF16).reshape(BS, BS, C)
        grid = lax.dot_general(
            wide_cot[...], jnp.concatenate(weights, axis=1), (((1,), (1,)), ((), ())),
            preferred_element_type=F32,
        )
        shift[0, :, pl.ds(8, BS), :] = grid[:, :C].reshape(ROWS, BS, C)
        shift[1, :, pl.ds(8, BS), :] = grid[:, 2 * C:].reshape(ROWS, BS, C)
        place = lax.broadcasted_iota(jnp.int32, (ROWS, BS, C), 1)
        main = grid[:, C:2 * C].reshape(ROWS, BS, C)
        main += jnp.where(place == BS - 1, 0.0, shift[0, :, pl.ds(9, BS), :])
        main += jnp.where(place == 0, 0.0, shift[1, :, pl.ds(7, BS), :])
        spread_stage[slot, pl.ds(0, CELLS)] = main.astype(BF16).reshape(CELLS, C)
        sides[pl.ds(0, ROWS), :] = shift[0, :, 8, :]
        sides[pl.ds(SIDE, ROWS), :] = shift[1, :, BS + 7, :]
        spread_stage[slot, pl.ds(CELLS, 40)] = sides[...].astype(BF16)

    own_cot.wait()
    own_patch.wait()

    @pl.loop(0, CAP * NLON)
    def _(step):
        r, k = step // NLON, lax.rem(step, NLON)
        source = source_lon(lon, k)

        @pl.when(k < PEERS)
        def _():
            cot_copy(k, r).wait_recv()
            patch_copy(k, r).wait_recv()

        convolve(2 * source + r, jnp.minimum(ids[source, 0, r], NLON - 1))

        @pl.when(k < PEERS)
        def _():
            spread_copy(k, r).start()

        @pl.when((k < PEERS) & (r == 0))
        def _():
            out_copy(k, r).start()

    @pl.loop(0, PEERS)
    def _(k):
        out_copy(k, 1).start()

    own_out.start()
    own_spread.start()

    @pl.loop(0, NLON * CAP)
    def _(j):
        slot = order[j]
        previous = order[jnp.maximum(j - 1, 0)]
        now = ids[slot >> 1, 0, slot & 1]
        same = (j > 0) & (ids[previous >> 1, 0, previous & 1] == now)
        build_taps(slot)
        cots = got_cot[slot].reshape(BS * BS, C)
        for a in range(3):
            term = lax.dot_general(
                taps[pl.ds(a * BS, BS * BS), :], cots, (((0,), (0,)), ((), ())),
                preferred_element_type=F32,
            ).reshape(3, C, C)
            sums = jnp.where(same, total[pl.ds(3 * a, 3)], 0.0) + term
            total[pl.ds(3 * a, 3)] = sums
            running[j, pl.ds(3 * a, 3)] = sums.astype(BF16)

    def gradient(e):
        at = final[e]
        return jnp.where(at < 0, 0.0, running[jnp.maximum(at, 0)].astype(F32))

    @pl.loop(0, NLAT)
    def _(i):
        e = 4 * (i // 2) + 2 * (1 - core) + lax.rem(i, 2)
        pair_stage[i] = gradient(e).astype(BF16)

    pair = remote(pair_stage, got_pair, pair_sem.at[0], pair_sem.at[1], (other, lon))
    pair.start()

    def chip_copy(j):
        to = lax.rem(chip + j, RING)
        return remote(
            chip_stage.at[to], got_chip.at[chip], chip_send.at[j], chip_recv.at[j], (2 * to + core, lon)
        )

    pair.wait()

    @pl.loop(1, RING)
    def _(j):
        to = lax.rem(chip + j, RING)
        for i in range(2):
            both = gradient(4 * to + 2 * core + i) + got_pair[2 * to + i].astype(F32)
            chip_stage[to, i] = both.astype(BF16)
        chip_copy(j).start()

    for i in range(2):
        bank_out[i] = gradient(4 * chip + 2 * core + i) + got_pair[2 * chip + i].astype(F32)

    own_spread.wait()

    @pl.loop(0, PEERS)
    def _(k):
        for r in range(CAP):
            spread_copy(k, r).wait_recv()

    @pl.loop(0, BLK)
    def _(b):
        bi, bj = b // BLON, lax.rem(b, BLON)
        base = bi * BS * EXT_COLS + (bj + 1) * BS
        block[...] = got_spread[block_slot[b]]

        for i in range(ROWS):
            at = pl.ds(pl.multiple_of(base + i * EXT_COLS, BS), BS)
            canvas[at, :] += block[pl.ds(i * BS, BS)].astype(F32)
        sides[...] = block[pl.ds(CELLS, 40)].astype(F32)
        canvas[pl.ds(base - 1, ROWS, stride=EXT_COLS), :] += sides[pl.ds(0, ROWS), :]
        canvas[pl.ds(base + BS, ROWS, stride=EXT_COLS), :] += sides[pl.ds(SIDE, ROWS), :]

    side_stage[0] = canvas[column(outer_left), :]
    side_stage[1] = canvas[column(outer_right), :]
    grid = canvas.reshape(EXT_ROWS, EXT_COLS, C)
    half = BS // 2
    edge_low, edge_high = pl.ds(half, half), pl.ds(BS + WIDTH, half)
    edges = (
        (grid.at[0, mid_cols], row_in.at[0], (up, lon)),
        (grid.at[EXT_ROWS - 1, mid_cols], row_in.at[1], (down, lon)),
        (side_stage.at[0], col_in.at[0], (lat, left)),
        (side_stage.at[1], col_in.at[1], (lat, right)),
        (grid.at[0, edge_low], corner_in.at[0], (up, left)),
        (grid.at[0, edge_high], corner_in.at[1], (up, right)),
        (grid.at[EXT_ROWS - 1, edge_low], corner_in.at[2], (down, left)),
        (grid.at[EXT_ROWS - 1, edge_high], corner_in.at[3], (down, right)),
    )
    edge_copies = []
    for i, (source, target, device) in enumerate(edges):
        copy = remote(source, target, edge_send.at[i], edge_recv.at[i], device)
        copy.start()
        edge_copies.append(copy)

    @pl.loop(1, RING)
    def _(j):
        chip_copy(j).wait()
        back = lax.rem(chip + RING - j, RING)
        for i in range(2):
            bank_out[i] += got_chip[back, i].astype(F32)

    writes = [
        pltpu.make_async_copy(x, y, write_sem.at[i])
        for i, (x, y) in enumerate(((bank_out, bank_hbm), (outputs, outputs_hbm), (result, result_hbm)))
    ]
    writes[0].start()
    own_out.wait()

    @pl.loop(0, PEERS)
    def _(k):
        for r in range(CAP):
            out_copy(k, r).wait_recv()

    @pl.loop(0, BLK)
    def _(b):
        bi, bj = b // BLON, lax.rem(b, BLON)
        outputs[
            pl.ds(pl.multiple_of(bi * BS, BS), BS), pl.ds(pl.multiple_of(bj * BS, BS), BS), :
        ] = got_out[block_slot[b]]

    writes[1].start()

    def round_cells(i, col, count):
        start = pl.multiple_of((i + 1) * EXT_COLS + BS + col, BS)
        result[i, pl.ds(col, count)] = canvas[pl.ds(start, count), :].astype(BF16)

    @pl.loop(1, HEIGHT - 1)
    def _(i):
        round_cells(i, BS, WIDTH - 2 * BS)

    for copy in edge_copies:
        copy.wait()
    from_down = jnp.where(lat < NLAT - 1, 1.0, 0.0).astype(F32)
    from_up = jnp.where(lat > 0, 1.0, 0.0).astype(F32)
    upper, lower = EXT_COLS, HEIGHT * EXT_COLS
    canvas[pl.ds(lower + BS, WIDTH), :] += row_in[0] * from_down
    canvas[pl.ds(upper + BS, WIDTH), :] += row_in[1] * from_up

    canvas[column(inner_right), :] += col_in[0]
    canvas[column(inner_left), :] += col_in[1]
    canvas[pl.ds(lower + BS + WIDTH - half, half), :] += corner_in[0] * from_down
    canvas[pl.ds(lower + BS, half), :] += corner_in[1] * from_down
    canvas[pl.ds(upper + BS + WIDTH - half, half), :] += corner_in[2] * from_up
    canvas[pl.ds(upper + BS, half), :] += corner_in[3] * from_up

    for i in (0, HEIGHT - 1):
        round_cells(i, 0, WIDTH)

    @pl.loop(1, HEIGHT - 1)
    def _(i):
        round_cells(i, 0, BS)
        round_cells(i, WIDTH - BS, BS)

    writes[2].start()

    @pl.loop(0, PEERS)
    def _(k):
        for r in range(CAP):
            cot_copy(k, r).wait_send()
            patch_copy(k, r).wait_send()
            spread_copy(k, r).wait_send()
            out_copy(k, r).wait_send()

    for copy in writes:
        copy.wait()


def write_kernel(a, b, c, a_out, b_out, c_out, sem):
    quarter = HEIGHT // 4
    copies = []
    for source, target in ((a, a_out), (b, b_out)):
        for i in range(4):
            part = pl.ds(i * quarter, quarter)
            copies.append((source.at[part], target.at[part]))
    for i in range(2):
        for part in (pl.ds(0, 5), pl.ds(5, 4)):
            copies.append((c.at[i, part], c_out.at[i, part]))
    copies = [pltpu.make_async_copy(x, y, sem.at[i]) for i, (x, y) in enumerate(copies)]
    for copy in copies:
        copy.start()
    for copy in copies:
        copy.wait()


def local(fields, cotangent, kernel_bank, block_expert, owner):
    hbm = pl.BlockSpec(memory_space=pltpu.HBM)
    smem = pl.BlockSpec(memory_space=pltpu.SMEM)
    vmem = pl.BlockSpec(memory_space=pltpu.VMEM)
    dma = pltpu.SemaphoreType.DMA
    slots = NLON * CAP
    results = pl.pallas_call(
        fused_kernel,
        out_shape=(
            jax.ShapeDtypeStruct((HEIGHT, WIDTH, C), BF16),
            jax.ShapeDtypeStruct((HEIGHT, WIDTH, C), BF16),
            jax.ShapeDtypeStruct((2, 9, C, C), F32),
        ),
        in_specs=[smem, smem, hbm, hbm, hbm],
        out_specs=(hbm, hbm, hbm),
        scratch_shapes=[
            pltpu.VMEM((HEIGHT, WIDTH, C), BF16),
            pltpu.VMEM((HEIGHT, WIDTH, C), BF16),
            pltpu.VMEM((2, 9, C, C), F32),
            pltpu.SMEM((BLK,), jnp.int32),
            pltpu.SMEM((BLK,), jnp.int32),
            pltpu.SMEM((slots,), jnp.int32),
            pltpu.SMEM((BLK,), jnp.int32),
            pltpu.SMEM((NLON, 1, C), jnp.int32),
            pltpu.SMEM((slots,), jnp.int32),
            pltpu.SMEM((slots,), jnp.int32),
            pltpu.SMEM((NLON,), jnp.int32),
            pltpu.VMEM((EXT_ROWS * EXT_COLS, C), F32),
            pltpu.VMEM((EXT_ROWS, EXT_COLS, C), BF16),
            pltpu.VMEM((2, HEIGHT, C), BF16),
            pltpu.VMEM((2, HEIGHT, C), BF16),
            pltpu.VMEM((2, HEIGHT, C), F32),
            pltpu.VMEM((40, C), F32),
            pltpu.VMEM((BLK, BS, BS, C), BF16),
            pltpu.VMEM((BLK, PIECE, C), BF16),
            pltpu.VMEM((NLON, CAP, BS, BS, C), BF16),
            pltpu.VMEM((NLON, CAP, PIECE, C), BF16),
            pltpu.VMEM((NLON, 1, C), jnp.int32),
            pltpu.VMEM((slots, BS, BS, C), BF16),
            pltpu.VMEM((slots, PIECE, C), BF16),
            pltpu.VMEM((NLON, 1, C), jnp.int32),
            pltpu.VMEM((NLON, 9, C, C), BF16),
            pltpu.VMEM((ROWS, 2 * BS, C), F32),
            pltpu.VMEM((ROWS * BS, 3 * C), BF16),
            pltpu.VMEM((ROWS * BS, 3 * C), BF16),
            pltpu.VMEM((2, ROWS, 2 * BS, C), F32),
            pltpu.VMEM((9, C, C), F32),
            pltpu.VMEM((slots, 9, C, C), BF16),
            pltpu.VMEM((slots, BS, BS, C), BF16),
            pltpu.VMEM((slots, PIECE, C), BF16),
            pltpu.VMEM((slots, BS, BS, C), BF16),
            pltpu.VMEM((slots, PIECE, C), BF16),
            pltpu.VMEM((PIECE, C), BF16),
            pltpu.VMEM((NLAT, 9, C, C), BF16),
            pltpu.VMEM((NLAT, 9, C, C), BF16),
            pltpu.VMEM((RING, 2, 9, C, C), BF16),
            pltpu.VMEM((RING, 2, 9, C, C), BF16),
            pltpu.VMEM((2, WIDTH, C), F32),
            pltpu.VMEM((2, HEIGHT, C), F32),
            pltpu.VMEM((4, BS // 2, C), F32),
            dma((3,)), dma((BLK,)),
            dma((8,)), dma((8,)),
            dma((RING,)), dma((RING,)),
            dma((RING,)), dma((RING,)),
            dma((CAP, NLON)), dma((CAP, NLON)),
            dma((CAP, NLON)), dma((CAP, NLON)),
            dma((NLON,)), dma((NLON,)),
            dma((CAP, NLON)), dma((CAP, NLON)),
            dma((CAP, NLON)), dma((CAP, NLON)),
            dma((2,)),
            dma((RING,)), dma((RING,)),
            dma((8,)), dma((8,)),
            dma((5,)), dma((3,)),
        ],
        compiler_params=pltpu.CompilerParams(
            collective_id=0, has_side_effects=True, vmem_limit_bytes=62 << 20
        ),
    )(block_expert, owner, fields, cotangent, kernel_bank)
    return pl.pallas_call(
        write_kernel,
        out_shape=tuple(jax.ShapeDtypeStruct(x.shape, x.dtype) for x in results),
        in_specs=[vmem, vmem, vmem],
        out_specs=(hbm, hbm, hbm),
        scratch_shapes=[dma((12,))],
    )(*results)


def solution(mesh):
    return jax.shard_map(
        local,
        mesh=mesh,
        in_specs=(
            P("lat", "lon", None),
            P("lat", "lon", None),
            P(("lat", "lon"), None, None, None),
            P("lat", "lon"),
            P(),
        ),
        out_specs=(
            P("lat", "lon", None),
            P("lat", "lon", None),
            P(("lat", "lon"), None, None, None),
        ),
        check_vma=False,
    )
```
